128 devices in a mesh: tile: 16 (over x, y), phi: 8 (over z, core).
Axes of the slice: x: 4, y: 4, z: 4, core: 2. Of those that a mesh axis runs over, the one named last changes fastest.
Arguments:
- blocks: bfloat16 [4096, 5, 64, 256], P(('tile', 'phi')), may hold values from -6 to 6
- levels: int32 [4096], P(('tile', 'phi')), may hold values from 0 to 3
- block_dest: int32 [4096], P(('tile', 'phi')), may hold values from 0 to 15, as said below
- block_phi: int32 [4096], P(('tile', 'phi')), may hold values from 0 to 3, as said below
- block_group: int32 [4096], P(('tile', 'phi')), may hold values from 0 to 7, as said below
Outputs:
- spectra: float32 [5, 128, 256, 2048], P(None, 'tile', 'phi')
The draws below stay inside these ranges and needn't reach their ends.
Inputs may be any that keep to these rules, and one draw needn't show every extreme that they name: `block_dest`: at most 4 of one device's blocks name one tile, and some device sends exactly 4 to some tile; for each tile and each phi segment, the blocks of that segment that name the tile are exactly 32. Among the blocks of one phi segment that name one tile, the pairs (block_phi, block_group) take each of the 32 values once. `block_group`: see block_phi.
All inputs are finite; a program needn't handle non-finite values.
Results may differ from the reference program's by a relative error of at most 0.003.
Values may be sent and summed in bfloat16 or wider, within the bound.
A program may use at most 192 MiB of HBM per device.

```python
import math
import jax
import jax.numpy as jnp
from jax import lax

FIELDS = 5
NPHI = 2048
BPHI = 64
COLS = 256
CG_DEV = 8
LEVELS = 4
PHIBLK = 32
PB_DEV = 4
SLOTS = 32
NB = 4096
NCG = 128
N_TILE = 16
N_PHI = 8


def block_layout(key):
    base = jax.random.fold_in(key, 11)
    keys = jax.random.split(base, 5)
    tile_count = N_TILE
    plane_count = N_PHI
    device_count = tile_count * plane_count
    average = SLOTS // tile_count

    def plane_counts(plane_key):
        order_key, delta_key = jax.random.split(plane_key)
        order = jax.random.permutation(order_key, tile_count)
        deltas = jax.random.randint(delta_key, (tile_count // 2,), 0, average + 1).at[0].set(average)
        counts = jnp.zeros((tile_count,), jnp.int32)
        counts = counts.at[order[0::2]].set(average + deltas)
        counts = counts.at[order[1::2]].set(average - deltas)
        return counts
    counts = jax.vmap(plane_counts)(jax.random.split(keys[0], plane_count))
    rho = jax.vmap(lambda kk: jax.random.permutation(kk, tile_count))(jax.random.split(keys[1], plane_count))
    tau = jax.vmap(lambda kk: jax.random.permutation(kk, tile_count))(jax.random.split(keys[2], plane_count))
    shift_table = jax.vmap(lambda cc: jnp.repeat(jnp.arange(tile_count, dtype=jnp.int32), cc, total_repeat_length=SLOTS))(counts)
    slot_perms = jax.vmap(lambda kk: jax.random.permutation(kk, SLOTS))(jax.random.split(keys[3], device_count))
    source = jnp.arange(device_count, dtype=jnp.int32)
    source_tile = source // plane_count
    source_plane = source % plane_count
    shifts = shift_table[source_plane[:, None], slot_perms]
    dest = rho[source_plane[:, None], (tau[source_plane, source_tile][:, None] + shifts) % tile_count]
    plane_full = jnp.broadcast_to(source_plane[:, None], (device_count, SLOTS))
    receiver = (dest * plane_count + plane_full).reshape(NB)
    onehot_dest = (receiver[:, None] == jnp.arange(device_count, dtype=jnp.int32)[None, :]).astype(jnp.int32)
    arrival = jnp.sum((jnp.cumsum(onehot_dest, axis=0) - 1) * onehot_dest, axis=1)
    place_perms = jax.vmap(lambda kk: jax.random.permutation(kk, SLOTS))(jax.random.split(keys[4], device_count))
    position = place_perms[receiver, arrival]
    return (dest.reshape(NB).astype(jnp.int32), (position // CG_DEV).astype(jnp.int32), (position % CG_DEV).astype(jnp.int32))


def draw_block_dest(key, part):
    return block_layout(key)[0]


def draw_block_phi(key, part):
    return block_layout(key)[1]


def draw_block_group(key, part):
    return block_layout(key)[2]


def set_ends(values, rng, least, top_value):
    longest = values.shape.index(max(values.shape))
    spots = []
    for shift in (0, 1):
        where = [jax.random.randint(jax.random.fold_in(rng, axis), (), 0, length) for axis, length in enumerate(values.shape)]
        where[longest] = (where[longest] + shift) % values.shape[longest]
        spots.append(tuple(where))
    return values.at[spots[0]].set(least).at[spots[1]].set(top_value)


def block_scale(own_key, extent, cuts, least, largest):
    level = 1.0
    for dim, parts in cuts:
        steps = jax.random.uniform(jax.random.fold_in(jax.random.fold_in(own_key, 6), dim), (parts,), jnp.float32, least / len(cuts), largest / len(cuts))
        level = level * jnp.repeat(jnp.exp(steps), extent[dim] // parts).reshape((-1,) + (1,) * (len(extent) - 1 - dim))
    return level


def centred(stream_key, shape, deviation, bound, pieces=(), held_as=jnp.bfloat16):
    entries = jax.random.normal(stream_key, shape, jnp.float32) * deviation
    if len(pieces) > 0:
        entries = block_scale(stream_key, shape, pieces, -0.22, 0.18) * entries
    return jnp.clip(entries, min=-bound, max=bound).astype(held_as)


def setup_inputs(seed: int = 0) -> dict:
    splits = jax.random.split(jax.random.key(seed), 6)
    blocks = centred(splits[0], (NB, FIELDS, BPHI, COLS), 1.0, 6.0, ((0, 128),))
    levels = set_ends(jax.random.randint(splits[1], (NB,), 0, LEVELS), jax.random.fold_in(splits[1], 1), 0, LEVELS - 1).astype(jnp.int32)
    block_dest = draw_block_dest(jax.random.fold_in(splits[5], 71), 0)
    block_phi = draw_block_phi(jax.random.fold_in(splits[5], 71), 0)
    block_group = draw_block_group(jax.random.fold_in(splits[5], 71), 0)
    return {"blocks": blocks, "levels": levels, "block_dest": block_dest, "block_phi": block_phi, "block_group": block_group}


def dft_basis(length):
    column = jnp.arange(length, dtype=jnp.int32)
    half = length // 2
    mode = jnp.where(column <= half, column, column - half)
    phase = column[:, None] * mode[None, :] % length
    angle = phase.astype(jnp.float32) * jnp.float32(2.0 * math.pi / length)
    values = jnp.where((column <= half)[None, :], jnp.cos(angle), jnp.sin(angle))
    return (values * jnp.float32(1.0 / math.sqrt(length))).astype(jnp.bfloat16)

def reference(blocks, levels, block_dest, block_phi, block_group):
    weight = (1.0 / jnp.left_shift(1, levels).astype(jnp.float32)).astype(jnp.bfloat16)
    weighted = blocks * weight[:, None, None, None]
    index_all = jnp.arange(NB, dtype=jnp.int32)
    segment = index_all // SLOTS % N_PHI
    global_phi = (segment * PB_DEV + block_phi).astype(jnp.int32)
    global_group = (block_dest * CG_DEV + block_group).astype(jnp.int32)
    field = jnp.zeros((PHIBLK, NCG, FIELDS, BPHI, COLS), jnp.bfloat16)
    field = field.at[global_phi, global_group].set(weighted)
    basis_table = dft_basis(NPHI).astype(jnp.float32)

    def one_group(group_index):
        column_block = field[:, group_index]
        column_block = jnp.transpose(column_block, (1, 0, 2, 3)).reshape(FIELDS, NPHI, COLS)
        return jnp.einsum('fpc,pk->fck', column_block.astype(jnp.float32), basis_table, precision=lax.Precision.HIGHEST)
    stacked = lax.map(one_group, jnp.arange(NCG, dtype=jnp.int32))
    return jnp.transpose(stacked, (1, 0, 2, 3))
```

```python
import math

import jax
import jax.numpy as jnp
from jax import lax
from jax.sharding import PartitionSpec as P

FIELDS = 5
NPHI = 2048
BPHI = 64
COLS = 256
CG_DEV = 8


def dft_basis(length):
    half = length // 2
    column = jnp.arange(length, dtype=jnp.int32)
    mode = jnp.where(column <= half, column, column - half)
    scale = jnp.float32(2.0 * math.pi / length)
    hi = jnp.arange(length // BPHI, dtype=jnp.int32) * BPHI
    lo = jnp.arange(BPHI, dtype=jnp.int32)
    angle_hi = (hi[:, None] * mode[None, :] % length).astype(jnp.float32) * scale
    angle_lo = (lo[:, None] * mode[None, :] % length).astype(jnp.float32) * scale
    ch, sh = jnp.cos(angle_hi)[:, None, :], jnp.sin(angle_hi)[:, None, :]
    cl, sl = jnp.cos(angle_lo)[None, :, :], jnp.sin(angle_lo)[None, :, :]
    is_cos = (column <= half)[None, None, :]
    values = jnp.where(is_cos, ch * cl - sh * sl, sh * cl + ch * sl)
    values = values * jnp.float32(1.0 / math.sqrt(length))
    return values.reshape(length, length).astype(jnp.bfloat16)


def local(blocks, levels, block_dest, block_phi, block_group):
    tile_count = lax.axis_size("tile")
    plane_count = lax.axis_size("phi")
    slot_count = blocks.shape[0]
    fields = blocks.shape[1]
    per_plane = NPHI // BPHI // plane_count
    capacity = 2 * slot_count // tile_count
    sliver = COLS // plane_count
    weight = (1.0 / jnp.left_shift(1, levels).astype(jnp.float32)).astype(jnp.bfloat16)

    onehot_dest = (block_dest[:, None] == jnp.arange(tile_count, dtype=jnp.int32)[None, :]).astype(
        jnp.int32
    )
    slot_rank = jnp.sum((jnp.cumsum(onehot_dest, axis=0) - 1) * onehot_dest, axis=1)
    send_slot = block_dest * capacity + slot_rank
    slot_ids = jnp.arange(tile_count * capacity, dtype=jnp.int32)
    match = send_slot[None, :] == slot_ids[:, None]
    filled = jnp.any(match, axis=1)
    source = jnp.argmax(match, axis=1).astype(jnp.int32)
    slot_weight = jnp.where(filled, weight[source], jnp.zeros((), jnp.bfloat16))
    outbox = blocks[source] * slot_weight[:, None, None, None]
    code = jnp.where(filled, block_phi[source] * CG_DEV + block_group[source], -1)

    arrived = lax.all_to_all(outbox, "tile", split_axis=0, concat_axis=0, tiled=True)
    arrived_code = lax.all_to_all(code, "tile", split_axis=0, concat_axis=0, tiled=True)

    want = jnp.arange(slot_count, dtype=jnp.int32)
    pick = jnp.argmax(arrived_code[None, :] == want[:, None], axis=1).astype(jnp.int32)
    arranged = arrived[pick].reshape(per_plane, CG_DEV, fields, BPHI, plane_count, sliver)
    outgoing = jnp.transpose(arranged, (4, 0, 3, 2, 1, 5)).reshape(
        plane_count, per_plane * BPHI, fields, CG_DEV * sliver
    )
    pieces = lax.all_to_all(outgoing, "phi", split_axis=0, concat_axis=0, tiled=True)
    pieces = pieces.reshape(NPHI, fields, CG_DEV * sliver)
    basis = dft_basis(NPHI)
    spectra = lax.dot_general(
        pieces, basis, (((0,), (0,)), ((), ())), preferred_element_type=jnp.float32
    )
    return spectra.reshape(fields, CG_DEV, sliver, NPHI)


def solution(mesh):
    in_specs = (
        P(("tile", "phi"), None, None, None),
        P(("tile", "phi")),
        P(("tile", "phi")),
        P(("tile", "phi")),
        P(("tile", "phi")),
    )
    out_specs = P(None, "tile", "phi", None)
    return jax.shard_map(local, mesh=mesh, in_specs=in_specs, out_specs=out_specs, check_vma=False)
```

```python
import functools
import math

import jax
import jax.numpy as jnp
from jax import lax
from jax.experimental import pallas as pl
from jax.experimental.pallas import tpu as pltpu
from jax.sharding import PartitionSpec as P

FIELDS = 5
NPHI = 2048
BPHI = 64
COLS = 256
CG_DEV = 8


def dft_basis(length):
    half = length // 2
    column = jnp.arange(length, dtype=jnp.int32)
    mode = jnp.where(column <= half, column, column - half)
    scale = jnp.float32(2.0 * math.pi / length)
    hi = jnp.arange(length // BPHI, dtype=jnp.int32) * BPHI
    lo = jnp.arange(BPHI, dtype=jnp.int32)
    angle_hi = (hi[:, None] * mode[None, :] % length).astype(jnp.float32) * scale
    angle_lo = (lo[:, None] * mode[None, :] % length).astype(jnp.float32) * scale
    ch, sh = jnp.cos(angle_hi)[:, None, :], jnp.sin(angle_hi)[:, None, :]
    cl, sl = jnp.cos(angle_lo)[None, :, :], jnp.sin(angle_lo)[None, :, :]
    is_cos = (column <= half)[None, None, :]
    values = jnp.where(is_cos, ch * cl - sh * sl, sh * cl + ch * sl)
    values = values * jnp.float32(1.0 / math.sqrt(length))
    return values.reshape(length, length).astype(jnp.bfloat16)


def exchange_kernel(tile_count, capacity, src_ref, dst_ref, send_sem, recv_sem, own_sem):
    me = lax.axis_index("tile")
    plane = lax.axis_index("phi")
    mesh_ids = pl.DeviceIdType.MESH
    barrier = pltpu.get_barrier_semaphore()
    for step in range(1, tile_count):
        peer = lax.rem(me + step, tile_count)
        pl.semaphore_signal(barrier, inc=1, device_id=(peer, plane), device_id_type=mesh_ids)
    pl.semaphore_wait(barrier, tile_count - 1)
    own = pltpu.make_async_copy(
        src_ref.at[pl.ds(me * capacity, capacity)],
        dst_ref.at[pl.ds(me * capacity, capacity)],
        own_sem,
    )
    own.start()
    copies = []
    for step in range(1, tile_count):
        peer = lax.rem(me + step, tile_count)
        copy = pltpu.make_async_remote_copy(
            src_ref=src_ref.at[pl.ds(peer * capacity, capacity)],
            dst_ref=dst_ref.at[pl.ds(me * capacity, capacity)],
            send_sem=send_sem.at[step],
            recv_sem=recv_sem.at[step],
            device_id=(peer, plane),
            device_id_type=mesh_ids,
        )
        copy.start()
        copies.append(copy)
    for copy in copies:
        copy.wait()
    own.wait()


def tile_exchange(outbox, tile_count, capacity):
    return pl.pallas_call(
        functools.partial(exchange_kernel, tile_count, capacity),
        out_shape=jax.ShapeDtypeStruct(outbox.shape, outbox.dtype),
        in_specs=[pl.BlockSpec(memory_space=pl.ANY)],
        out_specs=pl.BlockSpec(memory_space=pl.ANY),
        scratch_shapes=[
            pltpu.SemaphoreType.DMA((tile_count,)),
            pltpu.SemaphoreType.DMA((tile_count,)),
            pltpu.SemaphoreType.DMA,
        ],
        compiler_params=pltpu.CompilerParams(collective_id=0, has_side_effects=True),
    )(outbox)


def local(blocks, levels, block_dest, block_phi, block_group):
    tile_count = lax.axis_size("tile")
    plane_count = lax.axis_size("phi")
    slot_count = blocks.shape[0]
    fields = blocks.shape[1]
    per_plane = NPHI // BPHI // plane_count
    capacity = 2 * slot_count // tile_count
    sliver = COLS // plane_count
    onehot_dest = (block_dest[:, None] == jnp.arange(tile_count, dtype=jnp.int32)[None, :]).astype(
        jnp.int32
    )
    slot_rank = jnp.sum((jnp.cumsum(onehot_dest, axis=0) - 1) * onehot_dest, axis=1)
    send_slot = block_dest * capacity + slot_rank
    slot_ids = jnp.arange(tile_count * capacity, dtype=jnp.int32)
    match = send_slot[None, :] == slot_ids[:, None]
    filled = jnp.any(match, axis=1)
    source = jnp.argmax(match, axis=1).astype(jnp.int32)
    outbox = blocks[source]
    place = block_phi[source] * CG_DEV + block_group[source]
    code = jnp.where(filled, levels[source] * slot_count + place, -1)

    arrived = tile_exchange(outbox, tile_count, capacity)
    arrived_code = lax.all_to_all(code, "tile", split_axis=0, concat_axis=0, tiled=True)

    want = jnp.arange(slot_count, dtype=jnp.int32)
    hit = (arrived_code[None, :] % slot_count == want[:, None]) & (arrived_code[None, :] >= 0)
    pick = jnp.argmax(hit, axis=1).astype(jnp.int32)
    level_of = arrived_code[pick] // slot_count
    weight = (1.0 / jnp.left_shift(1, level_of).astype(jnp.float32)).astype(jnp.bfloat16)
    arranged = arrived[pick] * weight[:, None, None, None]
    arranged = arranged.reshape(per_plane, CG_DEV, fields, BPHI, plane_count, sliver)
    outgoing = jnp.transpose(arranged, (4, 0, 3, 2, 1, 5)).reshape(
        plane_count, per_plane * BPHI, fields, CG_DEV * sliver
    )
    pieces = lax.all_to_all(outgoing, "phi", split_axis=0, concat_axis=0, tiled=True)
    pieces = pieces.reshape(NPHI, fields, CG_DEV * sliver)
    basis = dft_basis(NPHI)
    spectra = lax.dot_general(
        pieces, basis, (((0,), (0,)), ((), ())), preferred_element_type=jnp.float32
    )
    return spectra.reshape(fields, CG_DEV, sliver, NPHI)


def solution(mesh):
    in_specs = (
        P(("tile", "phi"), None, None, None),
        P(("tile", "phi")),
        P(("tile", "phi")),
        P(("tile", "phi")),
        P(("tile", "phi")),
    )
    out_specs = P(None, "tile", "phi", None)
    return jax.shard_map(local, mesh=mesh, in_specs=in_specs, out_specs=out_specs, check_vma=False)
```

```python
import math

import jax
import jax.numpy as jnp
from jax import lax
from jax.sharding import PartitionSpec as P

FIELDS = 5
NPHI = 2048
BPHI = 64
COLS = 256
CG_DEV = 8


def dft_basis(length):
    half = length // 2
    column = jnp.arange(length, dtype=jnp.int32)
    mode = jnp.where(column <= half, column, column - half)
    scale = jnp.float32(2.0 * math.pi / length)
    hi = jnp.arange(length // BPHI, dtype=jnp.int32) * BPHI
    lo = jnp.arange(BPHI, dtype=jnp.int32)
    angle_hi = (hi[:, None] * mode[None, :] % length).astype(jnp.float32) * scale
    angle_lo = (lo[:, None] * mode[None, :] % length).astype(jnp.float32) * scale
    ch, sh = jnp.cos(angle_hi)[:, None, :], jnp.sin(angle_hi)[:, None, :]
    cl, sl = jnp.cos(angle_lo)[None, :, :], jnp.sin(angle_lo)[None, :, :]
    is_cos = (column <= half)[None, None, :]
    values = jnp.where(is_cos, ch * cl - sh * sl, sh * cl + ch * sl)
    values = values * jnp.float32(1.0 / math.sqrt(length))
    return values.reshape(length, length).astype(jnp.bfloat16)


def local(blocks, levels, block_dest, block_phi, block_group):
    tile_count = lax.axis_size("tile")
    plane_count = lax.axis_size("phi")
    slot_count = blocks.shape[0]
    fields = blocks.shape[1]
    per_plane = NPHI // BPHI // plane_count
    capacity = 2 * slot_count // tile_count
    sliver = COLS // plane_count
    weight = (1.0 / jnp.left_shift(1, levels).astype(jnp.float32)).astype(jnp.bfloat16)

    onehot_dest = (block_dest[:, None] == jnp.arange(tile_count, dtype=jnp.int32)[None, :]).astype(
        jnp.int32
    )
    slot_rank = jnp.sum((jnp.cumsum(onehot_dest, axis=0) - 1) * onehot_dest, axis=1)
    send_slot = block_dest * capacity + slot_rank
    slot_ids = jnp.arange(tile_count * capacity, dtype=jnp.int32)
    match = send_slot[None, :] == slot_ids[:, None]
    filled = jnp.any(match, axis=1)
    source = jnp.argmax(match, axis=1).astype(jnp.int32)
    place = block_phi[source] * CG_DEV + block_group[source]
    code = jnp.where(filled, levels[source] * slot_count + place, -1)
    arrived_code = lax.all_to_all(code, "tile", split_axis=0, concat_axis=0, tiled=True)

    want = jnp.arange(slot_count, dtype=jnp.int32)
    hit = (arrived_code[None, :] % slot_count == want[:, None]) & (arrived_code[None, :] >= 0)
    pick = jnp.argmax(hit, axis=1).astype(jnp.int32)
    level_of = arrived_code[pick] // slot_count
    weight = (1.0 / jnp.left_shift(1, level_of).astype(jnp.float32)).astype(jnp.bfloat16)
    basis = dft_basis(NPHI)

    parts = []
    for field in range(fields):
        outbox = blocks[:, field][source]
        arrived = lax.all_to_all(outbox, "tile", split_axis=0, concat_axis=0, tiled=True)
        arranged = arrived[pick] * weight[:, None, None]
        arranged = arranged.reshape(per_plane, CG_DEV, BPHI, plane_count, sliver)
        outgoing = jnp.transpose(arranged, (3, 0, 2, 1, 4)).reshape(
            plane_count, per_plane * BPHI, CG_DEV * sliver
        )
        pieces = lax.all_to_all(outgoing, "phi", split_axis=0, concat_axis=0, tiled=True)
        pieces = pieces.reshape(NPHI, CG_DEV * sliver)
        parts.append(
            lax.dot_general(
                pieces, basis, (((0,), (0,)), ((), ())), preferred_element_type=jnp.float32
            )
        )
    spectra = jnp.stack(parts)
    return spectra.reshape(fields, CG_DEV, sliver, NPHI)


def solution(mesh):
    in_specs = (
        P(("tile", "phi"), None, None, None),
        P(("tile", "phi")),
        P(("tile", "phi")),
        P(("tile", "phi")),
        P(("tile", "phi")),
    )
    out_specs = P(None, "tile", "phi", None)
    return jax.shard_map(local, mesh=mesh, in_specs=in_specs, out_specs=out_specs, check_vma=False)
```

```python
import math

import jax
import jax.numpy as jnp
from jax import lax
from jax.sharding import PartitionSpec as P

FIELDS = 5
NPHI = 2048
BPHI = 64
COLS = 256
CG_DEV = 8


def dft_basis(length):
    half = length // 2
    column = jnp.arange(length, dtype=jnp.int32)
    mode = jnp.where(column <= half, column, column - half)
    scale = jnp.float32(2.0 * math.pi / length)
    hi = jnp.arange(length // BPHI, dtype=jnp.int32) * BPHI
    lo = jnp.arange(BPHI, dtype=jnp.int32)
    angle_hi = (hi[:, None] * mode[None, :] % length).astype(jnp.float32) * scale
    angle_lo = (lo[:, None] * mode[None, :] % length).astype(jnp.float32) * scale
    ch, sh = jnp.cos(angle_hi)[:, None, :], jnp.sin(angle_hi)[:, None, :]
    cl, sl = jnp.cos(angle_lo)[None, :, :], jnp.sin(angle_lo)[None, :, :]
    is_cos = (column <= half)[None, None, :]
    values = jnp.where(is_cos, ch * cl - sh * sl, sh * cl + ch * sl)
    values = values * jnp.float32(1.0 / math.sqrt(length))
    return values.reshape(length, length).astype(jnp.bfloat16)


def local(blocks, levels, block_dest, block_phi, block_group):
    tile_count = lax.axis_size("tile")
    plane_count = lax.axis_size("phi")
    slot_count = blocks.shape[0]
    fields = blocks.shape[1]
    per_plane = NPHI // BPHI // plane_count
    capacity = 2 * slot_count // tile_count
    sliver = COLS // plane_count
    weight = (1.0 / jnp.left_shift(1, levels).astype(jnp.float32)).astype(jnp.bfloat16)

    onehot_dest = (block_dest[:, None] == jnp.arange(tile_count, dtype=jnp.int32)[None, :]).astype(
        jnp.int32
    )
    slot_rank = jnp.sum((jnp.cumsum(onehot_dest, axis=0) - 1) * onehot_dest, axis=1)
    send_slot = block_dest * capacity + slot_rank
    slot_ids = jnp.arange(tile_count * capacity, dtype=jnp.int32)
    match = send_slot[None, :] == slot_ids[:, None]
    filled = jnp.any(match, axis=1)
    source = jnp.argmax(match, axis=1).astype(jnp.int32)
    place = block_phi[source] * CG_DEV + block_group[source]
    code = jnp.where(filled, levels[source] * slot_count + place, -1)
    device_count = tile_count * plane_count

    outbox = blocks[source].reshape(tile_count, capacity, fields, BPHI, plane_count, sliver)
    outbox = jnp.transpose(outbox, (0, 4, 1, 2, 3, 5)).reshape(
        device_count, capacity, fields, BPHI, sliver
    )
    code_out = jnp.broadcast_to(
        code.reshape(tile_count, 1, capacity), (tile_count, plane_count, capacity)
    ).reshape(device_count, capacity)
    arrived = lax.all_to_all(outbox, ("tile", "phi"), split_axis=0, concat_axis=0, tiled=True)
    arrived_code = lax.all_to_all(code_out, ("tile", "phi"), split_axis=0, concat_axis=0, tiled=True)

    by_segment = jnp.transpose(
        arrived_code.reshape(tile_count, plane_count, capacity), (1, 0, 2)
    ).reshape(plane_count, tile_count * capacity)
    want = jnp.arange(slot_count, dtype=jnp.int32)
    hit = (by_segment[:, None, :] % slot_count == want[None, :, None]) & (
        by_segment[:, None, :] >= 0
    )
    pick = jnp.argmax(hit, axis=2).astype(jnp.int32)
    origin = pick // capacity
    segment = jnp.arange(plane_count, dtype=jnp.int32)[:, None]
    flat = (origin * plane_count + segment) * capacity + pick % capacity
    level_of = jnp.take_along_axis(by_segment, pick, axis=1) // slot_count
    weight = (1.0 / jnp.left_shift(1, level_of).astype(jnp.float32)).astype(jnp.bfloat16)
    gathered = arrived.reshape(device_count * capacity, fields, BPHI, sliver)[flat.reshape(-1)]
    gathered = gathered * weight.reshape(-1)[:, None, None, None]
    gathered = gathered.reshape(plane_count, per_plane, CG_DEV, fields, BPHI, sliver)
    pieces = jnp.transpose(gathered, (0, 1, 4, 3, 2, 5)).reshape(NPHI, fields, CG_DEV * sliver)
    basis = dft_basis(NPHI)
    spectra = lax.dot_general(
        pieces, basis, (((0,), (0,)), ((), ())), preferred_element_type=jnp.float32
    )
    return spectra.reshape(fields, CG_DEV, sliver, NPHI)


def solution(mesh):
    in_specs = (
        P(("tile", "phi"), None, None, None),
        P(("tile", "phi")),
        P(("tile", "phi")),
        P(("tile", "phi")),
        P(("tile", "phi")),
    )
    out_specs = P(None, "tile", "phi", None)
    return jax.shard_map(local, mesh=mesh, in_specs=in_specs, out_specs=out_specs, check_vma=False)
```

```python
import functools
import math

import jax
import jax.numpy as jnp
from jax import lax
from jax.experimental import pallas as pl
from jax.experimental.pallas import tpu as pltpu
from jax.sharding import PartitionSpec as P

FIELDS = 5
NPHI = 2048
BPHI = 64
COLS = 256
CG_DEV = 8


def dft_basis(length):
    half = length // 2
    column = jnp.arange(length, dtype=jnp.int32)
    mode = jnp.where(column <= half, column, column - half)
    scale = jnp.float32(2.0 * math.pi / length)
    hi = jnp.arange(length // BPHI, dtype=jnp.int32) * BPHI
    lo = jnp.arange(BPHI, dtype=jnp.int32)
    angle_hi = (hi[:, None] * mode[None, :] % length).astype(jnp.float32) * scale
    angle_lo = (lo[:, None] * mode[None, :] % length).astype(jnp.float32) * scale
    ch, sh = jnp.cos(angle_hi)[:, None, :], jnp.sin(angle_hi)[:, None, :]
    cl, sl = jnp.cos(angle_lo)[None, :, :], jnp.sin(angle_lo)[None, :, :]
    is_cos = (column <= half)[None, None, :]
    values = jnp.where(is_cos, ch * cl - sh * sl, sh * cl + ch * sl)
    values = values * jnp.float32(1.0 / math.sqrt(length))
    return values.reshape(length, length).astype(jnp.bfloat16)


def pack_kernel(source_ref, scale_ref, first_ref, second_ref, out_ref):
    tile = pl.program_id(0)
    pair = pl.program_id(1)
    slot = (tile * pl.num_programs(1) + pair) * 2
    first_scale = scale_ref[slot]
    second_scale = scale_ref[slot + 1]
    fields, planes, sliver = out_ref.shape[3], out_ref.shape[1], out_ref.shape[4]
    for field in range(fields):
        both = jnp.concatenate(
            [
                first_ref[0, field].astype(jnp.float32) * first_scale,
                second_ref[0, field].astype(jnp.float32) * second_scale,
            ],
            axis=0,
        )
        flipped = both.T.reshape(planes, sliver, both.shape[0])
        out_ref[0, :, 0, field] = flipped.astype(out_ref.dtype)


def pack_outbox(blocks, source, scale, tile_count, capacity, plane_count):
    slot_count, fields, bphi, cols = blocks.shape
    pairs = capacity // 2
    sliver = cols // plane_count

    def block_map(half):
        return lambda t, q, src_ref: (src_ref[(t * pairs + q) * 2 + half], 0, 0, 0)

    return pl.pallas_call(
        pack_kernel,
        out_shape=jax.ShapeDtypeStruct(
            (tile_count, plane_count, pairs, fields, sliver, 2 * bphi), blocks.dtype
        ),
        grid_spec=pltpu.PrefetchScalarGridSpec(
            num_scalar_prefetch=1,
            grid=(tile_count, pairs),
            in_specs=[
                pl.BlockSpec(memory_space=pltpu.SMEM),
                pl.BlockSpec((1, fields, bphi, cols), block_map(0)),
                pl.BlockSpec((1, fields, bphi, cols), block_map(1)),
            ],
            out_specs=pl.BlockSpec(
                (1, plane_count, 1, fields, sliver, 2 * bphi),
                lambda t, q, src_ref: (t, 0, q, 0, 0, 0),
            ),
        ),
    )(source, scale, blocks, blocks)


def unpack_kernel(groups, row_ref, half_ref, *refs):
    out_ref = refs[-1]
    segment = pl.program_id(0)
    quad = pl.program_id(1)
    lanes = out_ref.shape[-1]
    shape = out_ref.shape[:1] + out_ref.shape[2:]
    lane = lax.broadcasted_iota(jnp.int32, shape, 2)
    for group in range(groups):
        parts = []
        for side in range(2):
            index = ((segment * 2 * pl.num_programs(1) + quad * 2 + side) * groups) + group
            piece = refs[group * 2 + side][0].astype(jnp.float32)
            turned = pltpu.roll(piece, lanes // 2, 2)
            keep = half_ref[index] == side
            parts.append(jnp.where(keep, piece, turned))
        merged = jnp.where(lane < lanes // 2, parts[0], parts[1])
        out_ref[:, group] = merged.astype(out_ref.dtype)


def unpack_lhs(landed, row, half, plane_count, per_plane, groups):
    _, fields, sliver, lanes = landed.shape
    quads = per_plane // 2

    def piece_map(side, group):
        def index_map(s, q, row_ref, half_ref):
            return (row_ref[((s * per_plane + q * 2 + side) * groups) + group], 0, 0, 0)

        return index_map

    in_specs = [
        pl.BlockSpec((1, fields, sliver, lanes), piece_map(side, group))
        for group in range(groups)
        for side in range(2)
    ]
    return pl.pallas_call(
        functools.partial(unpack_kernel, groups),
        out_shape=jax.ShapeDtypeStruct(
            (fields, groups, sliver, plane_count * per_plane * lanes // 2), landed.dtype
        ),
        grid_spec=pltpu.PrefetchScalarGridSpec(
            num_scalar_prefetch=2,
            grid=(plane_count, quads),
            in_specs=in_specs,
            out_specs=pl.BlockSpec(
                (fields, groups, sliver, lanes),
                lambda s, q, row_ref, half_ref: (0, 0, 0, s * quads + q),
            ),
        ),
    )(row, half, *([landed] * (2 * groups)))


def local(blocks, levels, block_dest, block_phi, block_group):
    tile_count = lax.axis_size("tile")
    plane_count = lax.axis_size("phi")
    slot_count = blocks.shape[0]
    fields = blocks.shape[1]
    per_plane = NPHI // BPHI // plane_count
    capacity = 2 * slot_count // tile_count
    sliver = COLS // plane_count

    onehot_dest = (block_dest[:, None] == jnp.arange(tile_count, dtype=jnp.int32)[None, :]).astype(
        jnp.int32
    )
    slot_rank = jnp.sum((jnp.cumsum(onehot_dest, axis=0) - 1) * onehot_dest, axis=1)
    send_slot = block_dest * capacity + slot_rank
    slot_ids = jnp.arange(tile_count * capacity, dtype=jnp.int32)
    match = send_slot[None, :] == slot_ids[:, None]
    filled = jnp.any(match, axis=1)
    source = jnp.argmax(match, axis=1).astype(jnp.int32)
    place = block_phi[source] * CG_DEV + block_group[source]
    code = jnp.where(filled, place, -1)
    scale = 1.0 / jnp.left_shift(1, levels[source]).astype(jnp.float32)
    device_count = tile_count * plane_count
    pairs = capacity // 2

    outbox = pack_outbox(blocks, source, scale, tile_count, capacity, plane_count)
    outbox = outbox.reshape(device_count, pairs * fields * sliver, 2 * BPHI)
    code_out = jnp.broadcast_to(
        code.reshape(tile_count, 1, capacity), (tile_count, plane_count, capacity)
    ).reshape(device_count, capacity)
    arrived = lax.all_to_all(outbox, ("tile", "phi"), split_axis=0, concat_axis=0, tiled=True)
    arrived_code = lax.all_to_all(code_out, ("tile", "phi"), split_axis=0, concat_axis=0, tiled=True)

    by_segment = jnp.transpose(
        arrived_code.reshape(tile_count, plane_count, capacity), (1, 0, 2)
    ).reshape(plane_count, tile_count * capacity)
    want = jnp.arange(slot_count, dtype=jnp.int32)
    hit = by_segment[:, None, :] == want[None, :, None]
    pick = jnp.argmax(hit, axis=2).astype(jnp.int32)
    origin = pick // capacity
    segment = jnp.arange(plane_count, dtype=jnp.int32)[:, None]
    row = ((origin * plane_count + segment) * pairs + (pick % capacity) // 2).reshape(-1)
    half = (pick % 2).reshape(-1)
    landed = arrived.reshape(device_count * pairs, fields, sliver, 2 * BPHI)
    lhs = unpack_lhs(landed, row, half, plane_count, per_plane, CG_DEV)
    basis = dft_basis(NPHI)
    spectra = jnp.dot(
        lhs.reshape(fields * CG_DEV * sliver, NPHI), basis, preferred_element_type=jnp.float32
    )
    return spectra.reshape(fields, CG_DEV, sliver, NPHI)


def solution(mesh):
    in_specs = (
        P(("tile", "phi"), None, None, None),
        P(("tile", "phi")),
        P(("tile", "phi")),
        P(("tile", "phi")),
        P(("tile", "phi")),
    )
    out_specs = P(None, "tile", "phi", None)
    return jax.shard_map(local, mesh=mesh, in_specs=in_specs, out_specs=out_specs, check_vma=False)
```

```python
import functools
import math

import jax
import jax.numpy as jnp
from jax import lax
from jax.experimental import pallas as pl
from jax.experimental.pallas import tpu as pltpu
from jax.sharding import PartitionSpec as P

FIELDS = 5
NPHI = 2048
BPHI = 64
COLS = 256
CG_DEV = 8


def dft_basis(length):
    half = length // 2
    column = jnp.arange(length, dtype=jnp.int32)
    mode = jnp.where(column <= half, column, column - half)
    scale = jnp.float32(2.0 * math.pi / length)
    hi = jnp.arange(length // BPHI, dtype=jnp.int32) * BPHI
    lo = jnp.arange(BPHI, dtype=jnp.int32)
    angle_hi = (hi[:, None] * mode[None, :] % length).astype(jnp.float32) * scale
    angle_lo = (lo[:, None] * mode[None, :] % length).astype(jnp.float32) * scale
    ch, sh = jnp.cos(angle_hi)[:, None, :], jnp.sin(angle_hi)[:, None, :]
    cl, sl = jnp.cos(angle_lo)[None, :, :], jnp.sin(angle_lo)[None, :, :]
    is_cos = (column <= half)[None, None, :]
    values = jnp.where(is_cos, ch * cl - sh * sl, sh * cl + ch * sl)
    values = values * jnp.float32(1.0 / math.sqrt(length))
    return values.reshape(length, length).astype(jnp.bfloat16)


def pack_kernel(source_ref, scale_ref, first_ref, second_ref, out_ref):
    tile = pl.program_id(0)
    pair = pl.program_id(1)
    slot = (tile * pl.num_programs(1) + pair) * 2
    first_scale = scale_ref[slot]
    second_scale = scale_ref[slot + 1]
    fields, planes, sliver = out_ref.shape[3], out_ref.shape[1], out_ref.shape[4]
    for field in range(fields):
        both = jnp.concatenate(
            [
                first_ref[0, field].astype(jnp.float32) * first_scale,
                second_ref[0, field].astype(jnp.float32) * second_scale,
            ],
            axis=0,
        )
        flipped = both.T.reshape(planes, sliver, both.shape[0])
        out_ref[0, :, 0, field] = flipped.astype(out_ref.dtype)


def pack_outbox(blocks, source, scale, tile_count, capacity, plane_count, field):
    slot_count, _, bphi, cols = blocks.shape
    fields = 1
    pairs = capacity // 2
    sliver = cols // plane_count

    def block_map(half):
        return lambda t, q, src_ref: (src_ref[(t * pairs + q) * 2 + half], field, 0, 0)

    return pl.pallas_call(
        pack_kernel,
        out_shape=jax.ShapeDtypeStruct(
            (tile_count, plane_count, pairs, fields, sliver, 2 * bphi), blocks.dtype
        ),
        grid_spec=pltpu.PrefetchScalarGridSpec(
            num_scalar_prefetch=1,
            grid=(tile_count, pairs),
            in_specs=[
                pl.BlockSpec(memory_space=pltpu.SMEM),
                pl.BlockSpec((1, fields, bphi, cols), block_map(0)),
                pl.BlockSpec((1, fields, bphi, cols), block_map(1)),
            ],
            out_specs=pl.BlockSpec(
                (1, plane_count, 1, fields, sliver, 2 * bphi),
                lambda t, q, src_ref: (t, 0, q, 0, 0, 0),
            ),
        ),
    )(source, scale, blocks, blocks)


def unpack_kernel(groups, row_ref, half_ref, *refs):
    out_ref = refs[-1]
    segment = pl.program_id(0)
    quad = pl.program_id(1)
    lanes = out_ref.shape[-1]
    shape = out_ref.shape[:1] + out_ref.shape[2:]
    lane = lax.broadcasted_iota(jnp.int32, shape, 2)
    for group in range(groups):
        parts = []
        for side in range(2):
            index = ((segment * 2 * pl.num_programs(1) + quad * 2 + side) * groups) + group
            piece = refs[group * 2 + side][0].astype(jnp.float32)
            turned = pltpu.roll(piece, lanes // 2, 2)
            keep = half_ref[index] == side
            parts.append(jnp.where(keep, piece, turned))
        merged = jnp.where(lane < lanes // 2, parts[0], parts[1])
        out_ref[:, group] = merged.astype(out_ref.dtype)


def unpack_lhs(landed, row, half, plane_count, per_plane, groups):
    _, fields, sliver, lanes = landed.shape
    quads = per_plane // 2

    def piece_map(side, group):
        def index_map(s, q, row_ref, half_ref):
            return (row_ref[((s * per_plane + q * 2 + side) * groups) + group], 0, 0, 0)

        return index_map

    in_specs = [
        pl.BlockSpec((1, fields, sliver, lanes), piece_map(side, group))
        for group in range(groups)
        for side in range(2)
    ]
    return pl.pallas_call(
        functools.partial(unpack_kernel, groups),
        out_shape=jax.ShapeDtypeStruct(
            (fields, groups, sliver, plane_count * per_plane * lanes // 2), landed.dtype
        ),
        grid_spec=pltpu.PrefetchScalarGridSpec(
            num_scalar_prefetch=2,
            grid=(plane_count, quads),
            in_specs=in_specs,
            out_specs=pl.BlockSpec(
                (fields, groups, sliver, lanes),
                lambda s, q, row_ref, half_ref: (0, 0, 0, s * quads + q),
            ),
        ),
    )(row, half, *([landed] * (2 * groups)))


def local(blocks, levels, block_dest, block_phi, block_group):
    tile_count = lax.axis_size("tile")
    plane_count = lax.axis_size("phi")
    slot_count = blocks.shape[0]
    fields = blocks.shape[1]
    per_plane = NPHI // BPHI // plane_count
    capacity = 2 * slot_count // tile_count
    sliver = COLS // plane_count

    onehot_dest = (block_dest[:, None] == jnp.arange(tile_count, dtype=jnp.int32)[None, :]).astype(
        jnp.int32
    )
    slot_rank = jnp.sum((jnp.cumsum(onehot_dest, axis=0) - 1) * onehot_dest, axis=1)
    send_slot = block_dest * capacity + slot_rank
    slot_ids = jnp.arange(tile_count * capacity, dtype=jnp.int32)
    match = send_slot[None, :] == slot_ids[:, None]
    filled = jnp.any(match, axis=1)
    source = jnp.argmax(match, axis=1).astype(jnp.int32)
    place = block_phi[source] * CG_DEV + block_group[source]
    code = jnp.where(filled, place, -1)
    scale = 1.0 / jnp.left_shift(1, levels[source]).astype(jnp.float32)
    device_count = tile_count * plane_count
    pairs = capacity // 2

    code_out = jnp.broadcast_to(
        code.reshape(tile_count, 1, capacity), (tile_count, plane_count, capacity)
    ).reshape(device_count, capacity)
    arrived_code = lax.all_to_all(code_out, ("tile", "phi"), split_axis=0, concat_axis=0, tiled=True)

    by_segment = jnp.transpose(
        arrived_code.reshape(tile_count, plane_count, capacity), (1, 0, 2)
    ).reshape(plane_count, tile_count * capacity)
    want = jnp.arange(slot_count, dtype=jnp.int32)
    hit = by_segment[:, None, :] == want[None, :, None]
    pick = jnp.argmax(hit, axis=2).astype(jnp.int32)
    origin = pick // capacity
    segment = jnp.arange(plane_count, dtype=jnp.int32)[:, None]
    row = ((origin * plane_count + segment) * pairs + (pick % capacity) // 2).reshape(-1)
    half = (pick % 2).reshape(-1)
    basis = dft_basis(NPHI)

    parts = []
    for field in range(fields):
        outbox = pack_outbox(blocks, source, scale, tile_count, capacity, plane_count, field)
        outbox = outbox.reshape(device_count, pairs * sliver, 2 * BPHI)
        arrived = lax.all_to_all(outbox, ("tile", "phi"), split_axis=0, concat_axis=0, tiled=True)
        landed = arrived.reshape(device_count * pairs, 1, sliver, 2 * BPHI)
        lhs = unpack_lhs(landed, row, half, plane_count, per_plane, CG_DEV)
        parts.append(
            jnp.dot(lhs.reshape(CG_DEV * sliver, NPHI), basis, preferred_element_type=jnp.float32)
        )
    spectra = jnp.stack(parts)
    return spectra.reshape(fields, CG_DEV, sliver, NPHI)


def solution(mesh):
    in_specs = (
        P(("tile", "phi"), None, None, None),
        P(("tile", "phi")),
        P(("tile", "phi")),
        P(("tile", "phi")),
        P(("tile", "phi")),
    )
    out_specs = P(None, "tile", "phi", None)
    return jax.shard_map(local, mesh=mesh, in_specs=in_specs, out_specs=out_specs, check_vma=False)
```

```python
import functools
import math

import jax
import jax.numpy as jnp
from jax import lax
from jax.experimental import pallas as pl
from jax.experimental.pallas import tpu as pltpu
from jax.sharding import PartitionSpec as P

FIELDS = 5
NPHI = 2048
BPHI = 64
COLS = 256
CG_DEV = 8


def dft_basis(length):
    half = length // 2
    column = jnp.arange(length, dtype=jnp.int32)
    mode = jnp.where(column <= half, column, column - half)
    scale = jnp.float32(2.0 * math.pi / length)
    hi = jnp.arange(length // BPHI, dtype=jnp.int32) * BPHI
    lo = jnp.arange(BPHI, dtype=jnp.int32)
    angle_hi = (hi[:, None] * mode[None, :] % length).astype(jnp.float32) * scale
    angle_lo = (lo[:, None] * mode[None, :] % length).astype(jnp.float32) * scale
    ch, sh = jnp.cos(angle_hi)[:, None, :], jnp.sin(angle_hi)[:, None, :]
    cl, sl = jnp.cos(angle_lo)[None, :, :], jnp.sin(angle_lo)[None, :, :]
    is_cos = (column <= half)[None, None, :]
    values = jnp.where(is_cos, ch * cl - sh * sl, sh * cl + ch * sl)
    values = values * jnp.float32(1.0 / math.sqrt(length))
    return values.reshape(length, length).astype(jnp.bfloat16)


def pack_kernel(source_ref, scale_ref, first_ref, second_ref, out_ref):
    tile = pl.program_id(0)
    pair = pl.program_id(1)
    slot = (tile * pl.num_programs(1) + pair) * 2
    first_scale = scale_ref[slot].astype(first_ref.dtype)
    second_scale = scale_ref[slot + 1].astype(first_ref.dtype)
    fields, planes, sliver = out_ref.shape[3], out_ref.shape[1], out_ref.shape[4]
    for field in range(fields):
        both = jnp.concatenate(
            [
                first_ref[0, field] * first_scale,
                second_ref[0, field] * second_scale,
            ],
            axis=0,
        )
        flipped = both.T.reshape(planes, sliver, both.shape[0])
        out_ref[0, :, 0, field] = flipped.astype(out_ref.dtype)


def pack_outbox(blocks, source, scale, tile_count, capacity, plane_count):
    slot_count, fields, bphi, cols = blocks.shape
    pairs = capacity // 2
    sliver = cols // plane_count

    def block_map(half):
        return lambda t, q, src_ref: (src_ref[(t * pairs + q) * 2 + half], 0, 0, 0)

    return pl.pallas_call(
        pack_kernel,
        out_shape=jax.ShapeDtypeStruct(
            (tile_count, plane_count, pairs, fields, sliver, 2 * bphi), blocks.dtype
        ),
        grid_spec=pltpu.PrefetchScalarGridSpec(
            num_scalar_prefetch=1,
            grid=(tile_count, pairs),
            in_specs=[
                pl.BlockSpec(memory_space=pltpu.SMEM),
                pl.BlockSpec((1, fields, bphi, cols), block_map(0)),
                pl.BlockSpec((1, fields, bphi, cols), block_map(1)),
            ],
            out_specs=pl.BlockSpec(
                (1, plane_count, 1, fields, sliver, 2 * bphi),
                lambda t, q, src_ref: (t, 0, q, 0, 0, 0),
            ),
        ),
    )(source, scale, blocks, blocks)


def unpack_kernel(groups, row_ref, half_ref, *refs):
    out_ref = refs[-1]
    segment = pl.program_id(0)
    quad = pl.program_id(1)
    lanes = out_ref.shape[-1]
    shape = out_ref.shape[:1] + out_ref.shape[2:]
    lane = lax.broadcasted_iota(jnp.int32, shape, 2)
    for group in range(groups):
        parts = []
        for side in range(2):
            index = ((segment * 2 * pl.num_programs(1) + quad * 2 + side) * groups) + group
            piece = refs[group * 2 + side][0]
            turned = pltpu.roll(piece, lanes // 2, 2)
            keep = half_ref[index] == side
            parts.append(jnp.where(keep, piece, turned))
        merged = jnp.where(lane < lanes // 2, parts[0], parts[1])
        out_ref[:, group] = merged.astype(out_ref.dtype)


def unpack_lhs(landed, row, half, plane_count, per_plane, groups):
    _, fields, sliver, lanes = landed.shape
    quads = per_plane // 2

    def piece_map(side, group):
        def index_map(s, q, row_ref, half_ref):
            return (row_ref[((s * per_plane + q * 2 + side) * groups) + group], 0, 0, 0)

        return index_map

    in_specs = [
        pl.BlockSpec((1, fields, sliver, lanes), piece_map(side, group))
        for group in range(groups)
        for side in range(2)
    ]
    return pl.pallas_call(
        functools.partial(unpack_kernel, groups),
        out_shape=jax.ShapeDtypeStruct(
            (fields, groups, sliver, plane_count * per_plane * lanes // 2), landed.dtype
        ),
        grid_spec=pltpu.PrefetchScalarGridSpec(
            num_scalar_prefetch=2,
            grid=(plane_count, quads),
            in_specs=in_specs,
            out_specs=pl.BlockSpec(
                (fields, groups, sliver, lanes),
                lambda s, q, row_ref, half_ref: (0, 0, 0, s * quads + q),
            ),
        ),
    )(row, half, *([landed] * (2 * groups)))


def local(blocks, levels, block_dest, block_phi, block_group):
    tile_count = lax.axis_size("tile")
    plane_count = lax.axis_size("phi")
    slot_count = blocks.shape[0]
    fields = blocks.shape[1]
    per_plane = NPHI // BPHI // plane_count
    capacity = 2 * slot_count // tile_count
    sliver = COLS // plane_count

    onehot_dest = (block_dest[:, None] == jnp.arange(tile_count, dtype=jnp.int32)[None, :]).astype(
        jnp.int32
    )
    slot_rank = jnp.sum((jnp.cumsum(onehot_dest, axis=0) - 1) * onehot_dest, axis=1)
    send_slot = block_dest * capacity + slot_rank
    slot_ids = jnp.arange(tile_count * capacity, dtype=jnp.int32)
    match = send_slot[None, :] == slot_ids[:, None]
    filled = jnp.any(match, axis=1)
    source = jnp.argmax(match, axis=1).astype(jnp.int32)
    place = block_phi[source] * CG_DEV + block_group[source]
    code = jnp.where(filled, place, -1)
    scale = 1.0 / jnp.left_shift(1, levels[source]).astype(jnp.float32)
    device_count = tile_count * plane_count
    pairs = capacity // 2

    outbox = pack_outbox(blocks, source, scale, tile_count, capacity, plane_count)
    outbox = outbox.reshape(device_count, pairs * fields * sliver, 2 * BPHI)
    code_out = jnp.broadcast_to(
        code.reshape(tile_count, 1, capacity), (tile_count, plane_count, capacity)
    ).reshape(device_count, capacity)
    arrived = lax.all_to_all(outbox, ("tile", "phi"), split_axis=0, concat_axis=0, tiled=True)
    arrived_code = lax.all_to_all(code_out, ("tile", "phi"), split_axis=0, concat_axis=0, tiled=True)

    by_segment = jnp.transpose(
        arrived_code.reshape(tile_count, plane_count, capacity), (1, 0, 2)
    ).reshape(plane_count, tile_count * capacity)
    want = jnp.arange(slot_count, dtype=jnp.int32)
    hit = by_segment[:, None, :] == want[None, :, None]
    pick = jnp.argmax(hit, axis=2).astype(jnp.int32)
    origin = pick // capacity
    segment = jnp.arange(plane_count, dtype=jnp.int32)[:, None]
    row = ((origin * plane_count + segment) * pairs + (pick % capacity) // 2).reshape(-1)
    half = (pick % 2).reshape(-1)
    landed = arrived.reshape(device_count * pairs, fields, sliver, 2 * BPHI)
    lhs = unpack_lhs(landed, row, half, plane_count, per_plane, CG_DEV)
    basis = dft_basis(NPHI)
    spectra = jnp.dot(
        lhs.reshape(fields * CG_DEV * sliver, NPHI), basis, preferred_element_type=jnp.float32
    )
    return spectra.reshape(fields, CG_DEV, sliver, NPHI)


def solution(mesh):
    in_specs = (
        P(("tile", "phi"), None, None, None),
        P(("tile", "phi")),
        P(("tile", "phi")),
        P(("tile", "phi")),
        P(("tile", "phi")),
    )
    out_specs = P(None, "tile", "phi", None)
    return jax.shard_map(local, mesh=mesh, in_specs=in_specs, out_specs=out_specs, check_vma=False)
```

```python
import functools
import math

import jax
import jax.numpy as jnp
from jax import lax
from jax.experimental import pallas as pl
from jax.experimental.pallas import tpu as pltpu
from jax.sharding import PartitionSpec as P

FIELDS = 5
NPHI = 2048
BPHI = 64
COLS = 256
CG_DEV = 8


def dft_basis(length):
    half = length // 2
    column = jnp.arange(length, dtype=jnp.int32)
    mode = jnp.where(column <= half, column, column - half)
    scale = jnp.float32(2.0 * math.pi / length)
    hi = jnp.arange(length // BPHI, dtype=jnp.int32) * BPHI
    lo = jnp.arange(BPHI, dtype=jnp.int32)
    angle_hi = (hi[:, None] * mode[None, :] % length).astype(jnp.float32) * scale
    angle_lo = (lo[:, None] * mode[None, :] % length).astype(jnp.float32) * scale
    ch, sh = jnp.cos(angle_hi)[:, None, :], jnp.sin(angle_hi)[:, None, :]
    cl, sl = jnp.cos(angle_lo)[None, :, :], jnp.sin(angle_lo)[None, :, :]
    is_cos = (column <= half)[None, None, :]
    values = jnp.where(is_cos, ch * cl - sh * sl, sh * cl + ch * sl)
    values = values * jnp.float32(1.0 / math.sqrt(length))
    return values.reshape(length, length).astype(jnp.bfloat16)


def pack_kernel(source_ref, scale_ref, *refs):
    out_ref = refs[-1]
    slots = len(refs) - 1
    tile = pl.program_id(0)
    fields, planes, sliver = out_ref.shape[3], out_ref.shape[1], out_ref.shape[4]
    for pair in range(slots // 2):
        first = tile * slots + 2 * pair
        first_scale = scale_ref[first].astype(out_ref.dtype)
        second_scale = scale_ref[first + 1].astype(out_ref.dtype)
        for field in range(fields):
            both = jnp.concatenate(
                [
                    refs[2 * pair][0, field] * first_scale,
                    refs[2 * pair + 1][0, field] * second_scale,
                ],
                axis=0,
            )
            flipped = both.T.reshape(planes, sliver, both.shape[0])
            out_ref[0, :, pair, field] = flipped.astype(out_ref.dtype)


def pack_outbox(blocks, source, scale, tile_count, capacity, plane_count):
    slot_count, fields, bphi, cols = blocks.shape
    pairs = capacity // 2
    sliver = cols // plane_count

    def block_map(slot):
        return lambda t, src_ref: (src_ref[t * capacity + slot], 0, 0, 0)

    return pl.pallas_call(
        pack_kernel,
        out_shape=jax.ShapeDtypeStruct(
            (tile_count, plane_count, pairs, fields, sliver, 2 * bphi), blocks.dtype
        ),
        grid_spec=pltpu.PrefetchScalarGridSpec(
            num_scalar_prefetch=1,
            grid=(tile_count,),
            in_specs=[pl.BlockSpec(memory_space=pltpu.SMEM)]
            + [pl.BlockSpec((1, fields, bphi, cols), block_map(slot)) for slot in range(capacity)],
            out_specs=pl.BlockSpec(
                (1, plane_count, pairs, fields, sliver, 2 * bphi),
                lambda t, src_ref: (t, 0, 0, 0, 0, 0),
            ),
        ),
    )(source, scale, *([blocks] * capacity))


def unpack_kernel(groups, per_plane, row_ref, half_ref, *refs):
    out_ref = refs[-1]
    segment = pl.program_id(0)
    lanes = refs[0].shape[-1]
    shape = refs[0].shape[1:]
    lane = lax.broadcasted_iota(jnp.int32, shape, 2)
    for group in range(groups):
        for quad in range(per_plane // 2):
            parts = []
            for side in range(2):
                position = quad * 2 + side
                index = (segment * per_plane + position) * groups + group
                piece = refs[position * groups + group][0]
                turned = pltpu.roll(piece, lanes // 2, 2)
                keep = half_ref[index] == side
                parts.append(jnp.where(keep, piece, turned))
            merged = jnp.where(lane < lanes // 2, parts[0], parts[1])
            out_ref[:, group, :, quad * lanes : (quad + 1) * lanes] = merged.astype(out_ref.dtype)


def unpack_lhs(landed, row, half, plane_count, per_plane, groups):
    _, fields, sliver, lanes = landed.shape

    def piece_map(position, group):
        def index_map(s, row_ref, half_ref):
            return (row_ref[(s * per_plane + position) * groups + group], 0, 0, 0)

        return index_map

    in_specs = [
        pl.BlockSpec((1, fields, sliver, lanes), piece_map(position, group))
        for position in range(per_plane)
        for group in range(groups)
    ]
    width = per_plane * lanes // 2
    return pl.pallas_call(
        functools.partial(unpack_kernel, groups, per_plane),
        out_shape=jax.ShapeDtypeStruct((fields, groups, sliver, plane_count * width), landed.dtype),
        grid_spec=pltpu.PrefetchScalarGridSpec(
            num_scalar_prefetch=2,
            grid=(plane_count,),
            in_specs=in_specs,
            out_specs=pl.BlockSpec(
                (fields, groups, sliver, width), lambda s, row_ref, half_ref: (0, 0, 0, s)
            ),
        ),
    )(row, half, *([landed] * (per_plane * groups)))


def local(blocks, levels, block_dest, block_phi, block_group):
    tile_count = lax.axis_size("tile")
    plane_count = lax.axis_size("phi")
    slot_count = blocks.shape[0]
    fields = blocks.shape[1]
    per_plane = NPHI // BPHI // plane_count
    capacity = 2 * slot_count // tile_count
    sliver = COLS // plane_count

    onehot_dest = (block_dest[:, None] == jnp.arange(tile_count, dtype=jnp.int32)[None, :]).astype(
        jnp.int32
    )
    slot_rank = jnp.sum((jnp.cumsum(onehot_dest, axis=0) - 1) * onehot_dest, axis=1)
    send_slot = block_dest * capacity + slot_rank
    slot_ids = jnp.arange(tile_count * capacity, dtype=jnp.int32)
    match = send_slot[None, :] == slot_ids[:, None]
    filled = jnp.any(match, axis=1)
    source = jnp.argmax(match, axis=1).astype(jnp.int32)
    place = block_phi[source] * CG_DEV + block_group[source]
    code = jnp.where(filled, place, -1)
    scale = 1.0 / jnp.left_shift(1, levels[source]).astype(jnp.float32)
    device_count = tile_count * plane_count
    pairs = capacity // 2

    outbox = pack_outbox(blocks, source, scale, tile_count, capacity, plane_count)
    outbox = outbox.reshape(device_count, pairs * fields * sliver, 2 * BPHI)
    code_out = jnp.broadcast_to(
        code.reshape(tile_count, 1, capacity), (tile_count, plane_count, capacity)
    ).reshape(device_count, capacity)
    arrived = lax.all_to_all(outbox, ("tile", "phi"), split_axis=0, concat_axis=0, tiled=True)
    arrived_code = lax.all_to_all(code_out, ("tile", "phi"), split_axis=0, concat_axis=0, tiled=True)

    by_segment = jnp.transpose(
        arrived_code.reshape(tile_count, plane_count, capacity), (1, 0, 2)
    ).reshape(plane_count, tile_count * capacity)
    want = jnp.arange(slot_count, dtype=jnp.int32)
    hit = by_segment[:, None, :] == want[None, :, None]
    pick = jnp.argmax(hit, axis=2).astype(jnp.int32)
    origin = pick // capacity
    segment = jnp.arange(plane_count, dtype=jnp.int32)[:, None]
    row = ((origin * plane_count + segment) * pairs + (pick % capacity) // 2).reshape(-1)
    half = (pick % 2).reshape(-1)
    landed = arrived.reshape(device_count * pairs, fields, sliver, 2 * BPHI)
    lhs = unpack_lhs(landed, row, half, plane_count, per_plane, CG_DEV)
    basis = dft_basis(NPHI)
    spectra = jnp.dot(
        lhs.reshape(fields * CG_DEV * sliver, NPHI), basis, preferred_element_type=jnp.float32
    )
    return spectra.reshape(fields, CG_DEV, sliver, NPHI)


def solution(mesh):
    in_specs = (
        P(("tile", "phi"), None, None, None),
        P(("tile", "phi")),
        P(("tile", "phi")),
        P(("tile", "phi")),
        P(("tile", "phi")),
    )
    out_specs = P(None, "tile", "phi", None)
    return jax.shard_map(local, mesh=mesh, in_specs=in_specs, out_specs=out_specs, check_vma=False)
```

```python
import functools
import math

import jax
import jax.numpy as jnp
from jax import lax
from jax.experimental import pallas as pl
from jax.experimental.pallas import tpu as pltpu
from jax.sharding import PartitionSpec as P

FIELDS = 5
NPHI = 2048
BPHI = 64
COLS = 256
CG_DEV = 8


def dft_basis(length):
    half = length // 2
    column = jnp.arange(length, dtype=jnp.int32)
    mode = jnp.where(column <= half, column, column - half)
    scale = jnp.float32(2.0 * math.pi / length)
    hi = jnp.arange(length // BPHI, dtype=jnp.int32) * BPHI
    lo = jnp.arange(BPHI, dtype=jnp.int32)
    angle_hi = (hi[:, None] * mode[None, :] % length).astype(jnp.float32) * scale
    angle_lo = (lo[:, None] * mode[None, :] % length).astype(jnp.float32) * scale
    ch, sh = jnp.cos(angle_hi)[:, None, :], jnp.sin(angle_hi)[:, None, :]
    cl, sl = jnp.cos(angle_lo)[None, :, :], jnp.sin(angle_lo)[None, :, :]
    is_cos = (column <= half)[None, None, :]
    values = jnp.where(is_cos, ch * cl - sh * sl, sh * cl + ch * sl)
    values = values * jnp.float32(1.0 / math.sqrt(length))
    return values.reshape(length, length).astype(jnp.bfloat16)


def pack_kernel(source_ref, scale_ref, *refs):
    out_ref = refs[-1]
    per_step, planes, pairs, fields, sliver = out_ref.shape[:5]
    step = pl.program_id(0)
    for local_tile in range(per_step):
        for pair in range(pairs):
            slot = (local_tile * pairs + pair) * 2
            first = step * (len(refs) - 1) + slot
            first_scale = scale_ref[first].astype(out_ref.dtype)
            second_scale = scale_ref[first + 1].astype(out_ref.dtype)
            for field in range(fields):
                both = jnp.concatenate(
                    [
                        refs[slot][0, field] * first_scale,
                        refs[slot + 1][0, field] * second_scale,
                    ],
                    axis=0,
                )
                flipped = both.T.reshape(planes, sliver, both.shape[0])
                out_ref[local_tile, :, pair, field] = flipped.astype(out_ref.dtype)


def pack_outbox(blocks, source, scale, tile_count, capacity, plane_count):
    slot_count, fields, bphi, cols = blocks.shape
    pairs = capacity // 2
    sliver = cols // plane_count

    per_step = 2
    per_call = per_step * capacity

    def block_map(slot):
        return lambda t, src_ref: (src_ref[t * per_call + slot], 0, 0, 0)

    return pl.pallas_call(
        pack_kernel,
        out_shape=jax.ShapeDtypeStruct(
            (tile_count, plane_count, pairs, fields, sliver, 2 * bphi), blocks.dtype
        ),
        grid_spec=pltpu.PrefetchScalarGridSpec(
            num_scalar_prefetch=1,
            grid=(tile_count // per_step,),
            in_specs=[pl.BlockSpec(memory_space=pltpu.SMEM)]
            + [pl.BlockSpec((1, fields, bphi, cols), block_map(slot)) for slot in range(per_call)],
            out_specs=pl.BlockSpec(
                (per_step, plane_count, pairs, fields, sliver, 2 * bphi),
                lambda t, src_ref: (t, 0, 0, 0, 0, 0),
            ),
        ),
    )(source, scale, *([blocks] * per_call))


def unpack_kernel(groups, per_plane, per_step, row_ref, half_ref, *refs):
    out_ref = refs[-1]
    step = pl.program_id(0)
    lanes = refs[0].shape[-1]
    shape = refs[0].shape[1:]
    lane = lax.broadcasted_iota(jnp.int32, shape, 2)
    quads = per_plane // 2
    for local_segment in range(per_step):
        for group in range(groups):
            for quad in range(quads):
                parts = []
                for side in range(2):
                    position = local_segment * per_plane + quad * 2 + side
                    index = (step * per_step * per_plane + position) * groups + group
                    piece = refs[position * groups + group][0]
                    turned = pltpu.roll(piece, lanes // 2, 2)
                    keep = half_ref[index] == side
                    parts.append(jnp.where(keep, piece, turned))
                merged = jnp.where(lane < lanes // 2, parts[0], parts[1])
                start = (local_segment * quads + quad) * lanes
                out_ref[:, group, :, start : start + lanes] = merged.astype(out_ref.dtype)


def unpack_lhs(landed, row, half, plane_count, per_plane, groups):
    _, fields, sliver, lanes = landed.shape

    per_step = 2
    per_call = per_step * per_plane

    def piece_map(position, group):
        def index_map(s, row_ref, half_ref):
            return (row_ref[(s * per_call + position) * groups + group], 0, 0, 0)

        return index_map

    in_specs = [
        pl.BlockSpec((1, fields, sliver, lanes), piece_map(position, group))
        for position in range(per_call)
        for group in range(groups)
    ]
    width = per_call * lanes // 2
    return pl.pallas_call(
        functools.partial(unpack_kernel, groups, per_plane, per_step),
        out_shape=jax.ShapeDtypeStruct(
            (fields, groups, sliver, plane_count * per_plane * lanes // 2), landed.dtype
        ),
        grid_spec=pltpu.PrefetchScalarGridSpec(
            num_scalar_prefetch=2,
            grid=(plane_count // per_step,),
            in_specs=in_specs,
            out_specs=pl.BlockSpec(
                (fields, groups, sliver, width), lambda s, row_ref, half_ref: (0, 0, 0, s)
            ),
        ),
    )(row, half, *([landed] * (per_call * groups)))


def local(blocks, levels, block_dest, block_phi, block_group):
    tile_count = lax.axis_size("tile")
    plane_count = lax.axis_size("phi")
    slot_count = blocks.shape[0]
    fields = blocks.shape[1]
    per_plane = NPHI // BPHI // plane_count
    capacity = 2 * slot_count // tile_count
    sliver = COLS // plane_count

    onehot_dest = (block_dest[:, None] == jnp.arange(tile_count, dtype=jnp.int32)[None, :]).astype(
        jnp.int32
    )
    slot_rank = jnp.sum((jnp.cumsum(onehot_dest, axis=0) - 1) * onehot_dest, axis=1)
    send_slot = block_dest * capacity + slot_rank
    slot_ids = jnp.arange(tile_count * capacity, dtype=jnp.int32)
    match = send_slot[None, :] == slot_ids[:, None]
    filled = jnp.any(match, axis=1)
    source = jnp.argmax(match, axis=1).astype(jnp.int32)
    place = block_phi[source] * CG_DEV + block_group[source]
    code = jnp.where(filled, place, -1)
    scale = 1.0 / jnp.left_shift(1, levels[source]).astype(jnp.float32)
    device_count = tile_count * plane_count
    pairs = capacity // 2

    outbox = pack_outbox(blocks, source, scale, tile_count, capacity, plane_count)
    outbox = outbox.reshape(device_count, pairs * fields * sliver, 2 * BPHI)
    code_out = jnp.broadcast_to(
        code.reshape(tile_count, 1, capacity), (tile_count, plane_count, capacity)
    ).reshape(device_count, capacity)
    arrived = lax.all_to_all(outbox, ("tile", "phi"), split_axis=0, concat_axis=0, tiled=True)
    arrived_code = lax.all_to_all(code_out, ("tile", "phi"), split_axis=0, concat_axis=0, tiled=True)

    by_segment = jnp.transpose(
        arrived_code.reshape(tile_count, plane_count, capacity), (1, 0, 2)
    ).reshape(plane_count, tile_count * capacity)
    want = jnp.arange(slot_count, dtype=jnp.int32)
    hit = by_segment[:, None, :] == want[None, :, None]
    pick = jnp.argmax(hit, axis=2).astype(jnp.int32)
    origin = pick // capacity
    segment = jnp.arange(plane_count, dtype=jnp.int32)[:, None]
    row = ((origin * plane_count + segment) * pairs + (pick % capacity) // 2).reshape(-1)
    half = (pick % 2).reshape(-1)
    landed = arrived.reshape(device_count * pairs, fields, sliver, 2 * BPHI)
    lhs = unpack_lhs(landed, row, half, plane_count, per_plane, CG_DEV)
    basis = dft_basis(NPHI)
    spectra = jnp.dot(
        lhs.reshape(fields * CG_DEV * sliver, NPHI), basis, preferred_element_type=jnp.float32
    )
    return spectra.reshape(fields, CG_DEV, sliver, NPHI)


def solution(mesh):
    in_specs = (
        P(("tile", "phi"), None, None, None),
        P(("tile", "phi")),
        P(("tile", "phi")),
        P(("tile", "phi")),
        P(("tile", "phi")),
    )
    out_specs = P(None, "tile", "phi", None)
    return jax.shard_map(local, mesh=mesh, in_specs=in_specs, out_specs=out_specs, check_vma=False)
```

```python
import functools
import math

import jax
import jax.numpy as jnp
from jax import lax
from jax.experimental import pallas as pl
from jax.experimental.pallas import tpu as pltpu
from jax.sharding import PartitionSpec as P

FIELDS = 5
NPHI = 2048
BPHI = 64
COLS = 256
CG_DEV = 8


def dft_basis(length):
    half = length // 2
    column = jnp.arange(length, dtype=jnp.int32)
    mode = jnp.where(column <= half, column, column - half)
    scale = jnp.float32(2.0 * math.pi / length)
    hi = jnp.arange(length // BPHI, dtype=jnp.int32) * BPHI
    lo = jnp.arange(BPHI, dtype=jnp.int32)
    angle_hi = (hi[:, None] * mode[None, :] % length).astype(jnp.float32) * scale
    angle_lo = (lo[:, None] * mode[None, :] % length).astype(jnp.float32) * scale
    ch, sh = jnp.cos(angle_hi)[:, None, :], jnp.sin(angle_hi)[:, None, :]
    cl, sl = jnp.cos(angle_lo)[None, :, :], jnp.sin(angle_lo)[None, :, :]
    is_cos = (column <= half)[None, None, :]
    values = jnp.where(is_cos, ch * cl - sh * sl, sh * cl + ch * sl)
    values = values * jnp.float32(1.0 / math.sqrt(length))
    return values.reshape(length, length).astype(jnp.bfloat16)


def pack_kernel(source_ref, scale_ref, *refs):
    out_ref = refs[-1]
    per_step, planes, pairs, fields, sliver = out_ref.shape[:5]
    step = pl.program_id(0)
    for local_tile in range(per_step):
        for pair in range(pairs):
            slot = (local_tile * pairs + pair) * 2
            first = step * (len(refs) - 1) + slot
            first_scale = scale_ref[first].astype(out_ref.dtype)
            second_scale = scale_ref[first + 1].astype(out_ref.dtype)
            for field in range(fields):
                both = jnp.concatenate(
                    [
                        refs[slot][0, field] * first_scale,
                        refs[slot + 1][0, field] * second_scale,
                    ],
                    axis=0,
                )
                flipped = both.T.reshape(planes, sliver, both.shape[0])
                out_ref[local_tile, :, pair, field] = flipped.astype(out_ref.dtype)


def pack_outbox(blocks, source, scale, tile_count, capacity, plane_count):
    slot_count, fields, bphi, cols = blocks.shape
    pairs = capacity // 2
    sliver = cols // plane_count

    per_step = 2
    per_call = per_step * capacity

    def block_map(slot):
        return lambda t, src_ref: (src_ref[t * per_call + slot], 0, 0, 0)

    return pl.pallas_call(
        pack_kernel,
        out_shape=jax.ShapeDtypeStruct(
            (tile_count, plane_count, pairs, fields, sliver, 2 * bphi), blocks.dtype
        ),
        grid_spec=pltpu.PrefetchScalarGridSpec(
            num_scalar_prefetch=1,
            grid=(tile_count // per_step,),
            in_specs=[pl.BlockSpec(memory_space=pltpu.SMEM)]
            + [pl.BlockSpec((1, fields, bphi, cols), block_map(slot)) for slot in range(per_call)],
            out_specs=pl.BlockSpec(
                (per_step, plane_count, pairs, fields, sliver, 2 * bphi),
                lambda t, src_ref: (t, 0, 0, 0, 0, 0),
            ),
        ),
    )(source, scale, *([blocks] * per_call))


def spectra_kernel(groups, per_plane, row_ref, half_ref, *refs):
    pieces = refs[: per_plane * groups]
    basis_ref, out_ref, lhs_ref = refs[per_plane * groups :]
    segment = pl.program_id(0)
    lanes = pieces[0].shape[-1]
    shape = pieces[0].shape[1:]
    lane = lax.broadcasted_iota(jnp.int32, shape, 2)
    for group in range(groups):
        for quad in range(per_plane // 2):
            parts = []
            for side in range(2):
                position = quad * 2 + side
                index = (segment * per_plane + position) * groups + group
                piece = pieces[position * groups + group][0]
                turned = pltpu.roll(piece, lanes // 2, 2)
                keep = half_ref[index] == side
                parts.append(jnp.where(keep, piece, turned))
            merged = jnp.where(lane < lanes // 2, parts[0], parts[1])
            lhs_ref[:, group, :, quad * lanes : (quad + 1) * lanes] = merged

    @pl.when(segment == 0)
    def _():
        out_ref[...] = jnp.zeros_like(out_ref)

    rows = out_ref.shape[0]
    lhs = lhs_ref[...].reshape(rows, lhs_ref.shape[-1])
    width = 512
    for chunk in range(out_ref.shape[1] // width):
        columns = slice(chunk * width, (chunk + 1) * width)
        out_ref[:, columns] += jnp.dot(
            lhs, basis_ref[:, columns], preferred_element_type=jnp.float32
        )


def spectra_from(landed, row, half, basis, plane_count, per_plane, groups):
    _, fields, sliver, lanes = landed.shape
    depth = per_plane * lanes // 2
    length = basis.shape[1]

    def piece_map(position, group):
        def index_map(s, row_ref, half_ref):
            return (row_ref[(s * per_plane + position) * groups + group], 0, 0, 0)

        return index_map

    in_specs = [
        pl.BlockSpec((1, fields, sliver, lanes), piece_map(position, group))
        for position in range(per_plane)
        for group in range(groups)
    ]
    in_specs.append(pl.BlockSpec((depth, length), lambda s, row_ref, half_ref: (s, 0)))
    rows = fields * groups * sliver
    return pl.pallas_call(
        functools.partial(spectra_kernel, groups, per_plane),
        out_shape=jax.ShapeDtypeStruct((rows, length), jnp.float32),
        grid_spec=pltpu.PrefetchScalarGridSpec(
            num_scalar_prefetch=2,
            grid=(plane_count,),
            in_specs=in_specs,
            out_specs=pl.BlockSpec((rows, length), lambda s, row_ref, half_ref: (0, 0)),
            scratch_shapes=[pltpu.VMEM((fields, groups, sliver, depth), landed.dtype)],
        ),
        compiler_params=pltpu.CompilerParams(
            dimension_semantics=("arbitrary",), vmem_limit_bytes=60 * 1024 * 1024
        ),
    )(row, half, *([landed] * (per_plane * groups)), basis)


def local(blocks, levels, block_dest, block_phi, block_group):
    tile_count = lax.axis_size("tile")
    plane_count = lax.axis_size("phi")
    slot_count = blocks.shape[0]
    fields = blocks.shape[1]
    per_plane = NPHI // BPHI // plane_count
    capacity = 2 * slot_count // tile_count
    sliver = COLS // plane_count

    onehot_dest = (block_dest[:, None] == jnp.arange(tile_count, dtype=jnp.int32)[None, :]).astype(
        jnp.int32
    )
    slot_rank = jnp.sum((jnp.cumsum(onehot_dest, axis=0) - 1) * onehot_dest, axis=1)
    send_slot = block_dest * capacity + slot_rank
    slot_ids = jnp.arange(tile_count * capacity, dtype=jnp.int32)
    match = send_slot[None, :] == slot_ids[:, None]
    filled = jnp.any(match, axis=1)
    source = jnp.argmax(match, axis=1).astype(jnp.int32)
    place = block_phi[source] * CG_DEV + block_group[source]
    code = jnp.where(filled, place, -1)
    scale = 1.0 / jnp.left_shift(1, levels[source]).astype(jnp.float32)
    device_count = tile_count * plane_count
    pairs = capacity // 2

    outbox = pack_outbox(blocks, source, scale, tile_count, capacity, plane_count)
    outbox = outbox.reshape(device_count, pairs * fields * sliver, 2 * BPHI)
    code_out = jnp.broadcast_to(
        code.reshape(tile_count, 1, capacity), (tile_count, plane_count, capacity)
    ).reshape(device_count, capacity)
    arrived = lax.all_to_all(outbox, ("tile", "phi"), split_axis=0, concat_axis=0, tiled=True)
    arrived_code = lax.all_to_all(code_out, ("tile", "phi"), split_axis=0, concat_axis=0, tiled=True)

    by_segment = jnp.transpose(
        arrived_code.reshape(tile_count, plane_count, capacity), (1, 0, 2)
    ).reshape(plane_count, tile_count * capacity)
    want = jnp.arange(slot_count, dtype=jnp.int32)
    hit = by_segment[:, None, :] == want[None, :, None]
    pick = jnp.argmax(hit, axis=2).astype(jnp.int32)
    origin = pick // capacity
    segment = jnp.arange(plane_count, dtype=jnp.int32)[:, None]
    row = ((origin * plane_count + segment) * pairs + (pick % capacity) // 2).reshape(-1)
    half = (pick % 2).reshape(-1)
    landed = arrived.reshape(device_count * pairs, fields, sliver, 2 * BPHI)
    basis = dft_basis(NPHI)
    spectra = spectra_from(landed, row, half, basis, plane_count, per_plane, CG_DEV)
    return spectra.reshape(fields, CG_DEV, sliver, NPHI)


def solution(mesh):
    in_specs = (
        P(("tile", "phi"), None, None, None),
        P(("tile", "phi")),
        P(("tile", "phi")),
        P(("tile", "phi")),
        P(("tile", "phi")),
    )
    out_specs = P(None, "tile", "phi", None)
    return jax.shard_map(local, mesh=mesh, in_specs=in_specs, out_specs=out_specs, check_vma=False)
```

```python
import functools
import math

import jax
import jax.numpy as jnp
from jax import lax
from jax.experimental import pallas as pl
from jax.experimental.pallas import tpu as pltpu
from jax.sharding import PartitionSpec as P

FIELDS = 5
NPHI = 2048
BPHI = 64
COLS = 256
CG_DEV = 8


def dft_basis(length):
    half = length // 2
    column = jnp.arange(length, dtype=jnp.int32)
    mode = jnp.where(column <= half, column, column - half)
    scale = jnp.float32(2.0 * math.pi / length)
    hi = jnp.arange(length // BPHI, dtype=jnp.int32) * BPHI
    lo = jnp.arange(BPHI, dtype=jnp.int32)
    angle_hi = (hi[:, None] * mode[None, :] % length).astype(jnp.float32) * scale
    angle_lo = (lo[:, None] * mode[None, :] % length).astype(jnp.float32) * scale
    ch, sh = jnp.cos(angle_hi)[:, None, :], jnp.sin(angle_hi)[:, None, :]
    cl, sl = jnp.cos(angle_lo)[None, :, :], jnp.sin(angle_lo)[None, :, :]
    is_cos = (column <= half)[None, None, :]
    values = jnp.where(is_cos, ch * cl - sh * sl, sh * cl + ch * sl)
    values = values * jnp.float32(1.0 / math.sqrt(length))
    return values.reshape(length, length).astype(jnp.bfloat16)


def pack_kernel(source_ref, scale_ref, *refs):
    out_ref = refs[-1]
    per_step, planes, pairs, fields, sliver = out_ref.shape[:5]
    step = pl.program_id(0)
    for local_tile in range(per_step):
        for pair in range(pairs):
            slot = (local_tile * pairs + pair) * 2
            first = step * (len(refs) - 1) + slot
            first_scale = scale_ref[first].astype(out_ref.dtype)
            second_scale = scale_ref[first + 1].astype(out_ref.dtype)
            for field in range(fields):
                both = jnp.concatenate(
                    [
                        refs[slot][0, field] * first_scale,
                        refs[slot + 1][0, field] * second_scale,
                    ],
                    axis=0,
                )
                flipped = both.T.reshape(planes, sliver, both.shape[0])
                out_ref[local_tile, :, pair, field] = flipped.astype(out_ref.dtype)


def pack_outbox(blocks, source, scale, tile_count, capacity, plane_count, first, fields):
    slot_count, _, bphi, cols = blocks.shape
    pairs = capacity // 2
    sliver = cols // plane_count

    per_step = 2
    per_call = per_step * capacity

    def block_map(slot):
        return lambda t, src_ref: (src_ref[t * per_call + slot], first // fields, 0, 0)

    return pl.pallas_call(
        pack_kernel,
        out_shape=jax.ShapeDtypeStruct(
            (tile_count, plane_count, pairs, fields, sliver, 2 * bphi), blocks.dtype
        ),
        grid_spec=pltpu.PrefetchScalarGridSpec(
            num_scalar_prefetch=1,
            grid=(tile_count // per_step,),
            in_specs=[pl.BlockSpec(memory_space=pltpu.SMEM)]
            + [pl.BlockSpec((1, fields, bphi, cols), block_map(slot)) for slot in range(per_call)],
            out_specs=pl.BlockSpec(
                (per_step, plane_count, pairs, fields, sliver, 2 * bphi),
                lambda t, src_ref: (t, 0, 0, 0, 0, 0),
            ),
        ),
    )(source, scale, *([blocks] * per_call))


def spectra_kernel(groups, per_plane, row_ref, half_ref, *refs):
    pieces = refs[: per_plane * groups]
    basis_ref, out_ref, lhs_ref = refs[per_plane * groups :][0], refs[-2], refs[-1]
    segment = pl.program_id(0)
    lanes = pieces[0].shape[-1]
    shape = pieces[0].shape[1:]
    lane = lax.broadcasted_iota(jnp.int32, shape, 2)
    for group in range(groups):
        for quad in range(per_plane // 2):
            parts = []
            for side in range(2):
                position = quad * 2 + side
                index = (segment * per_plane + position) * groups + group
                piece = pieces[position * groups + group][0]
                turned = pltpu.roll(piece, lanes // 2, 2)
                keep = half_ref[index] == side
                parts.append(jnp.where(keep, piece, turned))
            merged = jnp.where(lane < lanes // 2, parts[0], parts[1])
            lhs_ref[:, group, :, quad * lanes : (quad + 1) * lanes] = merged

    @pl.when(segment == 0)
    def _():
        out_ref[...] = jnp.zeros_like(out_ref)

    rows = out_ref.shape[0]
    lhs = lhs_ref[...].reshape(rows, lhs_ref.shape[-1])
    width = 512
    for chunk in range(out_ref.shape[1] // width):
        columns = slice(chunk * width, (chunk + 1) * width)
        out_ref[:, columns] += jnp.dot(
            lhs, basis_ref[:, columns], preferred_element_type=jnp.float32
        )


def spectra_from(landed, row, half, basis, plane_count, per_plane, groups, rows, first, previous):
    _, fields, sliver, lanes = landed.shape
    depth = per_plane * lanes // 2
    length = basis.shape[1]

    def piece_map(position, group):
        def index_map(s, row_ref, half_ref):
            return (row_ref[(s * per_plane + position) * groups + group], 0, 0, 0)

        return index_map

    in_specs = [
        pl.BlockSpec((1, fields, sliver, lanes), piece_map(position, group))
        for position in range(per_plane)
        for group in range(groups)
    ]
    in_specs.append(pl.BlockSpec((depth, length), lambda s, row_ref, half_ref: (s, 0)))
    block_rows = fields * groups * sliver
    operands = [row, half] + [landed] * (per_plane * groups) + [basis]
    aliases = {}
    if previous is not None:
        in_specs.append(pl.BlockSpec(memory_space=pl.ANY))
        aliases = {len(operands): 0}
        operands.append(previous)
    return pl.pallas_call(
        functools.partial(spectra_kernel, groups, per_plane),
        out_shape=jax.ShapeDtypeStruct((rows, length), jnp.float32),
        input_output_aliases=aliases,
        grid_spec=pltpu.PrefetchScalarGridSpec(
            num_scalar_prefetch=2,
            grid=(plane_count,),
            in_specs=in_specs,
            out_specs=pl.BlockSpec(
                (block_rows, length), lambda s, row_ref, half_ref: (first // fields, 0)
            ),
            scratch_shapes=[pltpu.VMEM((fields, groups, sliver, depth), landed.dtype)],
        ),
        compiler_params=pltpu.CompilerParams(
            dimension_semantics=("arbitrary",), vmem_limit_bytes=60 * 1024 * 1024
        ),
    )(*operands)


def local(blocks, levels, block_dest, block_phi, block_group):
    tile_count = lax.axis_size("tile")
    plane_count = lax.axis_size("phi")
    slot_count = blocks.shape[0]
    fields = blocks.shape[1]
    per_plane = NPHI // BPHI // plane_count
    capacity = 2 * slot_count // tile_count
    sliver = COLS // plane_count

    onehot_dest = (block_dest[:, None] == jnp.arange(tile_count, dtype=jnp.int32)[None, :]).astype(
        jnp.int32
    )
    slot_rank = jnp.sum((jnp.cumsum(onehot_dest, axis=0) - 1) * onehot_dest, axis=1)
    send_slot = block_dest * capacity + slot_rank
    slot_ids = jnp.arange(tile_count * capacity, dtype=jnp.int32)
    match = send_slot[None, :] == slot_ids[:, None]
    filled = jnp.any(match, axis=1)
    source = jnp.argmax(match, axis=1).astype(jnp.int32)
    place = block_phi[source] * CG_DEV + block_group[source]
    code = jnp.where(filled, place, -1)
    scale = 1.0 / jnp.left_shift(1, levels[source]).astype(jnp.float32)
    device_count = tile_count * plane_count
    pairs = capacity // 2

    code_out = jnp.broadcast_to(
        code.reshape(tile_count, 1, capacity), (tile_count, plane_count, capacity)
    ).reshape(device_count, capacity)
    arrived_code = lax.all_to_all(code_out, ("tile", "phi"), split_axis=0, concat_axis=0, tiled=True)

    by_segment = jnp.transpose(
        arrived_code.reshape(tile_count, plane_count, capacity), (1, 0, 2)
    ).reshape(plane_count, tile_count * capacity)
    want = jnp.arange(slot_count, dtype=jnp.int32)
    hit = by_segment[:, None, :] == want[None, :, None]
    pick = jnp.argmax(hit, axis=2).astype(jnp.int32)
    origin = pick // capacity
    segment = jnp.arange(plane_count, dtype=jnp.int32)[:, None]
    row = ((origin * plane_count + segment) * pairs + (pick % capacity) // 2).reshape(-1)
    half = (pick % 2).reshape(-1)
    basis = dft_basis(NPHI)

    rows = fields * CG_DEV * sliver
    spectra = None
    for first, count in ((0, fields - 1), (fields - 1, 1)):
        outbox = pack_outbox(blocks, source, scale, tile_count, capacity, plane_count, first, count)
        outbox = outbox.reshape(device_count, pairs * count * sliver, 2 * BPHI)
        arrived = lax.all_to_all(outbox, ("tile", "phi"), split_axis=0, concat_axis=0, tiled=True)
        landed = arrived.reshape(device_count * pairs, count, sliver, 2 * BPHI)
        spectra = spectra_from(
            landed, row, half, basis, plane_count, per_plane, CG_DEV, rows, first, spectra
        )
    return spectra.reshape(fields, CG_DEV, sliver, NPHI)


def solution(mesh):
    in_specs = (
        P(("tile", "phi"), None, None, None),
        P(("tile", "phi")),
        P(("tile", "phi")),
        P(("tile", "phi")),
        P(("tile", "phi")),
    )
    out_specs = P(None, "tile", "phi", None)
    return jax.shard_map(local, mesh=mesh, in_specs=in_specs, out_specs=out_specs, check_vma=False)
```

```python
import functools
import math

import jax
import jax.numpy as jnp
from jax import lax
from jax.experimental import pallas as pl
from jax.experimental.pallas import tpu as pltpu
from jax.sharding import PartitionSpec as P

FIELDS = 5
NPHI = 2048
BPHI = 64
COLS = 256
CG_DEV = 8


def dft_basis(length):
    half = length // 2
    column = jnp.arange(length, dtype=jnp.int32)
    mode = jnp.where(column <= half, column, column - half)
    scale = jnp.float32(2.0 * math.pi / length)
    hi = jnp.arange(length // BPHI, dtype=jnp.int32) * BPHI
    lo = jnp.arange(BPHI, dtype=jnp.int32)
    angle_hi = (hi[:, None] * mode[None, :] % length).astype(jnp.float32) * scale
    angle_lo = (lo[:, None] * mode[None, :] % length).astype(jnp.float32) * scale
    ch, sh = jnp.cos(angle_hi)[:, None, :], jnp.sin(angle_hi)[:, None, :]
    cl, sl = jnp.cos(angle_lo)[None, :, :], jnp.sin(angle_lo)[None, :, :]
    is_cos = (column <= half)[None, None, :]
    values = jnp.where(is_cos, ch * cl - sh * sl, sh * cl + ch * sl)
    values = values * jnp.float32(1.0 / math.sqrt(length))
    return values.reshape(length, length).astype(jnp.bfloat16)


def pack_kernel(source_ref, scale_ref, *refs):
    out_ref = refs[-1]
    per_step, planes, pairs, fields, sliver = out_ref.shape[:5]
    step = pl.program_id(0)
    for local_tile in range(per_step):
        for pair in range(pairs):
            slot = (local_tile * pairs + pair) * 2
            first = step * (len(refs) - 1) + slot
            first_scale = scale_ref[first].astype(out_ref.dtype)
            second_scale = scale_ref[first + 1].astype(out_ref.dtype)
            for field in range(fields):
                both = jnp.concatenate(
                    [
                        refs[slot][0, field] * first_scale,
                        refs[slot + 1][0, field] * second_scale,
                    ],
                    axis=0,
                )
                flipped = both.T.reshape(planes, sliver, both.shape[0])
                out_ref[local_tile, :, pair, field] = flipped.astype(out_ref.dtype)


def pack_outbox(blocks, source, scale, tile_count, capacity, plane_count, first, fields):
    slot_count, _, bphi, cols = blocks.shape
    pairs = capacity // 2
    sliver = cols // plane_count

    per_step = 2
    per_call = per_step * capacity

    def block_map(slot):
        return lambda t, src_ref: (src_ref[t * per_call + slot], first // fields, 0, 0)

    return pl.pallas_call(
        pack_kernel,
        out_shape=jax.ShapeDtypeStruct(
            (tile_count, plane_count, pairs, fields, sliver, 2 * bphi), blocks.dtype
        ),
        grid_spec=pltpu.PrefetchScalarGridSpec(
            num_scalar_prefetch=1,
            grid=(tile_count // per_step,),
            in_specs=[pl.BlockSpec(memory_space=pltpu.SMEM)]
            + [pl.BlockSpec((1, fields, bphi, cols), block_map(slot)) for slot in range(per_call)],
            out_specs=pl.BlockSpec(
                (per_step, plane_count, pairs, fields, sliver, 2 * bphi),
                lambda t, src_ref: (t, 0, 0, 0, 0, 0),
            ),
        ),
    )(source, scale, *([blocks] * per_call))


def spectra_kernel(groups, per_plane, row_ref, half_ref, *refs):
    pieces = refs[: per_plane * groups]
    basis_ref, out_ref, lhs_ref = refs[per_plane * groups :][0], refs[-2], refs[-1]
    segment = pl.program_id(0)
    lanes = pieces[0].shape[-1]
    shape = pieces[0].shape[1:]
    lane = lax.broadcasted_iota(jnp.int32, shape, 2)
    for group in range(groups):
        for quad in range(per_plane // 2):
            parts = []
            for side in range(2):
                position = quad * 2 + side
                index = (segment * per_plane + position) * groups + group
                piece = pieces[position * groups + group][0]
                turned = pltpu.roll(piece, lanes // 2, 2)
                keep = half_ref[index] == side
                parts.append(jnp.where(keep, piece, turned))
            merged = jnp.where(lane < lanes // 2, parts[0], parts[1])
            lhs_ref[:, group, :, quad * lanes : (quad + 1) * lanes] = merged

    @pl.when(segment == 0)
    def _():
        out_ref[...] = jnp.zeros_like(out_ref)

    rows = out_ref.shape[0]
    lhs = lhs_ref[...].reshape(rows, lhs_ref.shape[-1])
    width = 512
    for chunk in range(out_ref.shape[1] // width):
        columns = slice(chunk * width, (chunk + 1) * width)
        out_ref[:, columns] += jnp.dot(
            lhs, basis_ref[:, columns], preferred_element_type=jnp.float32
        )


def spectra_from(landed, row, half, basis, plane_count, per_plane, groups, rows, first, previous):
    _, fields, sliver, lanes = landed.shape
    depth = per_plane * lanes // 2
    length = basis.shape[1]

    def piece_map(position, group):
        def index_map(s, row_ref, half_ref):
            return (row_ref[(s * per_plane + position) * groups + group], 0, 0, 0)

        return index_map

    in_specs = [
        pl.BlockSpec((1, fields, sliver, lanes), piece_map(position, group))
        for position in range(per_plane)
        for group in range(groups)
    ]
    in_specs.append(pl.BlockSpec((depth, length), lambda s, row_ref, half_ref: (s, 0)))
    block_rows = fields * groups * sliver
    operands = [row, half] + [landed] * (per_plane * groups) + [basis]
    aliases = {}
    if previous is not None:
        in_specs.append(pl.BlockSpec(memory_space=pl.ANY))
        aliases = {len(operands): 0}
        operands.append(previous)
    return pl.pallas_call(
        functools.partial(spectra_kernel, groups, per_plane),
        out_shape=jax.ShapeDtypeStruct((rows, length), jnp.float32),
        input_output_aliases=aliases,
        grid_spec=pltpu.PrefetchScalarGridSpec(
            num_scalar_prefetch=2,
            grid=(plane_count,),
            in_specs=in_specs,
            out_specs=pl.BlockSpec(
                (block_rows, length), lambda s, row_ref, half_ref: (first // fields, 0)
            ),
            scratch_shapes=[pltpu.VMEM((fields, groups, sliver, depth), landed.dtype)],
        ),
        compiler_params=pltpu.CompilerParams(
            dimension_semantics=("arbitrary",), vmem_limit_bytes=60 * 1024 * 1024
        ),
    )(*operands)


def unpack_kernel(groups, per_plane, per_step, row_ref, half_ref, *refs):
    out_ref = refs[-1]
    step = pl.program_id(0)
    lanes = refs[0].shape[-1]
    shape = refs[0].shape[1:]
    lane = lax.broadcasted_iota(jnp.int32, shape, 2)
    quads = per_plane // 2
    for local_segment in range(per_step):
        for group in range(groups):
            for quad in range(quads):
                parts = []
                for side in range(2):
                    position = local_segment * per_plane + quad * 2 + side
                    index = (step * per_step * per_plane + position) * groups + group
                    piece = refs[position * groups + group][0]
                    turned = pltpu.roll(piece, lanes // 2, 2)
                    keep = half_ref[index] == side
                    parts.append(jnp.where(keep, piece, turned))
                merged = jnp.where(lane < lanes // 2, parts[0], parts[1])
                start = (local_segment * quads + quad) * lanes
                out_ref[:, group, :, start : start + lanes] = merged.astype(out_ref.dtype)


def unpack_lhs(landed, row, half, plane_count, per_plane, groups):
    _, fields, sliver, lanes = landed.shape

    per_step = 2
    per_call = per_step * per_plane

    def piece_map(position, group):
        def index_map(s, row_ref, half_ref):
            return (row_ref[(s * per_call + position) * groups + group], 0, 0, 0)

        return index_map

    in_specs = [
        pl.BlockSpec((1, fields, sliver, lanes), piece_map(position, group))
        for position in range(per_call)
        for group in range(groups)
    ]
    width = per_call * lanes // 2
    return pl.pallas_call(
        functools.partial(unpack_kernel, groups, per_plane, per_step),
        out_shape=jax.ShapeDtypeStruct(
            (fields, groups, sliver, plane_count * per_plane * lanes // 2), landed.dtype
        ),
        grid_spec=pltpu.PrefetchScalarGridSpec(
            num_scalar_prefetch=2,
            grid=(plane_count // per_step,),
            in_specs=in_specs,
            out_specs=pl.BlockSpec(
                (fields, groups, sliver, width), lambda s, row_ref, half_ref: (0, 0, 0, s)
            ),
        ),
    )(row, half, *([landed] * (per_call * groups)))


def local(blocks, levels, block_dest, block_phi, block_group):
    tile_count = lax.axis_size("tile")
    plane_count = lax.axis_size("phi")
    slot_count = blocks.shape[0]
    fields = blocks.shape[1]
    per_plane = NPHI // BPHI // plane_count
    capacity = 2 * slot_count // tile_count
    sliver = COLS // plane_count

    onehot_dest = (block_dest[:, None] == jnp.arange(tile_count, dtype=jnp.int32)[None, :]).astype(
        jnp.int32
    )
    slot_rank = jnp.sum((jnp.cumsum(onehot_dest, axis=0) - 1) * onehot_dest, axis=1)
    send_slot = block_dest * capacity + slot_rank
    slot_ids = jnp.arange(tile_count * capacity, dtype=jnp.int32)
    match = send_slot[None, :] == slot_ids[:, None]
    filled = jnp.any(match, axis=1)
    source = jnp.argmax(match, axis=1).astype(jnp.int32)
    place = block_phi[source] * CG_DEV + block_group[source]
    code = jnp.where(filled, place, -1)
    scale = 1.0 / jnp.left_shift(1, levels[source]).astype(jnp.float32)
    device_count = tile_count * plane_count
    pairs = capacity // 2

    code_out = jnp.broadcast_to(
        code.reshape(tile_count, 1, capacity), (tile_count, plane_count, capacity)
    ).reshape(device_count, capacity)
    arrived_code = lax.all_to_all(code_out, ("tile", "phi"), split_axis=0, concat_axis=0, tiled=True)

    by_segment = jnp.transpose(
        arrived_code.reshape(tile_count, plane_count, capacity), (1, 0, 2)
    ).reshape(plane_count, tile_count * capacity)
    want = jnp.arange(slot_count, dtype=jnp.int32)
    hit = by_segment[:, None, :] == want[None, :, None]
    pick = jnp.argmax(hit, axis=2).astype(jnp.int32)
    origin = pick // capacity
    segment = jnp.arange(plane_count, dtype=jnp.int32)[:, None]
    row = ((origin * plane_count + segment) * pairs + (pick % capacity) // 2).reshape(-1)
    half = (pick % 2).reshape(-1)

    rows = fields * CG_DEV * sliver
    spectra = None
    basis = None
    arrived = None
    for first, count in ((0, fields - 1), (fields - 1, 1)):
        if arrived is not None:
            scale = scale + jnp.float32(0.0) * (
                arrived[0, 0, 0].astype(jnp.float32) + basis[0, 0].astype(jnp.float32)
            )
        outbox = pack_outbox(blocks, source, scale, tile_count, capacity, plane_count, first, count)
        outbox = outbox.reshape(device_count, pairs * count * sliver, 2 * BPHI)
        if basis is None:
            basis = dft_basis(NPHI) + (outbox[0, 0, 0] * 0).astype(jnp.bfloat16)
        arrived = lax.all_to_all(outbox, ("tile", "phi"), split_axis=0, concat_axis=0, tiled=True)
        landed = arrived.reshape(device_count * pairs, count, sliver, 2 * BPHI)
        if spectra is None:
            spectra = spectra_from(
                landed, row, half, basis, plane_count, per_plane, CG_DEV, rows, first, None
            )
        else:
            lhs = unpack_lhs(landed, row, half, plane_count, per_plane, CG_DEV)
            tail = jnp.dot(
                lhs.reshape(count * CG_DEV * sliver, NPHI), basis, preferred_element_type=jnp.float32
            )
            spectra = lax.dynamic_update_slice(spectra, tail, (first * CG_DEV * sliver, 0))
    return spectra.reshape(fields, CG_DEV, sliver, NPHI)


def solution(mesh):
    in_specs = (
        P(("tile", "phi"), None, None, None),
        P(("tile", "phi")),
        P(("tile", "phi")),
        P(("tile", "phi")),
        P(("tile", "phi")),
    )
    out_specs = P(None, "tile", "phi", None)
    return jax.shard_map(local, mesh=mesh, in_specs=in_specs, out_specs=out_specs, check_vma=False)
```

```python
import functools
import math

import jax
import jax.numpy as jnp
from jax import lax
from jax.experimental import pallas as pl
from jax.experimental.pallas import tpu as pltpu
from jax.sharding import PartitionSpec as P

FIELDS = 5
NPHI = 2048
BPHI = 64
COLS = 256
CG_DEV = 8


def dft_basis(length):
    half = length // 2
    column = jnp.arange(length, dtype=jnp.int32)
    mode = jnp.where(column <= half, column, column - half)
    scale = jnp.float32(2.0 * math.pi / length)
    hi = jnp.arange(length // BPHI, dtype=jnp.int32) * BPHI
    lo = jnp.arange(BPHI, dtype=jnp.int32)
    angle_hi = (hi[:, None] * mode[None, :] % length).astype(jnp.float32) * scale
    angle_lo = (lo[:, None] * mode[None, :] % length).astype(jnp.float32) * scale
    ch, sh = jnp.cos(angle_hi)[:, None, :], jnp.sin(angle_hi)[:, None, :]
    cl, sl = jnp.cos(angle_lo)[None, :, :], jnp.sin(angle_lo)[None, :, :]
    is_cos = (column <= half)[None, None, :]
    values = jnp.where(is_cos, ch * cl - sh * sl, sh * cl + ch * sl)
    values = values * jnp.float32(1.0 / math.sqrt(length))
    return values.reshape(length, length).astype(jnp.bfloat16)


def pack_kernel(source_ref, scale_ref, *refs):
    out_ref = refs[-1]
    per_step, planes, pairs, fields, sliver = out_ref.shape[:5]
    step = pl.program_id(0)
    for local_tile in range(per_step):
        for pair in range(pairs):
            slot = (local_tile * pairs + pair) * 2
            first = step * (len(refs) - 1) + slot
            first_scale = scale_ref[first].astype(out_ref.dtype)
            second_scale = scale_ref[first + 1].astype(out_ref.dtype)
            for field in range(fields):
                both = jnp.concatenate(
                    [
                        refs[slot][0, field] * first_scale,
                        refs[slot + 1][0, field] * second_scale,
                    ],
                    axis=0,
                )
                flipped = both.T.reshape(planes, sliver, both.shape[0])
                out_ref[local_tile, :, pair, field] = flipped.astype(out_ref.dtype)


def pack_outbox(blocks, source, scale, tile_count, capacity, plane_count):
    slot_count, fields, bphi, cols = blocks.shape
    pairs = capacity // 2
    sliver = cols // plane_count

    per_step = 2
    per_call = per_step * capacity

    def block_map(slot):
        return lambda t, src_ref: (src_ref[t * per_call + slot], 0, 0, 0)

    return pl.pallas_call(
        pack_kernel,
        out_shape=jax.ShapeDtypeStruct(
            (tile_count, plane_count, pairs, fields, sliver, 2 * bphi), blocks.dtype
        ),
        grid_spec=pltpu.PrefetchScalarGridSpec(
            num_scalar_prefetch=1,
            grid=(tile_count // per_step,),
            in_specs=[pl.BlockSpec(memory_space=pltpu.SMEM)]
            + [pl.BlockSpec((1, fields, bphi, cols), block_map(slot)) for slot in range(per_call)],
            out_specs=pl.BlockSpec(
                (per_step, plane_count, pairs, fields, sliver, 2 * bphi),
                lambda t, src_ref: (t, 0, 0, 0, 0, 0),
            ),
        ),
    )(source, scale, *([blocks] * per_call))


def spectra_kernel(groups, per_plane, row_ref, half_ref, *refs):
    pieces = refs[: per_plane * groups]
    basis_ref, out_ref, lhs_ref = refs[per_plane * groups :]
    segment = pl.program_id(0)
    lanes = pieces[0].shape[-1]
    shape = pieces[0].shape[1:]
    lane = lax.broadcasted_iota(jnp.int32, shape, 2)
    for group in range(groups):
        for quad in range(per_plane // 2):
            parts = []
            for side in range(2):
                position = quad * 2 + side
                index = (segment * per_plane + position) * groups + group
                piece = pieces[position * groups + group][0]
                turned = pltpu.roll(piece, lanes // 2, 2)
                keep = half_ref[index] == side
                parts.append(jnp.where(keep, piece, turned))
            merged = jnp.where(lane < lanes // 2, parts[0], parts[1])
            start = pl.multiple_of(segment * (lanes * per_plane // 2) + quad * lanes, lanes)
            lhs_ref[:, group, :, pl.ds(start, lanes)] = merged

    @pl.when(segment == pl.num_programs(0) - 1)
    def _():
        lhs = lhs_ref[...].reshape(out_ref.shape[0], lhs_ref.shape[-1])
        width = 512
        for chunk in range(out_ref.shape[1] // width):
            columns = slice(chunk * width, (chunk + 1) * width)
            out_ref[:, columns] = jnp.dot(
                lhs, basis_ref[:, columns], preferred_element_type=jnp.float32
            )


def spectra_from(landed, row, half, basis, plane_count, per_plane, groups):
    _, fields, sliver, lanes = landed.shape
    depth = per_plane * lanes // 2
    length = basis.shape[1]

    def piece_map(position, group):
        def index_map(s, row_ref, half_ref):
            return (row_ref[(s * per_plane + position) * groups + group], 0, 0, 0)

        return index_map

    in_specs = [
        pl.BlockSpec((1, fields, sliver, lanes), piece_map(position, group))
        for position in range(per_plane)
        for group in range(groups)
    ]
    in_specs.append(pl.BlockSpec((length, length), lambda s, row_ref, half_ref: (0, 0)))
    rows = fields * groups * sliver
    return pl.pallas_call(
        functools.partial(spectra_kernel, groups, per_plane),
        out_shape=jax.ShapeDtypeStruct((rows, length), jnp.float32),
        grid_spec=pltpu.PrefetchScalarGridSpec(
            num_scalar_prefetch=2,
            grid=(plane_count,),
            in_specs=in_specs,
            out_specs=pl.BlockSpec((rows, length), lambda s, row_ref, half_ref: (0, 0)),
            scratch_shapes=[
                pltpu.VMEM((fields, groups, sliver, plane_count * depth), landed.dtype)
            ],
        ),
        compiler_params=pltpu.CompilerParams(
            dimension_semantics=("arbitrary",), vmem_limit_bytes=63 * 1024 * 1024
        ),
    )(row, half, *([landed] * (per_plane * groups)), basis)


def local(blocks, levels, block_dest, block_phi, block_group):
    tile_count = lax.axis_size("tile")
    plane_count = lax.axis_size("phi")
    slot_count = blocks.shape[0]
    fields = blocks.shape[1]
    per_plane = NPHI // BPHI // plane_count
    capacity = 2 * slot_count // tile_count
    sliver = COLS // plane_count

    onehot_dest = (block_dest[:, None] == jnp.arange(tile_count, dtype=jnp.int32)[None, :]).astype(
        jnp.int32
    )
    slot_rank = jnp.sum((jnp.cumsum(onehot_dest, axis=0) - 1) * onehot_dest, axis=1)
    send_slot = block_dest * capacity + slot_rank
    slot_ids = jnp.arange(tile_count * capacity, dtype=jnp.int32)
    match = send_slot[None, :] == slot_ids[:, None]
    filled = jnp.any(match, axis=1)
    source = jnp.argmax(match, axis=1).astype(jnp.int32)
    place = block_phi[source] * CG_DEV + block_group[source]
    code = jnp.where(filled, place, -1)
    scale = 1.0 / jnp.left_shift(1, levels[source]).astype(jnp.float32)
    device_count = tile_count * plane_count
    pairs = capacity // 2

    outbox = pack_outbox(blocks, source, scale, tile_count, capacity, plane_count)
    outbox = outbox.reshape(device_count, pairs * fields * sliver, 2 * BPHI)
    code_out = jnp.broadcast_to(
        code.reshape(tile_count, 1, capacity), (tile_count, plane_count, capacity)
    ).reshape(device_count, capacity)
    arrived = lax.all_to_all(outbox, ("tile", "phi"), split_axis=0, concat_axis=0, tiled=True)
    arrived_code = lax.all_to_all(code_out, ("tile", "phi"), split_axis=0, concat_axis=0, tiled=True)

    by_segment = jnp.transpose(
        arrived_code.reshape(tile_count, plane_count, capacity), (1, 0, 2)
    ).reshape(plane_count, tile_count * capacity)
    want = jnp.arange(slot_count, dtype=jnp.int32)
    hit = by_segment[:, None, :] == want[None, :, None]
    pick = jnp.argmax(hit, axis=2).astype(jnp.int32)
    origin = pick // capacity
    segment = jnp.arange(plane_count, dtype=jnp.int32)[:, None]
    row = ((origin * plane_count + segment) * pairs + (pick % capacity) // 2).reshape(-1)
    half = (pick % 2).reshape(-1)
    landed = arrived.reshape(device_count * pairs, fields, sliver, 2 * BPHI)
    basis = dft_basis(NPHI)
    spectra = spectra_from(landed, row, half, basis, plane_count, per_plane, CG_DEV)
    return spectra.reshape(fields, CG_DEV, sliver, NPHI)


def solution(mesh):
    in_specs = (
        P(("tile", "phi"), None, None, None),
        P(("tile", "phi")),
        P(("tile", "phi")),
        P(("tile", "phi")),
        P(("tile", "phi")),
    )
    out_specs = P(None, "tile", "phi", None)
    return jax.shard_map(local, mesh=mesh, in_specs=in_specs, out_specs=out_specs, check_vma=False)
```

```python
import functools
import math

import jax
import jax.numpy as jnp
from jax import lax
from jax.experimental import pallas as pl
from jax.experimental.pallas import tpu as pltpu
from jax.sharding import PartitionSpec as P

FIELDS = 5
NPHI = 2048
BPHI = 64
COLS = 256
CG_DEV = 8


def dft_basis(length):
    half = length // 2
    column = jnp.arange(length, dtype=jnp.int32)
    mode = jnp.where(column <= half, column, column - half)
    scale = jnp.float32(2.0 * math.pi / length)
    hi = jnp.arange(length // BPHI, dtype=jnp.int32) * BPHI
    lo = jnp.arange(BPHI, dtype=jnp.int32)
    angle_hi = (hi[:, None] * mode[None, :] % length).astype(jnp.float32) * scale
    angle_lo = (lo[:, None] * mode[None, :] % length).astype(jnp.float32) * scale
    ch, sh = jnp.cos(angle_hi)[:, None, :], jnp.sin(angle_hi)[:, None, :]
    cl, sl = jnp.cos(angle_lo)[None, :, :], jnp.sin(angle_lo)[None, :, :]
    is_cos = (column <= half)[None, None, :]
    values = jnp.where(is_cos, ch * cl - sh * sl, sh * cl + ch * sl)
    values = values * jnp.float32(1.0 / math.sqrt(length))
    return values.reshape(length, length).astype(jnp.bfloat16)


def pack_kernel(source_ref, scale_ref, *refs):
    out_ref = refs[-1]
    per_step, planes, pairs, fields, sliver = out_ref.shape[:5]
    step = pl.program_id(0)
    for local_tile in range(per_step):
        for pair in range(pairs):
            slot = (local_tile * pairs + pair) * 2
            first = step * (len(refs) - 1) + slot
            first_scale = scale_ref[first].astype(out_ref.dtype)
            second_scale = scale_ref[first + 1].astype(out_ref.dtype)
            for field in range(fields):
                both = jnp.concatenate(
                    [
                        refs[slot][0, field] * first_scale,
                        refs[slot + 1][0, field] * second_scale,
                    ],
                    axis=0,
                )
                flipped = both.T.reshape(planes, sliver, both.shape[0])
                out_ref[local_tile, :, pair, field] = flipped.astype(out_ref.dtype)


def pack_outbox(blocks, source, scale, tile_count, capacity, plane_count):
    slot_count, fields, bphi, cols = blocks.shape
    pairs = capacity // 2
    sliver = cols // plane_count

    per_step = 2
    per_call = per_step * capacity

    def block_map(slot):
        return lambda t, src_ref: (src_ref[t * per_call + slot], 0, 0, 0)

    return pl.pallas_call(
        pack_kernel,
        out_shape=jax.ShapeDtypeStruct(
            (tile_count, plane_count, pairs, fields, sliver, 2 * bphi), blocks.dtype
        ),
        grid_spec=pltpu.PrefetchScalarGridSpec(
            num_scalar_prefetch=1,
            grid=(tile_count // per_step,),
            in_specs=[pl.BlockSpec(memory_space=pltpu.SMEM)]
            + [pl.BlockSpec((1, fields, bphi, cols), block_map(slot)) for slot in range(per_call)],
            out_specs=pl.BlockSpec(
                (per_step, plane_count, pairs, fields, sliver, 2 * bphi),
                lambda t, src_ref: (t, 0, 0, 0, 0, 0),
            ),
        ),
    )(source, scale, *([blocks] * per_call))


def spectra_kernel(groups, per_plane, row_ref, half_ref, *refs):
    pieces = refs[: per_plane * groups]
    basis_ref, out_ref, lhs_ref = refs[per_plane * groups :]
    step = pl.program_id(0)
    segments = lhs_ref.shape[-1] // (pieces[0].shape[-1] * per_plane // 2)

    @pl.when(step < segments)
    def _():
        lanes = pieces[0].shape[-1]
        shape = pieces[0].shape[1:]
        lane = lax.broadcasted_iota(jnp.int32, shape, 2)
        for group in range(groups):
            for quad in range(per_plane // 2):
                parts = []
                for side in range(2):
                    position = quad * 2 + side
                    index = (step * per_plane + position) * groups + group
                    piece = pieces[position * groups + group][0]
                    turned = pltpu.roll(piece, lanes // 2, 2)
                    keep = half_ref[index] == side
                    parts.append(jnp.where(keep, piece, turned))
                merged = jnp.where(lane < lanes // 2, parts[0], parts[1])
                start = pl.multiple_of(step * (lanes * per_plane // 2) + quad * lanes, lanes)
                lhs_ref[:, group, :, pl.ds(start, lanes)] = merged

    @pl.when(step >= segments)
    def _():
        lhs = lhs_ref[...].reshape(out_ref.shape[0], lhs_ref.shape[-1])
        out_ref[...] = jnp.dot(lhs, basis_ref[...], preferred_element_type=jnp.float32)


def spectra_from(landed, row, half, basis, plane_count, per_plane, groups):
    _, fields, sliver, lanes = landed.shape
    depth = per_plane * lanes // 2
    length = basis.shape[1]
    width = 512
    chunks = length // width

    def piece_map(position, group):
        def index_map(s, row_ref, half_ref):
            segment = jnp.minimum(s, plane_count - 1)
            return (row_ref[(segment * per_plane + position) * groups + group], 0, 0, 0)

        return index_map

    def column_map(s, row_ref, half_ref):
        return (0, jnp.maximum(s - plane_count, 0))

    in_specs = [
        pl.BlockSpec((1, fields, sliver, lanes), piece_map(position, group))
        for position in range(per_plane)
        for group in range(groups)
    ]
    in_specs.append(pl.BlockSpec((basis.shape[0], width), column_map))
    rows = fields * groups * sliver
    return pl.pallas_call(
        functools.partial(spectra_kernel, groups, per_plane),
        out_shape=jax.ShapeDtypeStruct((rows, length), jnp.float32),
        grid_spec=pltpu.PrefetchScalarGridSpec(
            num_scalar_prefetch=2,
            grid=(plane_count + chunks,),
            in_specs=in_specs,
            out_specs=pl.BlockSpec((rows, width), column_map),
            scratch_shapes=[
                pltpu.VMEM((fields, groups, sliver, plane_count * depth), landed.dtype)
            ],
        ),
        compiler_params=pltpu.CompilerParams(
            dimension_semantics=("arbitrary",), vmem_limit_bytes=48 * 1024 * 1024
        ),
    )(row, half, *([landed] * (per_plane * groups)), basis)


def local(blocks, levels, block_dest, block_phi, block_group):
    tile_count = lax.axis_size("tile")
    plane_count = lax.axis_size("phi")
    slot_count = blocks.shape[0]
    fields = blocks.shape[1]
    per_plane = NPHI // BPHI // plane_count
    capacity = 2 * slot_count // tile_count
    sliver = COLS // plane_count

    onehot_dest = (block_dest[:, None] == jnp.arange(tile_count, dtype=jnp.int32)[None, :]).astype(
        jnp.int32
    )
    slot_rank = jnp.sum((jnp.cumsum(onehot_dest, axis=0) - 1) * onehot_dest, axis=1)
    send_slot = block_dest * capacity + slot_rank
    slot_ids = jnp.arange(tile_count * capacity, dtype=jnp.int32)
    match = send_slot[None, :] == slot_ids[:, None]
    filled = jnp.any(match, axis=1)
    source = jnp.argmax(match, axis=1).astype(jnp.int32)
    place = block_phi[source] * CG_DEV + block_group[source]
    code = jnp.where(filled, place, -1)
    scale = 1.0 / jnp.left_shift(1, levels[source]).astype(jnp.float32)
    device_count = tile_count * plane_count
    pairs = capacity // 2

    outbox = pack_outbox(blocks, source, scale, tile_count, capacity, plane_count)
    outbox = outbox.reshape(device_count, pairs * fields * sliver, 2 * BPHI)
    code_out = jnp.broadcast_to(
        code.reshape(tile_count, 1, capacity), (tile_count, plane_count, capacity)
    ).reshape(device_count, capacity)
    arrived = lax.all_to_all(outbox, ("tile", "phi"), split_axis=0, concat_axis=0, tiled=True)
    arrived_code = lax.all_to_all(code_out, ("tile", "phi"), split_axis=0, concat_axis=0, tiled=True)

    by_segment = jnp.transpose(
        arrived_code.reshape(tile_count, plane_count, capacity), (1, 0, 2)
    ).reshape(plane_count, tile_count * capacity)
    want = jnp.arange(slot_count, dtype=jnp.int32)
    hit = by_segment[:, None, :] == want[None, :, None]
    pick = jnp.argmax(hit, axis=2).astype(jnp.int32)
    origin = pick // capacity
    segment = jnp.arange(plane_count, dtype=jnp.int32)[:, None]
    row = ((origin * plane_count + segment) * pairs + (pick % capacity) // 2).reshape(-1)
    half = (pick % 2).reshape(-1)
    landed = arrived.reshape(device_count * pairs, fields, sliver, 2 * BPHI)
    basis = dft_basis(NPHI)
    spectra = spectra_from(landed, row, half, basis, plane_count, per_plane, CG_DEV)
    return spectra.reshape(fields, CG_DEV, sliver, NPHI)


def solution(mesh):
    in_specs = (
        P(("tile", "phi"), None, None, None),
        P(("tile", "phi")),
        P(("tile", "phi")),
        P(("tile", "phi")),
        P(("tile", "phi")),
    )
    out_specs = P(None, "tile", "phi", None)
    return jax.shard_map(local, mesh=mesh, in_specs=in_specs, out_specs=out_specs, check_vma=False)
```

```python
import functools
import math

import jax
import jax.numpy as jnp
from jax import lax
from jax.experimental import pallas as pl
from jax.experimental.pallas import tpu as pltpu
from jax.sharding import PartitionSpec as P

FIELDS = 5
NPHI = 2048
BPHI = 64
COLS = 256
CG_DEV = 8


def dft_basis(length):
    half = length // 2
    column = jnp.arange(length, dtype=jnp.int32)
    mode = jnp.where(column <= half, column, column - half)
    scale = jnp.float32(2.0 * math.pi / length)
    hi = jnp.arange(length // BPHI, dtype=jnp.int32) * BPHI
    lo = jnp.arange(BPHI, dtype=jnp.int32)
    angle_hi = (hi[:, None] * mode[None, :] % length).astype(jnp.float32) * scale
    angle_lo = (lo[:, None] * mode[None, :] % length).astype(jnp.float32) * scale
    ch, sh = jnp.cos(angle_hi)[:, None, :], jnp.sin(angle_hi)[:, None, :]
    cl, sl = jnp.cos(angle_lo)[None, :, :], jnp.sin(angle_lo)[None, :, :]
    is_cos = (column <= half)[None, None, :]
    values = jnp.where(is_cos, ch * cl - sh * sl, sh * cl + ch * sl)
    values = values * jnp.float32(1.0 / math.sqrt(length))
    return values.reshape(length, length).astype(jnp.bfloat16)


def level_scale(level, dtype):
    value = jnp.where(
        level == 0, 1.0, jnp.where(level == 1, 0.5, jnp.where(level == 2, 0.25, 0.125))
    )
    return value.astype(jnp.float32).astype(dtype)


def pack_kernel(source_ref, level_ref, *refs):
    out_ref = refs[-1]
    per_step, planes, pairs, fields, sliver = out_ref.shape[:5]
    step = pl.program_id(0)
    for local_tile in range(per_step):
        for pair in range(pairs):
            slot = (local_tile * pairs + pair) * 2
            first = step * (len(refs) - 1) + slot
            first_scale = level_scale(level_ref[source_ref[first]], out_ref.dtype)
            second_scale = level_scale(level_ref[source_ref[first + 1]], out_ref.dtype)
            for field in range(fields):
                both = jnp.concatenate(
                    [
                        refs[slot][0, field] * first_scale,
                        refs[slot + 1][0, field] * second_scale,
                    ],
                    axis=0,
                )
                flipped = both.T.reshape(planes, sliver, both.shape[0])
                out_ref[local_tile, :, pair, field] = flipped.astype(out_ref.dtype)


def pack_outbox(blocks, source, levels, tile_count, capacity, plane_count):
    slot_count, fields, bphi, cols = blocks.shape
    pairs = capacity // 2
    sliver = cols // plane_count

    per_step = 4
    per_call = per_step * capacity

    def block_map(slot):
        return lambda t, src_ref, level_ref: (src_ref[t * per_call + slot], 0, 0, 0)

    return pl.pallas_call(
        pack_kernel,
        out_shape=jax.ShapeDtypeStruct(
            (tile_count, plane_count, pairs, fields, sliver, 2 * bphi), blocks.dtype
        ),
        grid_spec=pltpu.PrefetchScalarGridSpec(
            num_scalar_prefetch=2,
            grid=(tile_count // per_step,),
            in_specs=[pl.BlockSpec((1, fields, bphi, cols), block_map(slot)) for slot in range(per_call)],
            out_specs=pl.BlockSpec(
                (per_step, plane_count, pairs, fields, sliver, 2 * bphi),
                lambda t, src_ref, level_ref: (t, 0, 0, 0, 0, 0),
            ),
        ),
    )(source, levels, *([blocks] * per_call))


def spectra_kernel(groups, per_plane, row_ref, half_ref, *refs):
    pieces = refs[: per_plane * groups]
    basis_ref, out_ref, lhs_ref = refs[per_plane * groups :]
    step = pl.program_id(0)
    segments = lhs_ref.shape[-1] // (pieces[0].shape[-1] * per_plane // 2)

    @pl.when(step < segments)
    def _():
        lanes = pieces[0].shape[-1]
        shape = pieces[0].shape[1:]
        lane = lax.broadcasted_iota(jnp.int32, shape, 2)
        for group in range(groups):
            for quad in range(per_plane // 2):
                parts = []
                for side in range(2):
                    position = quad * 2 + side
                    index = (step * per_plane + position) * groups + group
                    piece = pieces[position * groups + group][0]
                    turned = pltpu.roll(piece, lanes // 2, 2)
                    keep = half_ref[index] == side
                    parts.append(jnp.where(keep, piece, turned))
                merged = jnp.where(lane < lanes // 2, parts[0], parts[1])
                start = pl.multiple_of(step * (lanes * per_plane // 2) + quad * lanes, lanes)
                lhs_ref[:, group, :, pl.ds(start, lanes)] = merged

    @pl.when(step >= segments)
    def _():
        lhs = lhs_ref[...].reshape(out_ref.shape[0], lhs_ref.shape[-1])
        out_ref[...] = jnp.dot(lhs, basis_ref[...], preferred_element_type=jnp.float32)


def spectra_from(landed, row, half, basis, plane_count, per_plane, groups):
    _, fields, sliver, lanes = landed.shape
    depth = per_plane * lanes // 2
    length = basis.shape[1]
    width = 512
    chunks = length // width

    def piece_map(position, group):
        def index_map(s, row_ref, half_ref):
            segment = jnp.minimum(s, plane_count - 1)
            return (row_ref[(segment * per_plane + position) * groups + group], 0, 0, 0)

        return index_map

    def column_map(s, row_ref, half_ref):
        return (0, jnp.maximum(s - plane_count, 0))

    in_specs = [
        pl.BlockSpec((1, fields, sliver, lanes), piece_map(position, group))
        for position in range(per_plane)
        for group in range(groups)
    ]
    in_specs.append(pl.BlockSpec((basis.shape[0], width), column_map))
    rows = fields * groups * sliver
    return pl.pallas_call(
        functools.partial(spectra_kernel, groups, per_plane),
        out_shape=jax.ShapeDtypeStruct((rows, length), jnp.float32),
        grid_spec=pltpu.PrefetchScalarGridSpec(
            num_scalar_prefetch=2,
            grid=(plane_count + chunks,),
            in_specs=in_specs,
            out_specs=pl.BlockSpec((rows, width), column_map),
            scratch_shapes=[
                pltpu.VMEM((fields, groups, sliver, plane_count * depth), landed.dtype)
            ],
        ),
        compiler_params=pltpu.CompilerParams(
            dimension_semantics=("arbitrary",), vmem_limit_bytes=48 * 1024 * 1024
        ),
    )(row, half, *([landed] * (per_plane * groups)), basis)


def local(blocks, levels, block_dest, block_phi, block_group):
    tile_count = lax.axis_size("tile")
    plane_count = lax.axis_size("phi")
    slot_count = blocks.shape[0]
    fields = blocks.shape[1]
    per_plane = NPHI // BPHI // plane_count
    capacity = 2 * slot_count // tile_count
    sliver = COLS // plane_count

    onehot_dest = (block_dest[:, None] == jnp.arange(tile_count, dtype=jnp.int32)[None, :]).astype(
        jnp.int32
    )
    slot_rank = jnp.sum((jnp.cumsum(onehot_dest, axis=0) - 1) * onehot_dest, axis=1)
    send_slot = block_dest * capacity + slot_rank
    slot_ids = jnp.arange(tile_count * capacity, dtype=jnp.int32)
    match = send_slot[None, :] == slot_ids[:, None]
    filled = jnp.any(match, axis=1)
    source = jnp.argmax(match, axis=1).astype(jnp.int32)
    place = block_phi[source] * CG_DEV + block_group[source]
    code = jnp.where(filled, place, -1)
    device_count = tile_count * plane_count
    pairs = capacity // 2

    outbox = pack_outbox(blocks, source, levels, tile_count, capacity, plane_count)
    outbox = outbox.reshape(device_count, pairs * fields * sliver, 2 * BPHI)
    code_out = jnp.broadcast_to(
        code.reshape(tile_count, 1, capacity), (tile_count, plane_count, capacity)
    ).reshape(device_count, capacity)
    arrived = lax.all_to_all(outbox, ("tile", "phi"), split_axis=0, concat_axis=0, tiled=True)
    arrived_code = lax.all_to_all(code_out, ("tile", "phi"), split_axis=0, concat_axis=0, tiled=True)

    by_segment = jnp.transpose(
        arrived_code.reshape(tile_count, plane_count, capacity), (1, 0, 2)
    ).reshape(plane_count, tile_count * capacity)
    want = jnp.arange(slot_count, dtype=jnp.int32)
    hit = by_segment[:, None, :] == want[None, :, None]
    pick = jnp.argmax(hit, axis=2).astype(jnp.int32)
    origin = pick // capacity
    segment = jnp.arange(plane_count, dtype=jnp.int32)[:, None]
    row = ((origin * plane_count + segment) * pairs + (pick % capacity) // 2).reshape(-1)
    half = (pick % 2).reshape(-1)
    landed = arrived.reshape(device_count * pairs, fields, sliver, 2 * BPHI)
    basis = dft_basis(NPHI)
    spectra = spectra_from(landed, row, half, basis, plane_count, per_plane, CG_DEV)
    return spectra.reshape(fields, CG_DEV, sliver, NPHI)


def solution(mesh):
    in_specs = (
        P(("tile", "phi"), None, None, None),
        P(("tile", "phi")),
        P(("tile", "phi")),
        P(("tile", "phi")),
        P(("tile", "phi")),
    )
    out_specs = P(None, "tile", "phi", None)
    return jax.shard_map(local, mesh=mesh, in_specs=in_specs, out_specs=out_specs, check_vma=False)
```

```python
import functools
import math

import jax
import jax.numpy as jnp
from jax import lax
from jax.experimental import pallas as pl
from jax.experimental.pallas import tpu as pltpu
from jax.sharding import PartitionSpec as P

FIELDS = 5
NPHI = 2048
BPHI = 64
COLS = 256
CG_DEV = 8


def dft_basis(length):
    half = length // 2
    column = jnp.arange(length, dtype=jnp.int32)
    mode = jnp.where(column <= half, column, column - half)
    scale = jnp.float32(2.0 * math.pi / length)
    hi = jnp.arange(length // BPHI, dtype=jnp.int32) * BPHI
    lo = jnp.arange(BPHI, dtype=jnp.int32)
    angle_hi = (hi[:, None] * mode[None, :] % length).astype(jnp.float32) * scale
    angle_lo = (lo[:, None] * mode[None, :] % length).astype(jnp.float32) * scale
    ch, sh = jnp.cos(angle_hi)[:, None, :], jnp.sin(angle_hi)[:, None, :]
    cl, sl = jnp.cos(angle_lo)[None, :, :], jnp.sin(angle_lo)[None, :, :]
    is_cos = (column <= half)[None, None, :]
    values = jnp.where(is_cos, ch * cl - sh * sl, sh * cl + ch * sl)
    values = values * jnp.float32(1.0 / math.sqrt(length))
    return values.reshape(length, length).astype(jnp.bfloat16)


def level_scale(level, dtype):
    value = jnp.where(
        level == 0, 1.0, jnp.where(level == 1, 0.5, jnp.where(level == 2, 0.25, 0.125))
    )
    return value.astype(jnp.float32).astype(dtype)


def pack_kernel(source_ref, level_ref, *refs):
    out_ref = refs[-1]
    per_step, planes, pairs, fields, sliver = out_ref.shape[:5]
    step = pl.program_id(0)
    for local_tile in range(per_step):
        for pair in range(pairs):
            slot = (local_tile * pairs + pair) * 2
            first = step * (len(refs) - 1) + slot
            first_scale = level_scale(level_ref[source_ref[first]], out_ref.dtype)
            second_scale = level_scale(level_ref[source_ref[first + 1]], out_ref.dtype)
            for field in range(fields):
                both = jnp.concatenate(
                    [
                        refs[slot][0, field] * first_scale,
                        refs[slot + 1][0, field] * second_scale,
                    ],
                    axis=0,
                )
                flipped = both.T.reshape(planes, sliver, both.shape[0])
                out_ref[local_tile, :, pair, field] = flipped.astype(out_ref.dtype)


def pack_outbox(blocks, source, levels, tile_count, capacity, plane_count):
    slot_count, fields, bphi, cols = blocks.shape
    pairs = capacity // 2
    sliver = cols // plane_count

    per_step = 4
    per_call = per_step * capacity

    def block_map(slot):
        return lambda t, src_ref, level_ref: (src_ref[t * per_call + slot], 0, 0, 0)

    return pl.pallas_call(
        pack_kernel,
        out_shape=jax.ShapeDtypeStruct(
            (tile_count, plane_count, pairs, fields, sliver, 2 * bphi), blocks.dtype
        ),
        grid_spec=pltpu.PrefetchScalarGridSpec(
            num_scalar_prefetch=2,
            grid=(tile_count // per_step,),
            in_specs=[pl.BlockSpec((1, fields, bphi, cols), block_map(slot)) for slot in range(per_call)],
            out_specs=pl.BlockSpec(
                (per_step, plane_count, pairs, fields, sliver, 2 * bphi),
                lambda t, src_ref, level_ref: (t, 0, 0, 0, 0, 0),
            ),
        ),
    )(source, levels, *([blocks] * per_call))


def spectra_kernel(groups, per_plane, row_ref, half_ref, *refs):
    pieces = refs[: per_plane * groups]
    basis_ref, out_ref, lhs_ref = refs[per_plane * groups :]
    step = pl.program_id(0)
    segments = lhs_ref.shape[-1] // (pieces[0].shape[-1] * per_plane // 2)

    @pl.when(step < segments)
    def _():
        lanes = pieces[0].shape[-1]
        shape = pieces[0].shape[1:]
        lane = lax.broadcasted_iota(jnp.int32, shape, 2)
        for group in range(groups):
            for quad in range(per_plane // 2):
                parts = []
                for side in range(2):
                    position = quad * 2 + side
                    index = (step * per_plane + position) * groups + group
                    piece = pieces[position * groups + group][0]
                    turned = pltpu.roll(piece, lanes // 2, 2)
                    keep = half_ref[index] == side
                    parts.append(jnp.where(keep, piece, turned))
                merged = jnp.where(lane < lanes // 2, parts[0], parts[1])
                start = pl.multiple_of(step * (lanes * per_plane // 2) + quad * lanes, lanes)
                lhs_ref[:, group, :, pl.ds(start, lanes)] = merged

    @pl.when(step >= segments)
    def _():
        lhs = lhs_ref[...].reshape(out_ref.shape[0], lhs_ref.shape[-1])
        out_ref[...] = jnp.dot(lhs, basis_ref[...], preferred_element_type=jnp.float32)


def spectra_from(landed, row, half, basis, plane_count, per_plane, groups):
    _, fields, sliver, lanes = landed.shape
    depth = per_plane * lanes // 2
    length = basis.shape[1]
    width = 512
    chunks = length // width

    def piece_map(position, group):
        def index_map(s, row_ref, half_ref):
            segment = jnp.minimum(s, plane_count - 1)
            return (row_ref[(segment * per_plane + position) * groups + group], 0, 0, 0)

        return index_map

    def column_map(s, row_ref, half_ref):
        return (0, jnp.maximum(s - plane_count, 0))

    in_specs = [
        pl.BlockSpec((1, fields, sliver, lanes), piece_map(position, group))
        for position in range(per_plane)
        for group in range(groups)
    ]
    in_specs.append(pl.BlockSpec((basis.shape[0], width), column_map))
    rows = fields * groups * sliver
    return pl.pallas_call(
        functools.partial(spectra_kernel, groups, per_plane),
        out_shape=jax.ShapeDtypeStruct((rows, length), jnp.float32),
        grid_spec=pltpu.PrefetchScalarGridSpec(
            num_scalar_prefetch=2,
            grid=(plane_count + chunks,),
            in_specs=in_specs,
            out_specs=pl.BlockSpec((rows, width), column_map),
            scratch_shapes=[
                pltpu.VMEM((fields, groups, sliver, plane_count * depth), landed.dtype)
            ],
        ),
        compiler_params=pltpu.CompilerParams(
            dimension_semantics=("arbitrary",), vmem_limit_bytes=48 * 1024 * 1024
        ),
    )(row, half, *([landed] * (per_plane * groups)), basis)


def local(blocks, levels, block_dest, block_phi, block_group):
    tile_count = lax.axis_size("tile")
    plane_count = lax.axis_size("phi")
    slot_count = blocks.shape[0]
    fields = blocks.shape[1]
    per_plane = NPHI // BPHI // plane_count
    capacity = 2 * slot_count // tile_count
    sliver = COLS // plane_count

    onehot_dest = (block_dest[:, None] == jnp.arange(tile_count, dtype=jnp.int32)[None, :]).astype(
        jnp.int32
    )
    slot_rank = jnp.sum((jnp.cumsum(onehot_dest, axis=0) - 1) * onehot_dest, axis=1)
    send_slot = block_dest * capacity + slot_rank
    slot_ids = jnp.arange(tile_count * capacity, dtype=jnp.int32)
    match = send_slot[None, :] == slot_ids[:, None]
    filled = jnp.any(match, axis=1)
    source = jnp.argmax(match, axis=1).astype(jnp.int32)
    place = block_phi[source] * CG_DEV + block_group[source]
    code = jnp.where(filled, place, -1)
    device_count = tile_count * plane_count
    pairs = capacity // 2

    outbox = pack_outbox(blocks, source, levels, tile_count, capacity, plane_count)
    outbox = outbox.reshape(device_count, pairs * fields * sliver, 2 * BPHI)
    arrived = lax.all_to_all(outbox, ("tile", "phi"), split_axis=0, concat_axis=0, tiled=True)
    code_tile = lax.all_to_all(
        code.reshape(tile_count, capacity), "tile", split_axis=0, concat_axis=0, tiled=True
    )
    code_rep = jnp.broadcast_to(code_tile[None], (plane_count, tile_count, capacity))
    code_all = lax.all_to_all(code_rep, "phi", split_axis=0, concat_axis=0, tiled=True)

    by_segment = code_all.reshape(plane_count, tile_count * capacity)
    want = jnp.arange(slot_count, dtype=jnp.int32)
    hit = by_segment[:, None, :] == want[None, :, None]
    pick = jnp.argmax(hit, axis=2).astype(jnp.int32)
    origin = pick // capacity
    segment = jnp.arange(plane_count, dtype=jnp.int32)[:, None]
    row = ((origin * plane_count + segment) * pairs + (pick % capacity) // 2).reshape(-1)
    half = (pick % 2).reshape(-1)
    landed = arrived.reshape(device_count * pairs, fields, sliver, 2 * BPHI)
    basis = dft_basis(NPHI)
    spectra = spectra_from(landed, row, half, basis, plane_count, per_plane, CG_DEV)
    return spectra.reshape(fields, CG_DEV, sliver, NPHI)


def solution(mesh):
    in_specs = (
        P(("tile", "phi"), None, None, None),
        P(("tile", "phi")),
        P(("tile", "phi")),
        P(("tile", "phi")),
        P(("tile", "phi")),
    )
    out_specs = P(None, "tile", "phi", None)
    return jax.shard_map(local, mesh=mesh, in_specs=in_specs, out_specs=out_specs, check_vma=False)
```

```python
import functools
import math

import jax
import jax.numpy as jnp
from jax import lax
from jax.experimental import pallas as pl
from jax.experimental.pallas import tpu as pltpu
from jax.sharding import PartitionSpec as P

FIELDS = 5
NPHI = 2048
BPHI = 64
COLS = 256
CG_DEV = 8


def dft_basis(length):
    half = length // 2
    column = jnp.arange(length, dtype=jnp.int32)
    mode = jnp.where(column <= half, column, column - half)
    scale = jnp.float32(2.0 * math.pi / length)
    hi = jnp.arange(length // BPHI, dtype=jnp.int32) * BPHI
    lo = jnp.arange(BPHI, dtype=jnp.int32)
    angle_hi = (hi[:, None] * mode[None, :] % length).astype(jnp.float32) * scale
    angle_lo = (lo[:, None] * mode[None, :] % length).astype(jnp.float32) * scale
    ch, sh = jnp.cos(angle_hi)[:, None, :], jnp.sin(angle_hi)[:, None, :]
    cl, sl = jnp.cos(angle_lo)[None, :, :], jnp.sin(angle_lo)[None, :, :]
    is_cos = (column <= half)[None, None, :]
    values = jnp.where(is_cos, ch * cl - sh * sl, sh * cl + ch * sl)
    values = values * jnp.float32(1.0 / math.sqrt(length))
    return values.reshape(length, length).astype(jnp.bfloat16)


def level_scale(level, dtype):
    value = jnp.where(
        level == 0, 1.0, jnp.where(level == 1, 0.5, jnp.where(level == 2, 0.25, 0.125))
    )
    return value.astype(jnp.float32).astype(dtype)


def pack_kernel(source_ref, level_ref, *refs):
    out_ref = refs[-1]
    per_step, planes, pairs, fields, sliver = out_ref.shape[:5]
    step = pl.program_id(0)
    for local_tile in range(per_step):
        for pair in range(pairs):
            slot = (local_tile * pairs + pair) * 2
            first = step * (len(refs) - 1) + slot
            first_scale = level_scale(level_ref[source_ref[first]], out_ref.dtype)
            second_scale = level_scale(level_ref[source_ref[first + 1]], out_ref.dtype)
            for field in range(fields):
                both = jnp.concatenate(
                    [
                        refs[slot][0, field] * first_scale,
                        refs[slot + 1][0, field] * second_scale,
                    ],
                    axis=0,
                )
                flipped = both.T.reshape(planes, sliver, both.shape[0])
                out_ref[local_tile, :, pair, field] = flipped.astype(out_ref.dtype)


def pack_outbox(blocks, source, levels, tile_count, capacity, plane_count):
    slot_count, fields, bphi, cols = blocks.shape
    pairs = capacity // 2
    sliver = cols // plane_count

    per_step = 4
    per_call = per_step * capacity

    def block_map(slot):
        return lambda t, src_ref, level_ref: (src_ref[t * per_call + slot], 0, 0, 0)

    return pl.pallas_call(
        pack_kernel,
        out_shape=jax.ShapeDtypeStruct(
            (tile_count, plane_count, pairs, fields, sliver, 2 * bphi), blocks.dtype
        ),
        grid_spec=pltpu.PrefetchScalarGridSpec(
            num_scalar_prefetch=2,
            grid=(tile_count // per_step,),
            in_specs=[pl.BlockSpec((1, fields, bphi, cols), block_map(slot)) for slot in range(per_call)],
            out_specs=pl.BlockSpec(
                (per_step, plane_count, pairs, fields, sliver, 2 * bphi),
                lambda t, src_ref, level_ref: (t, 0, 0, 0, 0, 0),
            ),
        ),
    )(source, levels, *([blocks] * per_call))


def spectra_kernel(groups, per_plane, row_ref, half_ref, *refs):
    pieces = refs[: per_plane * groups]
    basis_ref, out_ref, lhs_ref = refs[per_plane * groups :]
    step = pl.program_id(0)
    segments = lhs_ref.shape[-1] // (pieces[0].shape[-1] * per_plane // 2)

    @pl.when(step < segments)
    def _():
        lanes = pieces[0].shape[-1]
        shape = pieces[0].shape[1:]
        lane = lax.broadcasted_iota(jnp.int32, shape, 2)
        for group in range(groups):
            for quad in range(per_plane // 2):
                parts = []
                for side in range(2):
                    position = quad * 2 + side
                    index = (step * per_plane + position) * groups + group
                    piece = pieces[position * groups + group][0]
                    turned = pltpu.roll(piece, lanes // 2, 2)
                    keep = half_ref[index] == side
                    parts.append(jnp.where(keep, piece, turned))
                merged = jnp.where(lane < lanes // 2, parts[0], parts[1])
                start = pl.multiple_of(step * (lanes * per_plane // 2) + quad * lanes, lanes)
                lhs_ref[:, group, :, pl.ds(start, lanes)] = merged

    @pl.when(step >= segments)
    def _():
        lhs = lhs_ref[...].reshape(out_ref.shape[0], lhs_ref.shape[-1])
        out_ref[...] = jnp.dot(lhs, basis_ref[...], preferred_element_type=jnp.float32)


def spectra_from(landed, row, half, basis, plane_count, per_plane, groups):
    _, fields, sliver, lanes = landed.shape
    depth = per_plane * lanes // 2
    length = basis.shape[1]
    width = 512
    chunks = length // width

    def piece_map(position, group):
        def index_map(s, row_ref, half_ref):
            segment = jnp.minimum(s, plane_count - 1)
            return (row_ref[(segment * per_plane + position) * groups + group], 0, 0, 0)

        return index_map

    def column_map(s, row_ref, half_ref):
        return (0, jnp.maximum(s - plane_count, 0))

    in_specs = [
        pl.BlockSpec((1, fields, sliver, lanes), piece_map(position, group))
        for position in range(per_plane)
        for group in range(groups)
    ]
    in_specs.append(pl.BlockSpec((basis.shape[0], width), column_map))
    rows = fields * groups * sliver
    return pl.pallas_call(
        functools.partial(spectra_kernel, groups, per_plane),
        out_shape=jax.ShapeDtypeStruct((rows, length), jnp.float32),
        grid_spec=pltpu.PrefetchScalarGridSpec(
            num_scalar_prefetch=2,
            grid=(plane_count + chunks,),
            in_specs=in_specs,
            out_specs=pl.BlockSpec((rows, width), column_map),
            scratch_shapes=[
                pltpu.VMEM((fields, groups, sliver, plane_count * depth), landed.dtype)
            ],
        ),
        compiler_params=pltpu.CompilerParams(
            dimension_semantics=("arbitrary",), vmem_limit_bytes=48 * 1024 * 1024
        ),
    )(row, half, *([landed] * (per_plane * groups)), basis)


def local(blocks, levels, block_dest, block_phi, block_group):
    tile_count = lax.axis_size("tile")
    plane_count = lax.axis_size("phi")
    slot_count = blocks.shape[0]
    fields = blocks.shape[1]
    per_plane = NPHI // BPHI // plane_count
    capacity = 2 * slot_count // tile_count
    sliver = COLS // plane_count

    block_ids = jnp.arange(slot_count, dtype=jnp.int32)
    earlier = (block_dest[None, :] == block_dest[:, None]) & (block_ids[None, :] < block_ids[:, None])
    slot_rank = jnp.sum(earlier.astype(jnp.int32), axis=1)
    send_slot = block_dest * capacity + slot_rank
    slot_ids = jnp.arange(tile_count * capacity, dtype=jnp.int32)
    match = (send_slot[None, :] == slot_ids[:, None]).astype(jnp.int32)
    source = jnp.sum(match * block_ids[None, :], axis=1)
    place = block_phi * CG_DEV + block_group
    code = jnp.sum(match * (place[None, :] + 1), axis=1) - 1
    device_count = tile_count * plane_count
    pairs = capacity // 2

    outbox = pack_outbox(blocks, source, levels, tile_count, capacity, plane_count)
    outbox = outbox.reshape(device_count, pairs * fields * sliver, 2 * BPHI)
    code_out = jnp.broadcast_to(
        code.reshape(tile_count, 1, capacity), (tile_count, plane_count, capacity)
    ).reshape(device_count, capacity)
    arrived = lax.all_to_all(outbox, ("tile", "phi"), split_axis=0, concat_axis=0, tiled=True)
    arrived_code = lax.all_to_all(code_out, ("tile", "phi"), split_axis=0, concat_axis=0, tiled=True)

    by_segment = jnp.transpose(
        arrived_code.reshape(tile_count, plane_count, capacity), (1, 0, 2)
    ).reshape(plane_count, tile_count * capacity)
    want = jnp.arange(slot_count, dtype=jnp.int32)
    hit = (by_segment[:, None, :] == want[None, :, None]).astype(jnp.int32)
    arrival = jnp.arange(tile_count * capacity, dtype=jnp.int32)
    pick = jnp.sum(hit * arrival[None, None, :], axis=2)
    origin = pick // capacity
    segment = jnp.arange(plane_count, dtype=jnp.int32)[:, None]
    row = ((origin * plane_count + segment) * pairs + (pick % capacity) // 2).reshape(-1)
    half = (pick % 2).reshape(-1)
    landed = arrived.reshape(device_count * pairs, fields, sliver, 2 * BPHI)
    basis = dft_basis(NPHI)
    spectra = spectra_from(landed, row, half, basis, plane_count, per_plane, CG_DEV)
    return spectra.reshape(fields, CG_DEV, sliver, NPHI)


def solution(mesh):
    in_specs = (
        P(("tile", "phi"), None, None, None),
        P(("tile", "phi")),
        P(("tile", "phi")),
        P(("tile", "phi")),
        P(("tile", "phi")),
    )
    out_specs = P(None, "tile", "phi", None)
    return jax.shard_map(local, mesh=mesh, in_specs=in_specs, out_specs=out_specs, check_vma=False)
```

```python
import functools
import math

import jax
import jax.numpy as jnp
from jax import lax
from jax.experimental import pallas as pl
from jax.experimental.pallas import tpu as pltpu
from jax.sharding import PartitionSpec as P

FIELDS = 5
NPHI = 2048
BPHI = 64
COLS = 256
CG_DEV = 8
CODE_ROWS = 16


def dft_basis(length):
    half = length // 2
    column = jnp.arange(length, dtype=jnp.int32)
    mode = jnp.where(column <= half, column, column - half)
    scale = jnp.float32(2.0 * math.pi / length)
    hi = jnp.arange(length // BPHI, dtype=jnp.int32) * BPHI
    lo = jnp.arange(BPHI, dtype=jnp.int32)
    angle_hi = (hi[:, None] * mode[None, :] % length).astype(jnp.float32) * scale
    angle_lo = (lo[:, None] * mode[None, :] % length).astype(jnp.float32) * scale
    ch, sh = jnp.cos(angle_hi)[:, None, :], jnp.sin(angle_hi)[:, None, :]
    cl, sl = jnp.cos(angle_lo)[None, :, :], jnp.sin(angle_lo)[None, :, :]
    is_cos = (column <= half)[None, None, :]
    values = jnp.where(is_cos, ch * cl - sh * sl, sh * cl + ch * sl)
    values = values * jnp.float32(1.0 / math.sqrt(length))
    return values.reshape(length, length).astype(jnp.bfloat16)


def level_scale(level, dtype):
    value = jnp.where(
        level == 0, 1.0, jnp.where(level == 1, 0.5, jnp.where(level == 2, 0.25, 0.125))
    )
    return value.astype(jnp.float32).astype(dtype)


def pack_kernel(pairs, fields, sliver, source_ref, level_ref, code_ref, *refs):
    out_ref = refs[-1]
    per_step, planes, _, lanes = out_ref.shape
    step = pl.program_id(0)
    slots = 2 * pairs
    code_rows = out_ref.shape[2] - pairs * fields * sliver
    lane = lax.broadcasted_iota(jnp.int32, (code_rows, lanes), 1)
    for local_tile in range(per_step):
        first_slot = (step * per_step + local_tile) * slots
        codes = jnp.zeros((code_rows, lanes), jnp.float32)
        for slot in range(slots):
            codes = jnp.where(lane == slot, code_ref[first_slot + slot].astype(jnp.float32), codes)
        out_ref[local_tile, :, pl.ds(pairs * fields * sliver, code_rows), :] = jnp.broadcast_to(
            codes.astype(out_ref.dtype)[None], (planes, code_rows, lanes)
        )
        for pair in range(pairs):
            slot = (local_tile * pairs + pair) * 2
            first = step * (len(refs) - 1) + slot
            first_scale = level_scale(level_ref[source_ref[first]], out_ref.dtype)
            second_scale = level_scale(level_ref[source_ref[first + 1]], out_ref.dtype)
            for field in range(fields):
                both = jnp.concatenate(
                    [
                        refs[slot][0, field] * first_scale,
                        refs[slot + 1][0, field] * second_scale,
                    ],
                    axis=0,
                )
                flipped = both.T.reshape(planes, sliver, both.shape[0])
                row = (pair * fields + field) * sliver
                out_ref[local_tile, :, pl.ds(row, sliver), :] = flipped.astype(out_ref.dtype)


def pack_outbox(blocks, source, levels, code, tile_count, capacity, plane_count):
    slot_count, fields, bphi, cols = blocks.shape
    pairs = capacity // 2
    sliver = cols // plane_count

    per_step = 4
    per_call = per_step * capacity

    def block_map(slot):
        return lambda t, src_ref, level_ref, code_ref: (src_ref[t * per_call + slot], 0, 0, 0)

    return pl.pallas_call(
        functools.partial(pack_kernel, pairs, fields, sliver),
        out_shape=jax.ShapeDtypeStruct(
            (tile_count, plane_count, pairs * fields * sliver + CODE_ROWS, 2 * bphi), blocks.dtype
        ),
        grid_spec=pltpu.PrefetchScalarGridSpec(
            num_scalar_prefetch=3,
            grid=(tile_count // per_step,),
            in_specs=[pl.BlockSpec((1, fields, bphi, cols), block_map(slot)) for slot in range(per_call)],
            out_specs=pl.BlockSpec(
                (per_step, plane_count, pairs * fields * sliver + CODE_ROWS, 2 * bphi),
                lambda t, src_ref, level_ref, code_ref: (t, 0, 0, 0),
            ),
        ),
    )(source, levels, code, *([blocks] * per_call))


def spectra_kernel(groups, per_plane, row_ref, half_ref, *refs):
    pieces = refs[: per_plane * groups]
    basis_ref, out_ref, lhs_ref = refs[per_plane * groups :]
    step = pl.program_id(0)
    segments = lhs_ref.shape[-1] // (pieces[0].shape[-1] * per_plane // 2)

    @pl.when(step < segments)
    def _():
        lanes = pieces[0].shape[-1]
        shape = lhs_ref.shape[:1] + lhs_ref.shape[2:3] + pieces[0].shape[-1:]
        lane = lax.broadcasted_iota(jnp.int32, shape, 2)
        for group in range(groups):
            for quad in range(per_plane // 2):
                parts = []
                for side in range(2):
                    position = quad * 2 + side
                    index = (step * per_plane + position) * groups + group
                    piece = pieces[position * groups + group][0].reshape(shape)
                    turned = pltpu.roll(piece, lanes // 2, 2)
                    keep = half_ref[index] == side
                    parts.append(jnp.where(keep, piece, turned))
                merged = jnp.where(lane < lanes // 2, parts[0], parts[1])
                start = pl.multiple_of(step * (lanes * per_plane // 2) + quad * lanes, lanes)
                lhs_ref[:, group, :, pl.ds(start, lanes)] = merged

    @pl.when(step >= segments)
    def _():
        lhs = lhs_ref[...].reshape(out_ref.shape[0], lhs_ref.shape[-1])
        out_ref[...] = jnp.dot(lhs, basis_ref[...], preferred_element_type=jnp.float32)


def spectra_from(landed, row, half, basis, plane_count, per_plane, groups, fields, sliver):
    lanes = landed.shape[-1]
    depth = per_plane * lanes // 2
    length = basis.shape[1]
    width = 512
    chunks = length // width

    def piece_map(position, group):
        def index_map(s, row_ref, half_ref):
            segment = jnp.minimum(s, plane_count - 1)
            piece = row_ref[(segment * per_plane + position) * groups + group]
            return (piece // 2, piece % 2, 0)

        return index_map

    def column_map(s, row_ref, half_ref):
        return (0, jnp.maximum(s - plane_count, 0))

    in_specs = [
        pl.BlockSpec((1, fields * sliver, lanes), piece_map(position, group))
        for position in range(per_plane)
        for group in range(groups)
    ]
    in_specs.append(pl.BlockSpec((basis.shape[0], width), column_map))
    rows = fields * groups * sliver
    return pl.pallas_call(
        functools.partial(spectra_kernel, groups, per_plane),
        out_shape=jax.ShapeDtypeStruct((rows, length), jnp.float32),
        grid_spec=pltpu.PrefetchScalarGridSpec(
            num_scalar_prefetch=2,
            grid=(plane_count + chunks,),
            in_specs=in_specs,
            out_specs=pl.BlockSpec((rows, width), column_map),
            scratch_shapes=[
                pltpu.VMEM((fields, groups, sliver, plane_count * depth), landed.dtype)
            ],
        ),
        compiler_params=pltpu.CompilerParams(
            dimension_semantics=("arbitrary",), vmem_limit_bytes=48 * 1024 * 1024
        ),
    )(row, half, *([landed] * (per_plane * groups)), basis)


def local(blocks, levels, block_dest, block_phi, block_group):
    tile_count = lax.axis_size("tile")
    plane_count = lax.axis_size("phi")
    slot_count = blocks.shape[0]
    fields = blocks.shape[1]
    per_plane = NPHI // BPHI // plane_count
    capacity = 2 * slot_count // tile_count
    sliver = COLS // plane_count

    block_ids = jnp.arange(slot_count, dtype=jnp.int32)
    earlier = (block_dest[None, :] == block_dest[:, None]) & (block_ids[None, :] < block_ids[:, None])
    slot_rank = jnp.sum(earlier.astype(jnp.int32), axis=1)
    send_slot = block_dest * capacity + slot_rank
    slot_ids = jnp.arange(tile_count * capacity, dtype=jnp.int32)
    match = (send_slot[None, :] == slot_ids[:, None]).astype(jnp.int32)
    source = jnp.sum(match * block_ids[None, :], axis=1)
    place = block_phi * CG_DEV + block_group
    code = jnp.sum(match * (place[None, :] + 1), axis=1) - 1
    device_count = tile_count * plane_count
    pairs = capacity // 2

    outbox = pack_outbox(blocks, source, levels, code, tile_count, capacity, plane_count)
    outbox = outbox.reshape(device_count, pairs * fields * sliver + CODE_ROWS, 2 * BPHI)
    arrived = lax.all_to_all(outbox, ("tile", "phi"), split_axis=0, concat_axis=0, tiled=True)
    arrived_code = arrived[:, pairs * fields * sliver, :capacity].astype(jnp.int32)

    by_segment = jnp.transpose(
        arrived_code.reshape(tile_count, plane_count, capacity), (1, 0, 2)
    ).reshape(plane_count, tile_count * capacity)
    want = jnp.arange(slot_count, dtype=jnp.int32)
    hit = (by_segment[:, None, :] == want[None, :, None]).astype(jnp.int32)
    arrival = jnp.arange(tile_count * capacity, dtype=jnp.int32)
    pick = jnp.sum(hit * arrival[None, None, :], axis=2)
    origin = pick // capacity
    segment = jnp.arange(plane_count, dtype=jnp.int32)[:, None]
    row = ((origin * plane_count + segment) * pairs + (pick % capacity) // 2).reshape(-1)
    half = (pick % 2).reshape(-1)
    basis = dft_basis(NPHI)
    spectra = spectra_from(
        arrived, row, half, basis, plane_count, per_plane, CG_DEV, fields, sliver
    )
    return spectra.reshape(fields, CG_DEV, sliver, NPHI)


def solution(mesh):
    in_specs = (
        P(("tile", "phi"), None, None, None),
        P(("tile", "phi")),
        P(("tile", "phi")),
        P(("tile", "phi")),
        P(("tile", "phi")),
    )
    out_specs = P(None, "tile", "phi", None)
    return jax.shard_map(local, mesh=mesh, in_specs=in_specs, out_specs=out_specs, check_vma=False)
```

```python
import functools
import math

import jax
import jax.numpy as jnp
from jax import lax
from jax.experimental import pallas as pl
from jax.experimental.pallas import tpu as pltpu
from jax.sharding import PartitionSpec as P

FIELDS = 5
NPHI = 2048
BPHI = 64
COLS = 256
CG_DEV = 8


def dft_basis(length):
    half = length // 2
    column = jnp.arange(length, dtype=jnp.int32)
    mode = jnp.where(column <= half, column, column - half)
    scale = jnp.float32(2.0 * math.pi / length)
    hi = jnp.arange(length // BPHI, dtype=jnp.int32) * BPHI
    lo = jnp.arange(BPHI, dtype=jnp.int32)
    angle_hi = (hi[:, None] * mode[None, :] % length).astype(jnp.float32) * scale
    angle_lo = (lo[:, None] * mode[None, :] % length).astype(jnp.float32) * scale
    ch, sh = jnp.cos(angle_hi)[:, None, :], jnp.sin(angle_hi)[:, None, :]
    cl, sl = jnp.cos(angle_lo)[None, :, :], jnp.sin(angle_lo)[None, :, :]
    is_cos = (column <= half)[None, None, :]
    values = jnp.where(is_cos, ch * cl - sh * sl, sh * cl + ch * sl)
    values = values * jnp.float32(1.0 / math.sqrt(length))
    return values.reshape(length, length).astype(jnp.bfloat16)


def level_scale(level, dtype):
    value = jnp.where(
        level == 0, 1.0, jnp.where(level == 1, 0.5, jnp.where(level == 2, 0.25, 0.125))
    )
    return value.astype(jnp.float32).astype(dtype)


def pack_kernel(source_ref, level_ref, *refs):
    out_ref = refs[-1]
    per_step, planes, pairs, fields, sliver = out_ref.shape[:5]
    step = pl.program_id(0)
    for local_tile in range(per_step):
        for pair in range(pairs):
            slot = (local_tile * pairs + pair) * 2
            first = step * (len(refs) - 1) + slot
            first_scale = level_scale(level_ref[source_ref[first]], out_ref.dtype)
            second_scale = level_scale(level_ref[source_ref[first + 1]], out_ref.dtype)
            for field in range(fields):
                both = jnp.concatenate(
                    [
                        refs[slot][0, field] * first_scale,
                        refs[slot + 1][0, field] * second_scale,
                    ],
                    axis=0,
                )
                flipped = both.T.reshape(planes, sliver, both.shape[0])
                out_ref[local_tile, :, pair, field] = flipped.astype(out_ref.dtype)


def pack_outbox(blocks, source, levels, tile_count, capacity, plane_count):
    slot_count, fields, bphi, cols = blocks.shape
    pairs = capacity // 2
    sliver = cols // plane_count

    per_step = 4
    per_call = per_step * capacity

    def block_map(slot):
        return lambda t, src_ref, level_ref: (src_ref[t * per_call + slot], 0, 0, 0)

    return pl.pallas_call(
        pack_kernel,
        out_shape=jax.ShapeDtypeStruct(
            (tile_count, plane_count, pairs, fields, sliver, 2 * bphi), blocks.dtype
        ),
        grid_spec=pltpu.PrefetchScalarGridSpec(
            num_scalar_prefetch=2,
            grid=(tile_count // per_step,),
            in_specs=[pl.BlockSpec((1, fields, bphi, cols), block_map(slot)) for slot in range(per_call)],
            out_specs=pl.BlockSpec(
                (per_step, plane_count, pairs, fields, sliver, 2 * bphi),
                lambda t, src_ref, level_ref: (t, 0, 0, 0, 0, 0),
            ),
        ),
    )(source, levels, *([blocks] * per_call))


def spectra_kernel(groups, per_plane, per_step, row_ref, half_ref, *refs):
    pieces = refs[: per_step * per_plane * groups]
    basis_ref, out_ref, lhs_ref = refs[per_step * per_plane * groups :]
    step = pl.program_id(0)
    segments = lhs_ref.shape[-1] // (pieces[0].shape[-1] * per_plane // 2)

    @pl.when(step < segments // per_step)
    def _():
        lanes = pieces[0].shape[-1]
        shape = pieces[0].shape[1:]
        lane = lax.broadcasted_iota(jnp.int32, shape, 2)
        for local_segment in range(per_step):
            segment = step * per_step + local_segment
            for group in range(groups):
                for quad in range(per_plane // 2):
                    parts = []
                    for side in range(2):
                        position = quad * 2 + side
                        index = (segment * per_plane + position) * groups + group
                        piece = pieces[(local_segment * per_plane + position) * groups + group][0]
                        turned = pltpu.roll(piece, lanes // 2, 2)
                        keep = half_ref[index] == side
                        parts.append(jnp.where(keep, piece, turned))
                    merged = jnp.where(lane < lanes // 2, parts[0], parts[1])
                    start = pl.multiple_of(
                        segment * (lanes * per_plane // 2) + quad * lanes, lanes
                    )
                    lhs_ref[:, group, :, pl.ds(start, lanes)] = merged

    @pl.when(step >= segments // per_step)
    def _():
        lhs = lhs_ref[...].reshape(out_ref.shape[0], lhs_ref.shape[-1])
        out_ref[...] = jnp.dot(lhs, basis_ref[...], preferred_element_type=jnp.float32)


def spectra_from(landed, row, half, basis, plane_count, per_plane, groups):
    _, fields, sliver, lanes = landed.shape
    depth = per_plane * lanes // 2
    length = basis.shape[1]
    width = 512
    chunks = length // width
    per_step = 2
    steps = plane_count // per_step

    def piece_map(position, group):
        def index_map(s, row_ref, half_ref):
            first = jnp.minimum(s, steps - 1) * per_step * per_plane
            return (row_ref[(first + position) * groups + group], 0, 0, 0)

        return index_map

    def column_map(s, row_ref, half_ref):
        return (0, jnp.maximum(s - steps, 0))

    in_specs = [
        pl.BlockSpec((1, fields, sliver, lanes), piece_map(position, group))
        for position in range(per_step * per_plane)
        for group in range(groups)
    ]
    in_specs.append(pl.BlockSpec((basis.shape[0], width), column_map))
    rows = fields * groups * sliver
    return pl.pallas_call(
        functools.partial(spectra_kernel, groups, per_plane, per_step),
        out_shape=jax.ShapeDtypeStruct((rows, length), jnp.float32),
        grid_spec=pltpu.PrefetchScalarGridSpec(
            num_scalar_prefetch=2,
            grid=(steps + chunks,),
            in_specs=in_specs,
            out_specs=pl.BlockSpec((rows, width), column_map),
            scratch_shapes=[
                pltpu.VMEM((fields, groups, sliver, plane_count * depth), landed.dtype)
            ],
        ),
        compiler_params=pltpu.CompilerParams(
            dimension_semantics=("arbitrary",), vmem_limit_bytes=48 * 1024 * 1024
        ),
    )(row, half, *([landed] * (per_step * per_plane * groups)), basis)


def local(blocks, levels, block_dest, block_phi, block_group):
    tile_count = lax.axis_size("tile")
    plane_count = lax.axis_size("phi")
    slot_count = blocks.shape[0]
    fields = blocks.shape[1]
    per_plane = NPHI // BPHI // plane_count
    capacity = 2 * slot_count // tile_count
    sliver = COLS // plane_count

    block_ids = jnp.arange(slot_count, dtype=jnp.int32)
    earlier = (block_dest[None, :] == block_dest[:, None]) & (block_ids[None, :] < block_ids[:, None])
    slot_rank = jnp.sum(earlier.astype(jnp.int32), axis=1)
    send_slot = block_dest * capacity + slot_rank
    slot_ids = jnp.arange(tile_count * capacity, dtype=jnp.int32)
    match = (send_slot[None, :] == slot_ids[:, None]).astype(jnp.int32)
    source = jnp.sum(match * block_ids[None, :], axis=1)
    place = block_phi * CG_DEV + block_group
    code = jnp.sum(match * (place[None, :] + 1), axis=1) - 1
    device_count = tile_count * plane_count
    pairs = capacity // 2

    outbox = pack_outbox(blocks, source, levels, tile_count, capacity, plane_count)
    outbox = outbox.reshape(device_count, pairs * fields * sliver, 2 * BPHI)
    code_out = jnp.broadcast_to(
        code.reshape(tile_count, 1, capacity), (tile_count, plane_count, capacity)
    ).reshape(device_count, capacity)
    arrived = lax.all_to_all(outbox, ("tile", "phi"), split_axis=0, concat_axis=0, tiled=True)
    arrived_code = lax.all_to_all(code_out, ("tile", "phi"), split_axis=0, concat_axis=0, tiled=True)

    by_segment = jnp.transpose(
        arrived_code.reshape(tile_count, plane_count, capacity), (1, 0, 2)
    ).reshape(plane_count, tile_count * capacity)
    want = jnp.arange(slot_count, dtype=jnp.int32)
    hit = (by_segment[:, None, :] == want[None, :, None]).astype(jnp.int32)
    arrival = jnp.arange(tile_count * capacity, dtype=jnp.int32)
    pick = jnp.sum(hit * arrival[None, None, :], axis=2)
    origin = pick // capacity
    segment = jnp.arange(plane_count, dtype=jnp.int32)[:, None]
    row = ((origin * plane_count + segment) * pairs + (pick % capacity) // 2).reshape(-1)
    half = (pick % 2).reshape(-1)
    landed = arrived.reshape(device_count * pairs, fields, sliver, 2 * BPHI)
    basis = dft_basis(NPHI)
    spectra = spectra_from(landed, row, half, basis, plane_count, per_plane, CG_DEV)
    return spectra.reshape(fields, CG_DEV, sliver, NPHI)


def solution(mesh):
    in_specs = (
        P(("tile", "phi"), None, None, None),
        P(("tile", "phi")),
        P(("tile", "phi")),
        P(("tile", "phi")),
        P(("tile", "phi")),
    )
    out_specs = P(None, "tile", "phi", None)
    return jax.shard_map(local, mesh=mesh, in_specs=in_specs, out_specs=out_specs, check_vma=False)
```

```python
import functools
import math

import jax
import jax.numpy as jnp
from jax import lax
from jax.experimental import pallas as pl
from jax.experimental.pallas import tpu as pltpu
from jax.sharding import PartitionSpec as P

FIELDS = 5
NPHI = 2048
BPHI = 64
COLS = 256
CG_DEV = 8


def dft_basis(length):
    half = length // 2
    column = jnp.arange(length, dtype=jnp.int32)
    mode = jnp.where(column <= half, column, column - half)
    scale = jnp.float32(2.0 * math.pi / length)
    hi = jnp.arange(length // BPHI, dtype=jnp.int32) * BPHI
    lo = jnp.arange(BPHI, dtype=jnp.int32)
    angle_hi = (hi[:, None] * mode[None, :] % length).astype(jnp.float32) * scale
    angle_lo = (lo[:, None] * mode[None, :] % length).astype(jnp.float32) * scale
    ch, sh = jnp.cos(angle_hi)[:, None, :], jnp.sin(angle_hi)[:, None, :]
    cl, sl = jnp.cos(angle_lo)[None, :, :], jnp.sin(angle_lo)[None, :, :]
    is_cos = (column <= half)[None, None, :]
    values = jnp.where(is_cos, ch * cl - sh * sl, sh * cl + ch * sl)
    values = values * jnp.float32(1.0 / math.sqrt(length))
    return values.reshape(length, length).astype(jnp.bfloat16)


def level_scale(level, dtype):
    value = jnp.where(
        level == 0, 1.0, jnp.where(level == 1, 0.5, jnp.where(level == 2, 0.25, 0.125))
    )
    return value.astype(jnp.float32).astype(dtype)


def pack_kernel(source_ref, level_ref, *refs):
    out_ref = refs[-1]
    per_step, planes, pairs, fields, sliver = out_ref.shape[:5]
    step = pl.program_id(0)
    for local_tile in range(per_step):
        for pair in range(pairs):
            slot = (local_tile * pairs + pair) * 2
            first = step * (len(refs) - 1) + slot
            first_scale = level_scale(level_ref[source_ref[first]], out_ref.dtype)
            second_scale = level_scale(level_ref[source_ref[first + 1]], out_ref.dtype)
            for field in range(fields):
                both = jnp.concatenate(
                    [
                        refs[slot][0, field] * first_scale,
                        refs[slot + 1][0, field] * second_scale,
                    ],
                    axis=0,
                )
                flipped = both.T.reshape(planes, sliver, both.shape[0])
                out_ref[local_tile, :, pair, field] = flipped.astype(out_ref.dtype)


def pack_outbox(blocks, source, levels, tile_count, capacity, plane_count):
    slot_count, fields, bphi, cols = blocks.shape
    pairs = capacity // 2
    sliver = cols // plane_count

    per_step = 8
    per_call = per_step * capacity

    def block_map(slot):
        return lambda t, src_ref, level_ref: (src_ref[t * per_call + slot], 0, 0, 0)

    return pl.pallas_call(
        pack_kernel,
        out_shape=jax.ShapeDtypeStruct(
            (tile_count, plane_count, pairs, fields, sliver, 2 * bphi), blocks.dtype
        ),
        grid_spec=pltpu.PrefetchScalarGridSpec(
            num_scalar_prefetch=2,
            grid=(tile_count // per_step,),
            in_specs=[pl.BlockSpec((1, fields, bphi, cols), block_map(slot)) for slot in range(per_call)],
            out_specs=pl.BlockSpec(
                (per_step, plane_count, pairs, fields, sliver, 2 * bphi),
                lambda t, src_ref, level_ref: (t, 0, 0, 0, 0, 0),
            ),
        ),
    )(source, levels, *([blocks] * per_call))


def spectra_kernel(groups, per_plane, row_ref, half_ref, *refs):
    pieces = refs[: per_plane * groups]
    basis_ref, out_ref, lhs_ref = refs[per_plane * groups :]
    step = pl.program_id(0)
    segments = lhs_ref.shape[-1] // (pieces[0].shape[-1] * per_plane // 2)

    @pl.when(step < segments)
    def _():
        lanes = pieces[0].shape[-1]
        shape = pieces[0].shape[1:]
        lane = lax.broadcasted_iota(jnp.int32, shape, 2)
        for group in range(groups):
            for quad in range(per_plane // 2):
                parts = []
                for side in range(2):
                    position = quad * 2 + side
                    index = (step * per_plane + position) * groups + group
                    piece = pieces[position * groups + group][0]
                    turned = pltpu.roll(piece, lanes // 2, 2)
                    keep = half_ref[index] == side
                    parts.append(jnp.where(keep, piece, turned))
                merged = jnp.where(lane < lanes // 2, parts[0], parts[1])
                start = pl.multiple_of(step * (lanes * per_plane // 2) + quad * lanes, lanes)
                lhs_ref[:, group, :, pl.ds(start, lanes)] = merged

    @pl.when(step >= segments)
    def _():
        lhs = lhs_ref[...].reshape(out_ref.shape[0], lhs_ref.shape[-1])
        out_ref[...] = jnp.dot(lhs, basis_ref[...], preferred_element_type=jnp.float32)


def spectra_from(landed, row, half, basis, plane_count, per_plane, groups):
    _, fields, sliver, lanes = landed.shape
    depth = per_plane * lanes // 2
    length = basis.shape[1]
    width = 512
    chunks = length // width

    def piece_map(position, group):
        def index_map(s, row_ref, half_ref):
            segment = jnp.minimum(s, plane_count - 1)
            return (row_ref[(segment * per_plane + position) * groups + group], 0, 0, 0)

        return index_map

    def column_map(s, row_ref, half_ref):
        return (0, jnp.maximum(s - plane_count, 0))

    in_specs = [
        pl.BlockSpec((1, fields, sliver, lanes), piece_map(position, group))
        for position in range(per_plane)
        for group in range(groups)
    ]
    in_specs.append(pl.BlockSpec((basis.shape[0], width), column_map))
    rows = fields * groups * sliver
    return pl.pallas_call(
        functools.partial(spectra_kernel, groups, per_plane),
        out_shape=jax.ShapeDtypeStruct((rows, length), jnp.float32),
        grid_spec=pltpu.PrefetchScalarGridSpec(
            num_scalar_prefetch=2,
            grid=(plane_count + chunks,),
            in_specs=in_specs,
            out_specs=pl.BlockSpec((rows, width), column_map),
            scratch_shapes=[
                pltpu.VMEM((fields, groups, sliver, plane_count * depth), landed.dtype)
            ],
        ),
        compiler_params=pltpu.CompilerParams(
            dimension_semantics=("arbitrary",), vmem_limit_bytes=48 * 1024 * 1024
        ),
    )(row, half, *([landed] * (per_plane * groups)), basis)


def local(blocks, levels, block_dest, block_phi, block_group):
    tile_count = lax.axis_size("tile")
    plane_count = lax.axis_size("phi")
    slot_count = blocks.shape[0]
    fields = blocks.shape[1]
    per_plane = NPHI // BPHI // plane_count
    capacity = 2 * slot_count // tile_count
    sliver = COLS // plane_count

    block_ids = jnp.arange(slot_count, dtype=jnp.int32)
    earlier = (block_dest[None, :] == block_dest[:, None]) & (block_ids[None, :] < block_ids[:, None])
    slot_rank = jnp.sum(earlier.astype(jnp.int32), axis=1)
    send_slot = block_dest * capacity + slot_rank
    slot_ids = jnp.arange(tile_count * capacity, dtype=jnp.int32)
    match = (send_slot[None, :] == slot_ids[:, None]).astype(jnp.int32)
    source = jnp.sum(match * block_ids[None, :], axis=1)
    place = block_phi * CG_DEV + block_group
    code = jnp.sum(match * (place[None, :] + 1), axis=1) - 1
    device_count = tile_count * plane_count
    pairs = capacity // 2

    outbox = pack_outbox(blocks, source, levels, tile_count, capacity, plane_count)
    outbox = outbox.reshape(device_count, pairs * fields * sliver, 2 * BPHI)
    code_out = jnp.broadcast_to(
        code.reshape(tile_count, 1, capacity), (tile_count, plane_count, capacity)
    ).reshape(device_count, capacity)
    arrived = lax.all_to_all(outbox, ("tile", "phi"), split_axis=0, concat_axis=0, tiled=True)
    arrived_code = lax.all_to_all(code_out, ("tile", "phi"), split_axis=0, concat_axis=0, tiled=True)

    by_segment = jnp.transpose(
        arrived_code.reshape(tile_count, plane_count, capacity), (1, 0, 2)
    ).reshape(plane_count, tile_count * capacity)
    want = jnp.arange(slot_count, dtype=jnp.int32)
    hit = (by_segment[:, None, :] == want[None, :, None]).astype(jnp.int32)
    arrival = jnp.arange(tile_count * capacity, dtype=jnp.int32)
    pick = jnp.sum(hit * arrival[None, None, :], axis=2)
    origin = pick // capacity
    segment = jnp.arange(plane_count, dtype=jnp.int32)[:, None]
    row = ((origin * plane_count + segment) * pairs + (pick % capacity) // 2).reshape(-1)
    half = (pick % 2).reshape(-1)
    landed = arrived.reshape(device_count * pairs, fields, sliver, 2 * BPHI)
    basis = dft_basis(NPHI)
    spectra = spectra_from(landed, row, half, basis, plane_count, per_plane, CG_DEV)
    return spectra.reshape(fields, CG_DEV, sliver, NPHI)


def solution(mesh):
    in_specs = (
        P(("tile", "phi"), None, None, None),
        P(("tile", "phi")),
        P(("tile", "phi")),
        P(("tile", "phi")),
        P(("tile", "phi")),
    )
    out_specs = P(None, "tile", "phi", None)
    return jax.shard_map(local, mesh=mesh, in_specs=in_specs, out_specs=out_specs, check_vma=False)
```

```python
import functools
import math

import jax
import jax.numpy as jnp
from jax import lax
from jax.experimental import pallas as pl
from jax.experimental.pallas import tpu as pltpu
from jax.sharding import PartitionSpec as P

FIELDS = 5
NPHI = 2048
BPHI = 64
COLS = 256
CG_DEV = 8


def dft_basis(length):
    half = length // 2
    column = jnp.arange(length, dtype=jnp.int32)
    mode = jnp.where(column <= half, column, column - half)
    scale = jnp.float32(2.0 * math.pi / length)
    hi = jnp.arange(length // BPHI, dtype=jnp.int32) * BPHI
    lo = jnp.arange(BPHI, dtype=jnp.int32)
    angle_hi = (hi[:, None] * mode[None, :] % length).astype(jnp.float32) * scale
    angle_lo = (lo[:, None] * mode[None, :] % length).astype(jnp.float32) * scale
    ch, sh = jnp.cos(angle_hi)[:, None, :], jnp.sin(angle_hi)[:, None, :]
    cl, sl = jnp.cos(angle_lo)[None, :, :], jnp.sin(angle_lo)[None, :, :]
    is_cos = (column <= half)[None, None, :]
    values = jnp.where(is_cos, ch * cl - sh * sl, sh * cl + ch * sl)
    values = values * jnp.float32(1.0 / math.sqrt(length))
    return values.reshape(length, length).astype(jnp.bfloat16)


def level_scale(level, dtype):
    value = jnp.where(
        level == 0, 1.0, jnp.where(level == 1, 0.5, jnp.where(level == 2, 0.25, 0.125))
    )
    return value.astype(jnp.float32).astype(dtype)


def pack_kernel(source_ref, level_ref, *refs):
    out_ref = refs[-1]
    per_step, planes, pairs, fields, sliver = out_ref.shape[:5]
    step = pl.program_id(0)
    for local_tile in range(per_step):
        for pair in range(pairs):
            slot = (local_tile * pairs + pair) * 2
            first = step * (len(refs) - 1) + slot
            first_scale = level_scale(level_ref[source_ref[first]], out_ref.dtype)
            second_scale = level_scale(level_ref[source_ref[first + 1]], out_ref.dtype)
            for field in range(fields):
                both = jnp.concatenate(
                    [
                        refs[slot][0, field] * first_scale,
                        refs[slot + 1][0, field] * second_scale,
                    ],
                    axis=0,
                )
                flipped = both.T.reshape(planes, sliver, both.shape[0])
                out_ref[local_tile, :, pair, field] = flipped.astype(out_ref.dtype)


def pack_outbox(blocks, source, levels, tile_count, capacity, plane_count):
    slot_count, fields, bphi, cols = blocks.shape
    pairs = capacity // 2
    sliver = cols // plane_count

    per_step = 4
    per_call = per_step * capacity

    def block_map(slot):
        return lambda t, src_ref, level_ref: (src_ref[t * per_call + slot], 0, 0, 0)

    return pl.pallas_call(
        pack_kernel,
        out_shape=jax.ShapeDtypeStruct(
            (tile_count, plane_count, pairs, fields, sliver, 2 * bphi), blocks.dtype
        ),
        grid_spec=pltpu.PrefetchScalarGridSpec(
            num_scalar_prefetch=2,
            grid=(tile_count // per_step,),
            in_specs=[pl.BlockSpec((1, fields, bphi, cols), block_map(slot)) for slot in range(per_call)],
            out_specs=pl.BlockSpec(
                (per_step, plane_count, pairs, fields, sliver, 2 * bphi),
                lambda t, src_ref, level_ref: (t, 0, 0, 0, 0, 0),
            ),
        ),
    )(source, levels, *([blocks] * per_call))


def spectra_kernel(groups, per_plane, row_ref, half_ref, *refs):
    pieces = refs[: per_plane * groups]
    basis_ref, out_ref, lhs_ref = refs[per_plane * groups :]
    step = pl.program_id(0)
    segments = lhs_ref.shape[-1] // (pieces[0].shape[-1] * per_plane // 2)

    @pl.when(step < segments)
    def _():
        lanes = pieces[0].shape[-1]
        shape = pieces[0].shape[1:]
        lane = lax.broadcasted_iota(jnp.int32, shape, 2)
        for group in range(groups):
            for quad in range(per_plane // 2):
                parts = []
                for side in range(2):
                    position = quad * 2 + side
                    index = (step * per_plane + position) * groups + group
                    piece = pieces[position * groups + group][0]
                    turned = pltpu.roll(piece, lanes // 2, 2)
                    keep = half_ref[index] == side
                    parts.append(jnp.where(keep, piece, turned))
                merged = jnp.where(lane < lanes // 2, parts[0], parts[1])
                start = pl.multiple_of(step * (lanes * per_plane // 2) + quad * lanes, lanes)
                lhs_ref[:, group, :, pl.ds(start, lanes)] = merged

    @pl.when(step >= segments)
    def _():
        lhs = lhs_ref[...].reshape(out_ref.shape[0], lhs_ref.shape[-1])
        out_ref[...] = jnp.dot(lhs, basis_ref[...], preferred_element_type=jnp.float32)


def spectra_from(landed, row, half, basis, plane_count, per_plane, groups):
    _, fields, sliver, lanes = landed.shape
    depth = per_plane * lanes // 2
    length = basis.shape[1]
    width = 256
    chunks = length // width

    def piece_map(position, group):
        def index_map(s, row_ref, half_ref):
            segment = jnp.minimum(s, plane_count - 1)
            return (row_ref[(segment * per_plane + position) * groups + group], 0, 0, 0)

        return index_map

    def column_map(s, row_ref, half_ref):
        return (0, jnp.maximum(s - plane_count, 0))

    in_specs = [
        pl.BlockSpec((1, fields, sliver, lanes), piece_map(position, group))
        for position in range(per_plane)
        for group in range(groups)
    ]
    in_specs.append(pl.BlockSpec((basis.shape[0], width), column_map))
    rows = fields * groups * sliver
    return pl.pallas_call(
        functools.partial(spectra_kernel, groups, per_plane),
        out_shape=jax.ShapeDtypeStruct((rows, length), jnp.float32),
        grid_spec=pltpu.PrefetchScalarGridSpec(
            num_scalar_prefetch=2,
            grid=(plane_count + chunks,),
            in_specs=in_specs,
            out_specs=pl.BlockSpec((rows, width), column_map),
            scratch_shapes=[
                pltpu.VMEM((fields, groups, sliver, plane_count * depth), landed.dtype)
            ],
        ),
        compiler_params=pltpu.CompilerParams(
            dimension_semantics=("arbitrary",), vmem_limit_bytes=48 * 1024 * 1024
        ),
    )(row, half, *([landed] * (per_plane * groups)), basis)


def local(blocks, levels, block_dest, block_phi, block_group):
    tile_count = lax.axis_size("tile")
    plane_count = lax.axis_size("phi")
    slot_count = blocks.shape[0]
    fields = blocks.shape[1]
    per_plane = NPHI // BPHI // plane_count
    capacity = 2 * slot_count // tile_count
    sliver = COLS // plane_count

    block_ids = jnp.arange(slot_count, dtype=jnp.int32)
    earlier = (block_dest[None, :] == block_dest[:, None]) & (block_ids[None, :] < block_ids[:, None])
    slot_rank = jnp.sum(earlier.astype(jnp.int32), axis=1)
    send_slot = block_dest * capacity + slot_rank
    slot_ids = jnp.arange(tile_count * capacity, dtype=jnp.int32)
    match = (send_slot[None, :] == slot_ids[:, None]).astype(jnp.int32)
    source = jnp.sum(match * block_ids[None, :], axis=1)
    place = block_phi * CG_DEV + block_group
    code = jnp.sum(match * (place[None, :] + 1), axis=1) - 1
    device_count = tile_count * plane_count
    pairs = capacity // 2

    outbox = pack_outbox(blocks, source, levels, tile_count, capacity, plane_count)
    outbox = outbox.reshape(device_count, pairs * fields * sliver, 2 * BPHI)
    code_out = jnp.broadcast_to(
        code.reshape(tile_count, 1, capacity), (tile_count, plane_count, capacity)
    ).reshape(device_count, capacity)
    arrived = lax.all_to_all(outbox, ("tile", "phi"), split_axis=0, concat_axis=0, tiled=True)
    arrived_code = lax.all_to_all(code_out, ("tile", "phi"), split_axis=0, concat_axis=0, tiled=True)

    by_segment = jnp.transpose(
        arrived_code.reshape(tile_count, plane_count, capacity), (1, 0, 2)
    ).reshape(plane_count, tile_count * capacity)
    want = jnp.arange(slot_count, dtype=jnp.int32)
    hit = (by_segment[:, None, :] == want[None, :, None]).astype(jnp.int32)
    arrival = jnp.arange(tile_count * capacity, dtype=jnp.int32)
    pick = jnp.sum(hit * arrival[None, None, :], axis=2)
    origin = pick // capacity
    segment = jnp.arange(plane_count, dtype=jnp.int32)[:, None]
    row = ((origin * plane_count + segment) * pairs + (pick % capacity) // 2).reshape(-1)
    half = (pick % 2).reshape(-1)
    landed = arrived.reshape(device_count * pairs, fields, sliver, 2 * BPHI)
    basis = dft_basis(NPHI)
    spectra = spectra_from(landed, row, half, basis, plane_count, per_plane, CG_DEV)
    return spectra.reshape(fields, CG_DEV, sliver, NPHI)


def solution(mesh):
    in_specs = (
        P(("tile", "phi"), None, None, None),
        P(("tile", "phi")),
        P(("tile", "phi")),
        P(("tile", "phi")),
        P(("tile", "phi")),
    )
    out_specs = P(None, "tile", "phi", None)
    return jax.shard_map(local, mesh=mesh, in_specs=in_specs, out_specs=out_specs, check_vma=False)
```

```python
import functools
import math

import jax
import jax.numpy as jnp
from jax import lax
from jax.experimental import pallas as pl
from jax.experimental.pallas import tpu as pltpu
from jax.sharding import PartitionSpec as P

FIELDS = 5
NPHI = 2048
BPHI = 64
COLS = 256
CG_DEV = 8


def dft_basis(length):
    half = length // 2
    column = jnp.arange(length, dtype=jnp.int32)
    mode = jnp.where(column <= half, column, column - half)
    scale = jnp.float32(2.0 * math.pi / length)
    hi = jnp.arange(length // BPHI, dtype=jnp.int32) * BPHI
    lo = jnp.arange(BPHI, dtype=jnp.int32)
    angle_hi = (hi[:, None] * mode[None, :] % length).astype(jnp.float32) * scale
    angle_lo = (lo[:, None] * mode[None, :] % length).astype(jnp.float32) * scale
    ch, sh = jnp.cos(angle_hi)[:, None, :], jnp.sin(angle_hi)[:, None, :]
    cl, sl = jnp.cos(angle_lo)[None, :, :], jnp.sin(angle_lo)[None, :, :]
    is_cos = (column <= half)[None, None, :]
    values = jnp.where(is_cos, ch * cl - sh * sl, sh * cl + ch * sl)
    values = values * jnp.float32(1.0 / math.sqrt(length))
    return values.reshape(length, length).astype(jnp.bfloat16)


def level_scale(level, dtype):
    value = jnp.where(
        level == 0, 1.0, jnp.where(level == 1, 0.5, jnp.where(level == 2, 0.25, 0.125))
    )
    return value.astype(jnp.float32).astype(dtype)


def pack_kernel(source_ref, level_ref, *refs):
    out_ref = refs[-1]
    per_step, planes, pairs, fields, sliver = out_ref.shape[:5]
    step = pl.program_id(0)
    for local_tile in range(per_step):
        for pair in range(pairs):
            slot = (local_tile * pairs + pair) * 2
            first = step * (len(refs) - 1) + slot
            first_scale = level_scale(level_ref[source_ref[first]], out_ref.dtype)
            second_scale = level_scale(level_ref[source_ref[first + 1]], out_ref.dtype)
            for field in range(fields):
                both = jnp.concatenate(
                    [
                        refs[slot][0, field] * first_scale,
                        refs[slot + 1][0, field] * second_scale,
                    ],
                    axis=0,
                )
                flipped = both.T.reshape(planes, sliver, both.shape[0])
                out_ref[local_tile, :, pair, field] = flipped.astype(out_ref.dtype)


def pack_outbox(blocks, source, levels, tile_count, capacity, plane_count):
    slot_count, fields, bphi, cols = blocks.shape
    pairs = capacity // 2
    sliver = cols // plane_count

    per_step = 4
    per_call = per_step * capacity

    def block_map(slot):
        return lambda t, src_ref, level_ref: (src_ref[t * per_call + slot], 0, 0, 0)

    return pl.pallas_call(
        pack_kernel,
        out_shape=jax.ShapeDtypeStruct(
            (tile_count, plane_count, pairs, fields, sliver, 2 * bphi), blocks.dtype
        ),
        grid_spec=pltpu.PrefetchScalarGridSpec(
            num_scalar_prefetch=2,
            grid=(tile_count // per_step,),
            in_specs=[pl.BlockSpec((1, fields, bphi, cols), block_map(slot)) for slot in range(per_call)],
            out_specs=pl.BlockSpec(
                (per_step, plane_count, pairs, fields, sliver, 2 * bphi),
                lambda t, src_ref, level_ref: (t, 0, 0, 0, 0, 0),
            ),
        ),
    )(source, levels, *([blocks] * per_call))


def spectra_kernel(groups, per_plane, row_ref, half_ref, *refs):
    pieces = refs[: per_plane * groups]
    basis_ref, out_ref, lhs_ref = refs[per_plane * groups :]
    step = pl.program_id(0)
    segments = lhs_ref.shape[-1] // (pieces[0].shape[-1] * per_plane // 2)

    @pl.when(step < segments)
    def _():
        lanes = pieces[0].shape[-1]
        shape = pieces[0].shape[1:]
        lane = lax.broadcasted_iota(jnp.int32, shape, 2)
        for group in range(groups):
            for quad in range(per_plane // 2):
                parts = []
                for side in range(2):
                    position = quad * 2 + side
                    index = (step * per_plane + position) * groups + group
                    piece = pieces[position * groups + group][0]
                    turned = pltpu.roll(piece, lanes // 2, 2)
                    keep = half_ref[index] == side
                    parts.append(jnp.where(keep, piece, turned))
                merged = jnp.where(lane < lanes // 2, parts[0], parts[1])
                start = pl.multiple_of(step * (lanes * per_plane // 2) + quad * lanes, lanes)
                lhs_ref[:, group, :, pl.ds(start, lanes)] = merged

    @pl.when(step >= segments)
    def _():
        lhs = lhs_ref[...].reshape(out_ref.shape[0], lhs_ref.shape[-1])
        out_ref[...] = jnp.dot(lhs, basis_ref[...], preferred_element_type=jnp.float32)


def spectra_from(landed, row, half, basis, plane_count, per_plane, groups):
    _, fields, sliver, lanes = landed.shape
    depth = per_plane * lanes // 2
    length = basis.shape[1]
    width = 1024
    chunks = length // width

    def piece_map(position, group):
        def index_map(s, row_ref, half_ref):
            segment = jnp.minimum(s, plane_count - 1)
            return (row_ref[(segment * per_plane + position) * groups + group], 0, 0, 0)

        return index_map

    def column_map(s, row_ref, half_ref):
        return (0, jnp.maximum(s - plane_count, 0))

    in_specs = [
        pl.BlockSpec((1, fields, sliver, lanes), piece_map(position, group))
        for position in range(per_plane)
        for group in range(groups)
    ]
    in_specs.append(pl.BlockSpec((basis.shape[0], width), column_map))
    rows = fields * groups * sliver
    return pl.pallas_call(
        functools.partial(spectra_kernel, groups, per_plane),
        out_shape=jax.ShapeDtypeStruct((rows, length), jnp.float32),
        grid_spec=pltpu.PrefetchScalarGridSpec(
            num_scalar_prefetch=2,
            grid=(plane_count + chunks,),
            in_specs=in_specs,
            out_specs=pl.BlockSpec((rows, width), column_map),
            scratch_shapes=[
                pltpu.VMEM((fields, groups, sliver, plane_count * depth), landed.dtype)
            ],
        ),
        compiler_params=pltpu.CompilerParams(
            dimension_semantics=("arbitrary",), vmem_limit_bytes=48 * 1024 * 1024
        ),
    )(row, half, *([landed] * (per_plane * groups)), basis)


def local(blocks, levels, block_dest, block_phi, block_group):
    tile_count = lax.axis_size("tile")
    plane_count = lax.axis_size("phi")
    slot_count = blocks.shape[0]
    fields = blocks.shape[1]
    per_plane = NPHI // BPHI // plane_count
    capacity = 2 * slot_count // tile_count
    sliver = COLS // plane_count

    block_ids = jnp.arange(slot_count, dtype=jnp.int32)
    earlier = (block_dest[None, :] == block_dest[:, None]) & (block_ids[None, :] < block_ids[:, None])
    slot_rank = jnp.sum(earlier.astype(jnp.int32), axis=1)
    send_slot = block_dest * capacity + slot_rank
    slot_ids = jnp.arange(tile_count * capacity, dtype=jnp.int32)
    match = (send_slot[None, :] == slot_ids[:, None]).astype(jnp.int32)
    source = jnp.sum(match * block_ids[None, :], axis=1)
    place = block_phi * CG_DEV + block_group
    code = jnp.sum(match * (place[None, :] + 1), axis=1) - 1
    device_count = tile_count * plane_count
    pairs = capacity // 2

    outbox = pack_outbox(blocks, source, levels, tile_count, capacity, plane_count)
    outbox = outbox.reshape(device_count, pairs * fields * sliver, 2 * BPHI)
    code_out = jnp.broadcast_to(
        code.reshape(tile_count, 1, capacity), (tile_count, plane_count, capacity)
    ).reshape(device_count, capacity)
    arrived = lax.all_to_all(outbox, ("tile", "phi"), split_axis=0, concat_axis=0, tiled=True)
    arrived_code = lax.all_to_all(code_out, ("tile", "phi"), split_axis=0, concat_axis=0, tiled=True)

    by_segment = jnp.transpose(
        arrived_code.reshape(tile_count, plane_count, capacity), (1, 0, 2)
    ).reshape(plane_count, tile_count * capacity)
    want = jnp.arange(slot_count, dtype=jnp.int32)
    hit = (by_segment[:, None, :] == want[None, :, None]).astype(jnp.int32)
    arrival = jnp.arange(tile_count * capacity, dtype=jnp.int32)
    pick = jnp.sum(hit * arrival[None, None, :], axis=2)
    origin = pick // capacity
    segment = jnp.arange(plane_count, dtype=jnp.int32)[:, None]
    row = ((origin * plane_count + segment) * pairs + (pick % capacity) // 2).reshape(-1)
    half = (pick % 2).reshape(-1)
    landed = arrived.reshape(device_count * pairs, fields, sliver, 2 * BPHI)
    basis = dft_basis(NPHI)
    spectra = spectra_from(landed, row, half, basis, plane_count, per_plane, CG_DEV)
    return spectra.reshape(fields, CG_DEV, sliver, NPHI)


def solution(mesh):
    in_specs = (
        P(("tile", "phi"), None, None, None),
        P(("tile", "phi")),
        P(("tile", "phi")),
        P(("tile", "phi")),
        P(("tile", "phi")),
    )
    out_specs = P(None, "tile", "phi", None)
    return jax.shard_map(local, mesh=mesh, in_specs=in_specs, out_specs=out_specs, check_vma=False)
```

```python
import functools
import math

import jax
import jax.numpy as jnp
from jax import lax
from jax.experimental import pallas as pl
from jax.experimental.pallas import tpu as pltpu
from jax.sharding import PartitionSpec as P

FIELDS = 5
NPHI = 2048
BPHI = 64
COLS = 256
CG_DEV = 8


def dft_basis(length):
    half = length // 2
    column = jnp.arange(length, dtype=jnp.int32)
    mode = jnp.where(column <= half, column, column - half)
    scale = jnp.float32(2.0 * math.pi / length)
    hi = jnp.arange(length // BPHI, dtype=jnp.int32) * BPHI
    lo = jnp.arange(BPHI, dtype=jnp.int32)
    angle_hi = (hi[:, None] * mode[None, :] % length).astype(jnp.float32) * scale
    angle_lo = (lo[:, None] * mode[None, :] % length).astype(jnp.float32) * scale
    ch, sh = jnp.cos(angle_hi)[:, None, :], jnp.sin(angle_hi)[:, None, :]
    cl, sl = jnp.cos(angle_lo)[None, :, :], jnp.sin(angle_lo)[None, :, :]
    is_cos = (column <= half)[None, None, :]
    values = jnp.where(is_cos, ch * cl - sh * sl, sh * cl + ch * sl)
    values = values * jnp.float32(1.0 / math.sqrt(length))
    return values.reshape(length, length).astype(jnp.bfloat16)


def level_scale(level, dtype):
    value = jnp.where(
        level == 0, 1.0, jnp.where(level == 1, 0.5, jnp.where(level == 2, 0.25, 0.125))
    )
    return value.astype(jnp.float32).astype(dtype)


def pack_kernel(source_ref, level_ref, *refs):
    out_ref = refs[-1]
    per_step, planes, pairs, fields, sliver = out_ref.shape[:5]
    step = pl.program_id(0)
    for local_tile in range(per_step):
        for pair in range(pairs):
            slot = (local_tile * pairs + pair) * 2
            first = step * (len(refs) - 1) + slot
            first_scale = level_scale(level_ref[source_ref[first]], out_ref.dtype)
            second_scale = level_scale(level_ref[source_ref[first + 1]], out_ref.dtype)
            for field in range(fields):
                both = jnp.concatenate(
                    [
                        refs[slot][0, field] * first_scale,
                        refs[slot + 1][0, field] * second_scale,
                    ],
                    axis=0,
                )
                flipped = both.T.reshape(planes, sliver, both.shape[0])
                out_ref[local_tile, :, pair, field] = flipped.astype(out_ref.dtype)


def pack_outbox(blocks, source, levels, tile_count, capacity, plane_count):
    slot_count, fields, bphi, cols = blocks.shape
    pairs = capacity // 2
    sliver = cols // plane_count

    per_step = 4
    per_call = per_step * capacity

    def block_map(slot):
        return lambda t, src_ref, level_ref: (src_ref[t * per_call + slot], 0, 0, 0)

    return pl.pallas_call(
        pack_kernel,
        out_shape=jax.ShapeDtypeStruct(
            (tile_count, plane_count, pairs, fields, sliver, 2 * bphi), blocks.dtype
        ),
        grid_spec=pltpu.PrefetchScalarGridSpec(
            num_scalar_prefetch=2,
            grid=(tile_count // per_step,),
            in_specs=[pl.BlockSpec((1, fields, bphi, cols), block_map(slot)) for slot in range(per_call)],
            out_specs=pl.BlockSpec(
                (per_step, plane_count, pairs, fields, sliver, 2 * bphi),
                lambda t, src_ref, level_ref: (t, 0, 0, 0, 0, 0),
            ),
        ),
    )(source, levels, *([blocks] * per_call))


def spectra_kernel(groups, per_plane, row_ref, half_ref, *refs):
    pieces = refs[: per_plane * groups]
    basis_ref, out_ref, lhs_ref = refs[per_plane * groups :]
    step = pl.program_id(0)
    segments = lhs_ref.shape[-1] // (pieces[0].shape[-1] * per_plane // 2)

    @pl.when(step < segments)
    def _():
        lanes = pieces[0].shape[-1]
        shape = pieces[0].shape[1:]
        lane = lax.broadcasted_iota(jnp.int32, shape, 2)
        for group in range(groups):
            for quad in range(per_plane // 2):
                parts = []
                for side in range(2):
                    position = quad * 2 + side
                    index = (step * per_plane + position) * groups + group
                    piece = pieces[position * groups + group][0]
                    turned = pltpu.roll(piece, lanes // 2, 2)
                    keep = half_ref[index] == side
                    parts.append(jnp.where(keep, piece, turned))
                merged = jnp.where(lane < lanes // 2, parts[0], parts[1])
                start = pl.multiple_of(step * (lanes * per_plane // 2) + quad * lanes, lanes)
                lhs_ref[:, group, :, pl.ds(start, lanes)] = merged

    @pl.when(step >= segments)
    def _():
        lhs = lhs_ref[...].reshape(out_ref.shape[0], lhs_ref.shape[-1])
        out_ref[...] = jnp.dot(lhs, basis_ref[...], preferred_element_type=jnp.float32)


def spectra_from(landed, row, half, basis, plane_count, per_plane, groups):
    _, fields, sliver, lanes = landed.shape
    depth = per_plane * lanes // 2
    length = basis.shape[1]
    width = 512
    chunks = length // width

    def piece_map(position, group):
        def index_map(s, row_ref, half_ref):
            segment = jnp.minimum(s, plane_count - 1)
            return (row_ref[(segment * per_plane + position) * groups + group], 0, 0, 0)

        return index_map

    def column_map(s, row_ref, half_ref):
        return (0, jnp.maximum(s - plane_count, 0))

    in_specs = [
        pl.BlockSpec((1, fields, sliver, lanes), piece_map(position, group))
        for position in range(per_plane)
        for group in range(groups)
    ]
    in_specs.append(pl.BlockSpec((basis.shape[0], width), column_map))
    rows = fields * groups * sliver
    return pl.pallas_call(
        functools.partial(spectra_kernel, groups, per_plane),
        out_shape=jax.ShapeDtypeStruct((rows, length), jnp.float32),
        grid_spec=pltpu.PrefetchScalarGridSpec(
            num_scalar_prefetch=2,
            grid=(plane_count + chunks,),
            in_specs=in_specs,
            out_specs=pl.BlockSpec((rows, width), column_map),
            scratch_shapes=[
                pltpu.VMEM((fields, groups, sliver, plane_count * depth), landed.dtype)
            ],
        ),
        compiler_params=pltpu.CompilerParams(
            dimension_semantics=("arbitrary",), vmem_limit_bytes=48 * 1024 * 1024
        ),
    )(row, half, *([landed] * (per_plane * groups)), basis)


def local(blocks, levels, block_dest, block_phi, block_group):
    tile_count = lax.axis_size("tile")
    plane_count = lax.axis_size("phi")
    slot_count = blocks.shape[0]
    fields = blocks.shape[1]
    per_plane = NPHI // BPHI // plane_count
    capacity = 2 * slot_count // tile_count
    sliver = COLS // plane_count

    block_ids = jnp.arange(slot_count, dtype=jnp.int32)
    earlier = (block_dest[None, :] == block_dest[:, None]) & (block_ids[None, :] < block_ids[:, None])
    slot_rank = jnp.sum(earlier.astype(jnp.int32), axis=1)
    send_slot = block_dest * capacity + slot_rank
    slot_ids = jnp.arange(tile_count * capacity, dtype=jnp.int32)
    match = (send_slot[None, :] == slot_ids[:, None]).astype(jnp.int32)
    source = jnp.sum(match * block_ids[None, :], axis=1)
    place = block_phi * CG_DEV + block_group
    device_count = tile_count * plane_count
    pairs = capacity // 2

    outbox = pack_outbox(blocks, source, levels, tile_count, capacity, plane_count)
    outbox = outbox.reshape(device_count, pairs * fields * sliver, 2 * BPHI)
    arrived = lax.all_to_all(outbox, ("tile", "phi"), split_axis=0, concat_axis=0, tiled=True)
    dest_slot = (
        lax.broadcasted_iota(jnp.int32, (tile_count, plane_count, capacity), 0) * capacity
        + lax.broadcasted_iota(jnp.int32, (tile_count, plane_count, capacity), 2)
    )
    match_out = (send_slot == dest_slot[..., None]).astype(jnp.int32)
    code_out = (jnp.sum(match_out * (place + 1), axis=3) - 1).reshape(device_count, capacity)
    arrived_code = lax.all_to_all(code_out, ("tile", "phi"), split_axis=0, concat_axis=0, tiled=True)

    by_segment = jnp.transpose(
        arrived_code.reshape(tile_count, plane_count, capacity), (1, 0, 2)
    ).reshape(plane_count, tile_count * capacity)
    want = jnp.arange(slot_count, dtype=jnp.int32)
    hit = (by_segment[:, None, :] == want[None, :, None]).astype(jnp.int32)
    arrival = jnp.arange(tile_count * capacity, dtype=jnp.int32)
    pick = jnp.sum(hit * arrival[None, None, :], axis=2)
    origin = pick // capacity
    segment = jnp.arange(plane_count, dtype=jnp.int32)[:, None]
    row = ((origin * plane_count + segment) * pairs + (pick % capacity) // 2).reshape(-1)
    half = (pick % 2).reshape(-1)
    landed = arrived.reshape(device_count * pairs, fields, sliver, 2 * BPHI)
    basis = dft_basis(NPHI)
    spectra = spectra_from(landed, row, half, basis, plane_count, per_plane, CG_DEV)
    return spectra.reshape(fields, CG_DEV, sliver, NPHI)


def solution(mesh):
    in_specs = (
        P(("tile", "phi"), None, None, None),
        P(("tile", "phi")),
        P(("tile", "phi")),
        P(("tile", "phi")),
        P(("tile", "phi")),
    )
    out_specs = P(None, "tile", "phi", None)
    return jax.shard_map(local, mesh=mesh, in_specs=in_specs, out_specs=out_specs, check_vma=False)
```
